32 devices in a mesh: space: 4 (over z), tm: 4 (over x, core), cores: 2 (over y).
Axes of the slice: x: 2, y: 2, z: 4, core: 2. Of those that a mesh axis runs over, the one named last changes fastest.
Arguments:
- initial_state: float32 [128, 64, 512], P('space', 'cores'), may hold values from -6 to 6
- heat_source: float32 [128, 64, 512], P('space', 'cores'), may hold values from -3 to 3
- source_amplitude: float32 [32], P('tm'), may hold values from 0.5 to 1.5
- diffusivity: float32 [4], P('space'), may hold values from 0.5 to 2
- robin_param: float32 [4], P('space'), may hold values from 0.5 to 4
- spectrum_x: float32 [32], replicated, may hold values from 0.002 to 0.38
- spectrum_y: float32 [64], P('cores'), may hold values from 0.002 to 0.38
- spectrum_z: float32 [512], replicated, may hold values from 0.002 to 0.38
- robin_in: float32 [4, 2, 32, 64, 512], P('space', None, 'tm', 'cores'), may hold values from -8 to 8
- open_flag: int32 [4, 64], P(None, 'cores'), may hold values from 0 to 1, as said below
- owner_side: int32 [4, 64], P(None, 'cores'), may hold values from 0 to 1, as said below
Outputs:
- robin_out: float32 [4, 2, 32, 64, 512], P('space', None, 'tm', 'cores')
- window_end: float32 [4, 128, 64, 512], P('tm', 'space', 'cores')
The draws below stay inside these ranges and needn't reach their ends.
Inputs may be any that keep to these rules, and one draw needn't show every extreme that they name: In each aligned group of 4 modes b of an interface exactly one has open_flag 0. In each aligned pair of modes b of an interface exactly one has owner_side 1.
All inputs are finite; a program needn't handle non-finite values.
Results may differ from the reference program's by a relative error of at most 0.00015.
Values sent between devices are 32-bit elements; how exact they have to be, the bound alone decides.
No kernel may reach another device: no remote copies, remote signals or barrier semaphores. Data moves between devices by JAX's collectives and lax.ppermute only.
A program may use at most 128 MiB of HBM per device.

```python
import math
import jax
import jax.numpy as jnp
from jax import lax

NX = 32
NY = 64
NZ = 512
STEPS = 8
SUBDOMAINS = 4
LENGTH = 128
MOMENTS = 32
N_SPACE = 4
N_TM = 4


def draw_open_flag(key, part):
    closed_at = jax.random.randint(jax.random.fold_in(key, 11), (SUBDOMAINS, NY // 4), 0, 4)
    slots = jnp.arange(4, dtype=jnp.int32)[None, None, :]
    return (slots != closed_at[:, :, None]).astype(jnp.int32).reshape(SUBDOMAINS, NY)


def draw_owner_side(key, part):
    right_at = jax.random.randint(jax.random.fold_in(key, 23), (SUBDOMAINS, NY // 2), 0, 2)
    slots = jnp.arange(2, dtype=jnp.int32)[None, None, :]
    return (slots == right_at[:, :, None]).astype(jnp.int32).reshape(SUBDOMAINS, NY)


def block_levels(stream_key, extent, pieces, low, high):
    gain, own = 1.0, jax.random.fold_in(stream_key, 6)
    for axis_at, parts in pieces:
        steps = jnp.exp(jax.random.uniform(jax.random.fold_in(own, axis_at), (parts,), jnp.float32, low / len(pieces), high / len(pieces)))
        gain = gain * jnp.repeat(steps, extent[axis_at] // parts).reshape([-1 if axis == axis_at else 1 for axis in range(len(extent))])
    return gain


def gaussian(stream_key, shape, width, bound, pieces=(), kind=jnp.bfloat16):
    values = width * jax.random.normal(stream_key, shape, jnp.float32)
    if pieces:
        values = values * block_levels(stream_key, shape, pieces, -0.22, 0.18)
    return jnp.clip(values, -bound, bound).astype(kind)


def setup_inputs(seed: int = 0) -> dict:
    seeds = jax.random.split(jax.random.key(seed), 12)
    initial_state = gaussian(seeds[0], (LENGTH, NY, NZ), 1.0, 6.0, ((0, 4), (1, 2)), jnp.float32)
    heat_source = gaussian(seeds[1], (LENGTH, NY, NZ), 0.2, 3.0, ((0, 4), (1, 2)), jnp.float32)
    source_amplitude = jnp.clip(0.5 + 1.0 * jax.random.uniform(seeds[2], (MOMENTS,), jnp.float32) ** block_levels(seeds[2], (MOMENTS,), ((0, 4),), -0.2, 0.2), 0.5, 1.5)
    diffusivity = jnp.clip(jnp.exp(math.log(2.0) - 1.3862944 * jax.random.uniform(seeds[3], (SUBDOMAINS,), jnp.float32) ** block_levels(seeds[3], (SUBDOMAINS,), ((0, 4),), -0.2, 0.2)), 0.5, 2.0)
    robin_param = jnp.clip(jnp.exp(math.log(4.0) - 2.0794415 * jax.random.uniform(seeds[4], (SUBDOMAINS,), jnp.float32) ** block_levels(seeds[4], (SUBDOMAINS,), ((0, 4),), -0.2, 0.2)), 0.5, 4.0)
    spectrum_x = jnp.clip(jnp.exp(jax.random.uniform(seeds[5], (NX,), jnp.float32, math.log(0.002), math.log(0.38))), 0.002, 0.38)
    spectrum_y = jnp.clip(jnp.exp(math.log(0.38) - 5.247024 * jax.random.uniform(seeds[6], (NY,), jnp.float32) ** block_levels(seeds[6], (NY,), ((0, 2),), -0.2, 0.2)), 0.002, 0.38)
    spectrum_z = jnp.clip(jnp.exp(jax.random.uniform(seeds[7], (NZ,), jnp.float32, math.log(0.002), math.log(0.38))), 0.002, 0.38)
    robin_in = gaussian(seeds[8], (SUBDOMAINS, 2, MOMENTS, NY, NZ), 2.0, 8.0, ((0, 4), (2, 4), (3, 2)), jnp.float32)
    open_flag = draw_open_flag(jax.random.fold_in(seeds[11], 71), 0)
    owner_side = draw_owner_side(jax.random.fold_in(seeds[11], 71), 0)
    return {"initial_state": initial_state, "heat_source": heat_source, "source_amplitude": source_amplitude, "diffusivity": diffusivity, "robin_param": robin_param, "spectrum_x": spectrum_x, "spectrum_y": spectrum_y, "spectrum_z": spectrum_z, "robin_in": robin_in, "open_flag": open_flag, "owner_side": owner_side}


HIGHEST = lax.Precision.HIGHEST

def cosine_basis(order):
    mode_rows = jnp.arange(order, dtype=jnp.float32)[:, None]
    node_cols = jnp.arange(order, dtype=jnp.float32)[None, :]
    scaling = jnp.where(mode_rows == 0, jnp.sqrt(1.0 / order), jnp.sqrt(2.0 / order))
    return (scaling * jnp.cos(jnp.pi * mode_rows * (node_cols + 0.5) / order)).astype(jnp.float32)

def reference(initial_state, heat_source, source_amplitude, diffusivity, robin_param, spectrum_x, spectrum_y, spectrum_z, robin_in, open_flag, owner_side):
    subdomains = N_SPACE
    basis_x = cosine_basis(NX)
    basis_y = cosine_basis(NY)
    basis_z = cosine_basis(NZ)

    def forward(values):
        values = jnp.einsum('ax,sxyz->sayz', basis_x, values, precision=HIGHEST)
        values = jnp.einsum('by,sayz->sabz', basis_y, values, precision=HIGHEST)
        return jnp.einsum('cz,sabz->sabc', basis_z, values, precision=HIGHEST)

    def inverse(spectral):
        values = jnp.einsum('ax,sabc->sxbc', basis_x, spectral, precision=HIGHEST)
        values = jnp.einsum('by,sxbc->sxyc', basis_y, values, precision=HIGHEST)
        return jnp.einsum('cz,sxyc->sxyz', basis_z, values, precision=HIGHEST)
    current = forward(initial_state.reshape(subdomains, NX, NY, NZ))
    source_modes = forward(heat_source.reshape(subdomains, NX, NY, NZ))
    rates = spectrum_x[:, None, None] + spectrum_y[None, :, None] + spectrum_z[None, None, :]
    factor = 1.0 / (1.0 + diffusivity[:, None, None, None] * rates[None])
    edge_rows = jnp.stack([basis_x[:, 0], basis_x[:, 1] - basis_x[:, 0], basis_x[:, NX - 1], basis_x[:, NX - 1] - basis_x[:, NX - 2]])
    owners = (jnp.arange(subdomains, dtype=jnp.int32)[:, None] + owner_side) % subdomains
    weight = robin_param[owners][:, :, None]
    opened = open_flag.astype(jnp.float32)[:, :, None]
    left_col = basis_x[:, 0][None, :, None, None]
    right_col = basis_x[:, NX - 1][None, :, None, None]
    robin_steps = []
    window_ends = []
    for window in range(N_TM):
        for substep in range(STEPS):
            moment = window * STEPS + substep
            forcing = current + source_amplitude[moment] * source_modes
            forcing = forcing + left_col * robin_in[:, 0, moment][:, None] + right_col * robin_in[:, 1, moment][:, None]
            current = forcing * factor
            traces = jnp.einsum('ka,sabc->ksbc', edge_rows, current, precision=HIGHEST)
            right_data = opened * (jnp.roll(traces[1], -1, 0) + weight * jnp.roll(traces[0], -1, 0))
            left_data = jnp.roll(opened * (weight * traces[2] - traces[3]), 1, 0)
            robin_steps.append(jnp.stack([left_data, right_data], axis=1))
        window_ends.append(inverse(current))
    robin_out = jnp.stack(robin_steps, axis=2)
    window_end = jnp.stack(window_ends).reshape(N_TM, subdomains * NX, NY, NZ)
    return (robin_out, window_end)
```

```python
import functools
import jax
import jax.numpy as jnp
from jax import lax
from jax.experimental import pallas as pl
from jax.experimental.pallas import tpu as pltpu
from jax.sharding import PartitionSpec as P

F32 = jnp.float32
BF16 = jnp.bfloat16
SUB = 8
GROUPS = 2


VM = pl.BlockSpec(memory_space=pltpu.VMEM)
SM = pl.BlockSpec(memory_space=pltpu.SMEM)


def cosine(order, mode, node):
    mode = mode.astype(F32)
    node = node.astype(F32)
    scaling = jnp.where(mode == 0, jnp.sqrt(1.0 / order), jnp.sqrt(2.0 / order))
    return scaling * jnp.cos(jnp.pi * mode * (node + 0.5) / order)


def halves(w):
    hi = lax.reduce_precision(w, exponent_bits=8, mantissa_bits=7)
    return hi.astype(BF16), (w - hi).astype(BF16)


def iotas(rows, cols):
    shape = (rows, cols)
    return lax.broadcasted_iota(jnp.int32, shape, 0), lax.broadcasted_iota(jnp.int32, shape, 1)


def cut(x):
    hi = x.astype(BF16)
    return hi, (x - hi.astype(F32)).astype(BF16)


def mm(a, b):
    return jnp.dot(a, b, preferred_element_type=F32)


def const_times(wh, wl, x):
    n = x.shape[1]
    xh, xl = cut(x)
    both = mm(wh, jnp.concatenate([xh, xl], axis=1))
    return both[:, :n] + both[:, n:] + mm(wl, xh)


def split_kernel(nt, q_ref, amp_ref, *refs):
    ins, outs = refs[:nt], refs[nt:]
    rows = outs[0].shape[0] - amp_ref.shape[0]
    for d in range(nt):
        outs[d][0:rows, :] = ins[d][...].reshape(rows, ins[d].shape[-1])
        outs[d][rows:, :] = amp_ref[...]


def order_kernel(nt, ng, rows, steps, q_ref, *refs):
    ins, outs, amps = refs[:nt], refs[nt : nt + ng], refs[nt + ng]
    scratch = refs[nt + ng + 1]
    q = q_ref[0]
    for d in range(nt):
        scratch[jnp.bitwise_xor(q, d)] = ins[d][...]
    wg = nt // ng
    for w in range(nt):
        outs[w // wg][w % wg] = scratch[w, 0:rows, :].reshape(outs[0].shape[1:])
        amps[w * steps : (w + 1) * steps, :] = scratch[w, rows:, :]


def forward_kernel(init_ref, src_ref, wz_ref, kxh_ref, kxl_ref, out_ref):
    nx, _, nz = init_ref.shape
    cq = out_ref.shape[-1]
    for f, ref in enumerate((init_ref, src_ref)):
        x = ref[...].reshape(nx * SUB, nz)
        xh, xl = cut(x)
        both = mm(xh, wz_ref[...])
        z = both[:, :cq] + both[:, cq:] + mm(xl, wz_ref[:, :cq])
        out_ref[f] = const_times(kxh_ref[...], kxl_ref[...], z).reshape(nx, SUB, cq)


def factor_into(f_ref, sx_ref, diff_ref, sy, sz):
    for a in range(f_ref.shape[0]):
        rate = (sx_ref[a] + sy) + sz
        f_ref[a] = 1.0 / (1.0 + diff_ref[0] * rate)


def own_kernel(
    dims, sx_ref, diff_ref, no_ref, np_ref, *refs
):
    nt, ng, steps, nx, hy, cq = dims
    us = refs[:ng]
    (amp_ref, sy_ref, sz_ref, kyh_ref, kyl_ref, wv_ref, wd_ref, p_ref, le_ref) = refs[ng : ng + 9]
    ql_ref, qr_ref, clos_ref, mo_ref, so_ref = refs[ng + 9 : ng + 14]
    m_s, s_s, f_s, vd = refs[ng + 14 :]
    pack = kyh_ref.shape[0] // (2 * hy)
    half = pack * hy
    wg = nt // ng

    def ytrans(ag, _):
        for f, own, oth in ((0, m_s, mo_ref), (1, s_s, so_ref)):
            here = no_ref[f, pl.ds(ag * pack, pack)].reshape(half, cq)
            there = np_ref[f, pl.ds(ag * pack, pack)].reshape(half, cq)
            res = const_times(kyh_ref[...], kyl_ref[...], jnp.concatenate([here, there], axis=0))
            own[pl.ds(ag * pack, pack)] = res[:half].reshape(pack, hy, cq)
            oth[pl.ds(ag * pack, pack)] = res[half:].reshape(pack, hy, cq)
        return 0

    lax.fori_loop(0, nx // pack, ytrans, 0)
    factor_into(f_s, sx_ref, diff_ref, sy_ref[...], sz_ref[...])
    tiles = hy // SUB
    ha = nx // 2
    for j in range(tiles):
        rows = slice(j * SUB, (j + 1) * SUB)
        for par in range(2):
            aa = slice(par * ha, (par + 1) * ha)
            cur = m_s[aa, rows, :]
            for g in range(ng):

                def window(wl, cur, g=g, j=j, par=par, aa=aa, rows=rows):
                    w = g * wg + wl
                    for k in range(steps):
                        r0 = us[g][wl, 0, k, pl.ds(j, SUB, stride=tiles), :]
                        r1 = us[g][wl, 1, k, pl.ds(j, SUB, stride=tiles), :]
                        u = r0 + r1 if par == 0 else r0 - r1
                        m = w * steps + k
                        amp = amp_ref[pl.ds(m, 1), :]
                        cur = (cur + amp * s_s[aa, rows, :] + u) * f_s[aa, rows, :]
                        vd[par, 0, m, j] = jnp.sum(cur * wv_ref[aa], axis=0)
                        vd[par, 1, m, j] = jnp.sum(cur * wd_ref[aa], axis=0)
                    clos_ref[w, aa, rows, :] = cur
                    return cur

                cur = lax.fori_loop(0, wg, window, cur)

    def combine(m, _):
        left, right = [], []
        for j in range(tiles):
            rows = slice(j * SUB, (j + 1) * SUB)
            ve, vo = vd[0, 0, m, j], vd[1, 0, m, j]
            de, do = vd[0, 1, m, j], vd[1, 1, m, j]
            left.append((de + do) + p_ref[0, rows, :] * (ve + vo))
            right.append(p_ref[1, rows, :] * (ve - vo) + (de - do))
        for i in range(tiles - 1):
            rows = slice(i * SUB, (i + 1) * SUB)
            ql_ref[m, rows, :] = jnp.where(le_ref[0, i] > 0.5, left[i + 1], left[i])
            qr_ref[m, rows, :] = jnp.where(le_ref[1, i] > 0.5, right[i + 1], right[i])
        return 0

    lax.fori_loop(0, nt * steps, combine, 0)


def other_kernel(
    dims, g, q_ref, sx_ref, diff_ref, m_ref, s_ref, u_ref, amp_ref, sy_ref, sz_ref,
    clos_ref, kih_ref, kil_ref, kxh_ref, kxl_ref, *refs
):
    nt, ng, steps, nx, hy, cq = dims
    wg = nt // ng
    outs, st_ref = refs[:wg], refs[wg]
    f_s, cl, t_s = refs[wg + 1 :]
    factor_into(f_s, sx_ref, diff_ref, sy_ref[...], sz_ref[...])
    tiles = hy // SUB
    ha = nx // 2
    for j in range(tiles):
        rows = slice(j * SUB, (j + 1) * SUB)
        for par in range(2):
            aa = slice(par * ha, (par + 1) * ha)

            def window(wl, cur, j=j, par=par, aa=aa, rows=rows):
                for k in range(steps):
                    r0 = u_ref[wl, 0, k, pl.ds(j, SUB, stride=tiles), :]
                    r1 = u_ref[wl, 1, k, pl.ds(j, SUB, stride=tiles), :]
                    u = r0 + r1 if par == 0 else r0 - r1
                    amp = amp_ref[pl.ds((g * wg + wl) * steps + k, 1), :]
                    cur = (cur + amp * s_ref[aa, rows, :] + u) * f_s[aa, rows, :]
                cl[wl, aa, rows, :] = cur
                return cur

            st_ref[aa, rows, :] = lax.fori_loop(0, wg, window, m_ref[aa, rows, :])
    pack = kih_ref.shape[0] // hy
    half = pack * hy
    for e in range(wg):
        wl = jnp.bitwise_and(jnp.bitwise_xor(q_ref[0], e), wg - 1)

        def yback(ag, _, wl=wl):
            here = clos_ref[g * wg + wl, pl.ds(ag * pack, pack)].reshape(half, cq)
            there = cl[wl, pl.ds(ag * pack, pack)].reshape(half, cq)
            res = const_times(kih_ref[...], kil_ref[...], jnp.concatenate([here, there], axis=0))
            t_s[pl.ds(ag * pack, pack)] = res.reshape(pack, hy, cq)
            return 0

        lax.fori_loop(0, nx // pack, yback, 0)
        for yb in range(tiles):
            x = t_s[:, yb * SUB : (yb + 1) * SUB, :].reshape(nx * SUB, cq)
            res = const_times(kxh_ref[...], kxl_ref[...], x)
            outs[e][:, yb * SUB : (yb + 1) * SUB, :] = res.reshape(nx, SUB, cq)


def final_kernel(nt, ng, q_ref, wh_ref, wl_ref, *refs):
    out_ref = refs[-1]
    wg = nt // ng
    xb, hy, nz = out_ref.shape[1:]
    cq = nz // nt
    pieces = []
    for d in range(nt):
        x = refs[d * ng][...]
        for g in range(1, ng):
            x = jnp.where(q_ref[0] // wg == g, refs[d * ng + g][...], x)
        pieces.append(x.reshape(xb * hy, cq))
    xh, xl = cut(jnp.concatenate(pieces, axis=1))
    res = mm(xh, wh_ref[...]) + mm(xh, wl_ref[...]) + mm(xl, wh_ref[...])
    out_ref[0] = res.reshape(xb, hy, nz)


def deal_kernel(nt, steps, q_ref, f0_ref, f1_ref, *outs):
    for d in range(nt):
        w = jnp.bitwise_xor(q_ref[0], d)
        outs[d][0] = f0_ref[pl.ds(w * steps, steps)]
        outs[d][1] = f1_ref[pl.ds(w * steps, steps)]


def spread_kernel(nt, steps, q_ref, le_ref, *refs):
    ins, out_ref, slots, line = refs[:nt], refs[nt], refs[nt + 1], refs[nt + 2]
    hy = out_ref.shape[3]
    cq = out_ref.shape[4] // nt
    tiles = hy // SUB
    for d in range(nt):
        slots[jnp.bitwise_xor(q_ref[0], d)] = ins[d][...]
    for face in range(2):
        le = [le_ref[face, i] > 0.5 for i in range(tiles - 1)]
        zero = jnp.zeros((SUB, cq), F32)
        for c in range(nt):

            def step(k, _, face=face, c=c):
                r = [slots[c, face, k, i * SUB : (i + 1) * SUB, :] for i in range(tiles - 1)]
                for j in range(tiles):
                    if j == 0:
                        v = jnp.where(le[0], zero, r[0])
                    elif j < tiles - 1:
                        v = jnp.where(le[j], jnp.where(le[j - 1], r[j - 1], zero), r[j])
                    else:
                        v = jnp.where(le[j - 1], r[j - 1], zero)
                    line[face, k, pl.ds(j, SUB, stride=tiles), :] = v
                out_ref[0, face, k, :, c * cq : (c + 1) * cq] = line[face, k]
                return 0

            lax.fori_loop(0, steps, step, 0)


def sds(*shape):
    return jax.ShapeDtypeStruct(shape, F32)


def cost(flops, nbytes):
    return pl.CostEstimate(flops=int(flops), bytes_accessed=int(nbytes), transcendentals=0)


def local(
    initial_state,
    heat_source,
    source_amplitude,
    diffusivity,
    robin_param,
    spectrum_x,
    spectrum_y,
    spectrum_z,
    robin_in,
    open_flag,
    owner_side,
):
    nx, hy, nz = initial_state.shape
    nt = lax.axis_size("tm")
    ncores = lax.axis_size("cores")
    assert ncores == 2 and nt & (nt - 1) == 0 and nt >= 2
    ng = min(GROUPS, nt)
    wg = nt // ng
    ny = hy * ncores
    cq = nz // nt
    steps = source_amplitude.shape[0]
    tiles = hy // SUB
    assert tiles == 4 and nx % 2 == 0
    q = lax.axis_index("tm")
    yc = lax.axis_index("cores")
    space = lax.axis_size("space")
    me = lax.axis_index("space")
    left_index = (me + space - 1) % space
    qv = jnp.reshape(q, (1,)).astype(jnp.int32)
    dims = (nt, ng, steps, nx, hy, cq)
    ha = nx // 2

    def xor_permute(x, d):
        return lax.ppermute(x, "tm", [(i, i ^ d) for i in range(nt)])

    def swap(x):
        return lax.ppermute(x, "cores", [(0, 1), (1, 0)])

    def along(x, by):
        return lax.ppermute(x, "space", [(i, (i + by) % space) for i in range(space)])

    right_param = along(robin_param, -1)
    left_param = along(robin_param, 1)

    rows = 2 * steps * hy
    amp_rows = jnp.broadcast_to(source_amplitude[:, None], (steps, cq))
    block = (None, 2, steps, hy, cq)
    cuts = pl.pallas_call(
        functools.partial(split_kernel, nt),
        out_shape=[sds(rows + steps, cq)] * nt,
        grid_spec=pltpu.PrefetchScalarGridSpec(
            num_scalar_prefetch=1,
            grid=(1,),
            in_specs=[pl.BlockSpec((steps, cq), lambda i, q: (0, 0))]
            + [
                pl.BlockSpec(block, lambda i, q, d=d: (0, 0, 0, 0, jnp.bitwise_xor(q[0], d)))
                for d in range(nt)
            ],
            out_specs=[pl.BlockSpec((rows + steps, cq), lambda i, q: (0, 0))] * nt,
        ),
        cost_estimate=cost(0, 8 * nt * rows * cq),
        name="split",
    )(qv, amp_rows, *([robin_in] * nt))
    dealt = [cuts[0]] + [xor_permute(cuts[d], d) for d in range(1, nt)]

    r, c = iotas(nz, cq)
    wz = jnp.concatenate(halves(cosine(nz, q * cq + c, r)), axis=1)
    r, c = iotas(nx * SUB, nx * SUB)

    def a_of(i):
        return 2 * (i % ha) + i // ha

    def edge(a):
        return cosine(nx, a, jnp.zeros_like(a))

    a = a_of(r // SUB)
    kx = jnp.where(r % SUB == c % SUB, cosine(nx, a, c // SUB) / edge(a), 0.0)
    a = a_of(c // SUB)
    kxi = jnp.where(r % SUB == c % SUB, cosine(nx, a, r // SUB) * edge(a), 0.0)
    kxh, kxl = halves(kx)
    kxih, kxil = halves(kxi)
    full = lambda shape: pl.BlockSpec(shape, lambda i: (0,) * len(shape))
    nodes = pl.pallas_call(
        forward_kernel,
        out_shape=sds(2, nx, hy, cq),
        grid=(tiles,),
        in_specs=[
            pl.BlockSpec((nx, SUB, nz), lambda i: (0, i, 0)),
            pl.BlockSpec((nx, SUB, nz), lambda i: (0, i, 0)),
            full((nz, 2 * cq)),
            full((nx * SUB, nx * SUB)),
            full((nx * SUB, nx * SUB)),
        ],
        out_specs=pl.BlockSpec((2, nx, SUB, cq), lambda i: (0, 0, i, 0)),
        cost_estimate=cost(2e9, 6e6),
        name="forward",
    )(initial_state, heat_source, wz, kxh, kxl)
    nodes_there = swap(nodes)
    sy_there = swap(spectrum_y)

    *u_own, amps = pl.pallas_call(
        functools.partial(order_kernel, nt, ng, rows, steps),
        out_shape=[sds(wg, 2, steps, hy, cq)] * ng + [sds(nt * steps, cq)],
        in_specs=[SM] + [VM] * nt,
        out_specs=[VM] * (ng + 1),
        scratch_shapes=[pltpu.VMEM((nt, rows + steps, cq), F32)],
        cost_estimate=cost(0, 8 * nt * rows * cq),
        name="order",
    )(qv, *dealt)
    u_there = [swap(u) for u in u_own]

    pack = 256 // (2 * hy)
    half = pack * hy

    def mode_of(i):
        side = jnp.where(i // half == 0, yc, 1 - yc)
        line = i % hy
        return side * hy + tiles * (line % (hy // tiles)) + line // (hy // tiles)

    def node_of(i):
        return jnp.where(i // half == 0, yc, 1 - yc) * hy + i % hy

    r, c = iotas(2 * half, 2 * half)
    same = (r // hy) % pack == (c // hy) % pack
    kyh, kyl = halves(jnp.where(same, cosine(ny, mode_of(r), node_of(c)), 0.0))
    r, c = iotas(half, 2 * half)
    same = (r // hy) % pack == (c // hy) % pack
    kih, kil = halves(jnp.where(same, cosine(ny, mode_of(c), node_of(r)), 0.0))

    def lanes(v):
        return jnp.broadcast_to(v[..., None], v.shape + (cq,)).astype(F32)

    def modes_by_tile(v):
        lead = v.shape[:-1]
        v = v.reshape(lead + (hy // tiles, tiles))
        return jnp.swapaxes(v, -1, -2).reshape(lead + (hy,))

    sx = jnp.swapaxes(spectrum_x.reshape(ha, 2), 0, 1).reshape(nx)
    sy = lanes(modes_by_tile(spectrum_y))
    sy_there = lanes(modes_by_tile(sy_there))
    sz = lax.dynamic_slice_in_dim(spectrum_z, q * cq, cq, 0)[None]
    a = a_of(lax.broadcasted_iota(jnp.int32, (nx, SUB, cq), 0))
    first, second = edge(a), cosine(nx, a, jnp.ones_like(a))
    wv = first * first
    wd = first * (second - first)

    faces = jnp.stack([left_index, me])
    opened = open_flag[faces].reshape(2, hy // tiles, tiles)
    closed = jnp.stack(
        [jnp.any(opened[:, :, : i + 1] == 0, axis=2) for i in range(tiles - 1)], axis=1
    )
    le = lanes(closed.astype(F32))
    owner = owner_side[faces]
    near = jnp.stack([left_param[0], robin_param[0]])[:, None]
    far = jnp.stack([robin_param[0], right_param[0]])[:, None]
    param = lanes(modes_by_tile(jnp.where(owner == 0, near, far)))

    ql, qr, clos, m_there, s_there = pl.pallas_call(
        functools.partial(own_kernel, dims),
        out_shape=[sds(nt * steps, (tiles - 1) * SUB, cq)] * 2
        + [sds(nt, nx, hy, cq), sds(nx, hy, cq), sds(nx, hy, cq)],
        in_specs=[SM, SM] + [VM] * (2 + ng + 9),
        out_specs=[VM] * 5,
        scratch_shapes=[pltpu.VMEM((nx, hy, cq), F32)] * 3
        + [pltpu.VMEM((2, 2, nt * steps, tiles, SUB, cq), F32)],
        cost_estimate=cost(4e9, 8e6),
        name="own",
    )(sx, diffusivity, nodes, nodes_there, *u_own, amps, sy, sz, kyh, kyl, wv, wd, param, le)
    to_left = along(ql, -1)
    to_right = along(qr, 1)

    pieces = [[None] * ng for _ in range(nt)]
    state = m_there
    for g in range(ng):
        *outs, state = pl.pallas_call(
            functools.partial(other_kernel, dims, g),
            out_shape=[sds(nx, hy, cq)] * (wg + 1),
            in_specs=[SM] * 3 + [VM] * 11,
            out_specs=[VM] * (wg + 1),
            scratch_shapes=[
                pltpu.VMEM((nx, hy, cq), F32),
                pltpu.VMEM((wg, nx, hy, cq), F32),
                pltpu.VMEM((nx, hy, cq), F32),
            ],
            cost_estimate=cost(3e9, 6e6),
            name=f"other{g}",
        )(qv, sx, diffusivity, state, s_there, u_there[g], amps, sy_there, sz, clos, kih, kil, kxih, kxil)
        inside = [i for i in range(nt) if i // wg == g]
        for e in range(wg):
            for top in range(0, nt, wg):
                d = top + e
                if d == 0:
                    pieces[0][g] = outs[0]
                    continue
                pairs = [(i ^ d, i) for i in inside]
                pieces[d][g] = lax.ppermute(outs[e], "tm", pairs)

    r, c = iotas(nz, nz)
    wih, wil = halves(cosine(nz, jnp.bitwise_xor(q, r // cq) * cq + r % cq, c))
    xb = SUB
    full2 = lambda shape: pl.BlockSpec(shape, lambda i, q: (0,) * len(shape))
    flat = [pieces[d][g] for d in range(nt) for g in range(ng)]
    window_end = pl.pallas_call(
        functools.partial(final_kernel, nt, ng),
        out_shape=sds(1, nx, hy, nz),
        grid_spec=pltpu.PrefetchScalarGridSpec(
            num_scalar_prefetch=1,
            grid=(nx // xb,),
            in_specs=[full2((nz, nz))] * 2
            + [pl.BlockSpec((xb, hy, cq), lambda i, q: (i, 0, 0))] * len(flat),
            out_specs=pl.BlockSpec((1, xb, hy, nz), lambda i, q: (0, i, 0, 0)),
        ),
        cost_estimate=cost(2e9, 6e6),
        name="final",
    )(qv, wih, wil, *flat)

    short = sds(2, steps, (tiles - 1) * SUB, cq)
    hands = pl.pallas_call(
        functools.partial(deal_kernel, nt, steps),
        out_shape=[short] * nt,
        in_specs=[SM, VM, VM],
        out_specs=[VM] * nt,
        cost_estimate=cost(0, 2e6),
        name="deal",
    )(qv, to_right, to_left)
    hands = [hands[0]] + [xor_permute(hands[d], d) for d in range(1, nt)]
    robin_out = pl.pallas_call(
        functools.partial(spread_kernel, nt, steps),
        out_shape=sds(1, 2, steps, hy, nz),
        in_specs=[SM] + [VM] * (nt + 1),
        out_specs=VM,
        scratch_shapes=[
            pltpu.VMEM((nt,) + short.shape, F32),
            pltpu.VMEM((2, steps, hy, cq), F32),
        ],
        cost_estimate=cost(0, 2e6),
        name="spread",
    )(qv, le, *hands)
    return robin_out, window_end


def solution(mesh):
    placed = (
        P("space", "cores", None),
        P("space", "cores", None),
        P("tm"),
        P("space"),
        P("space"),
        P(),
        P("cores"),
        P(),
        P("space", None, "tm", "cores", None),
        P(None, "cores"),
        P(None, "cores"),
    )
    return jax.shard_map(
        local,
        mesh=mesh,
        in_specs=placed,
        out_specs=(P("space", None, "tm", "cores", None), P("tm", "space", "cores", None)),
        check_vma=False,
    )
```

```python
import functools
import jax
import numpy as np
import jax.numpy as jnp
from jax import lax
from jax.experimental import pallas as pl
from jax.experimental.pallas import tpu as pltpu
from jax.sharding import PartitionSpec as P


F32 = jnp.float32
BF16 = jnp.bfloat16
SUB = 8


VM = pl.BlockSpec(memory_space=pltpu.VMEM)
SM = pl.BlockSpec(memory_space=pltpu.SMEM)


def cosine(order, mode, node):
    mode = mode.astype(F32)
    node = node.astype(F32)
    scaling = jnp.where(mode == 0, jnp.sqrt(1.0 / order), jnp.sqrt(2.0 / order))
    return scaling * jnp.cos(jnp.pi * mode * (node + 0.5) / order)


def halves(w):
    hi = lax.reduce_precision(w, exponent_bits=8, mantissa_bits=7)
    return hi.astype(BF16), (w - hi).astype(BF16)


def iotas(rows, cols):
    shape = (rows, cols)
    return lax.broadcasted_iota(jnp.int32, shape, 0), lax.broadcasted_iota(jnp.int32, shape, 1)


def cut(x):
    hi = x.astype(BF16)
    return hi, (x - hi.astype(F32)).astype(BF16)


def mm(a, b):
    return jnp.dot(a, b, preferred_element_type=F32)


def mmt(a, b):
    return lax.dot_general(a, b, (((1,), (1,)), ((), ())), preferred_element_type=F32)


def const_times(wh, wl, x):
    xh, xl = cut(x)
    return mm(wh, xh) + mm(wh, xl) + mm(wl, xh)


def np_cosine(order, mode, node):
    mode = np.asarray(mode, np.float32)
    node = np.asarray(node, np.float32)
    scaling = np.where(mode == 0, np.sqrt(np.float32(1.0 / order)), np.sqrt(np.float32(2.0 / order)))
    angle = np.float32(np.pi) * mode * (node + np.float32(0.5)) / np.float32(order)
    return (scaling * np.cos(angle.astype(np.float64))).astype(np.float32)


def np_halves(w):
    hi = w.astype(BF16)
    return hi, (w - hi.astype(np.float32)).astype(BF16)


def np_modes(n):
    return np.concatenate([np.arange(0, n, 2), np.arange(1, n, 2)])


def np_bar(n, back):
    a = np_modes(n)
    base = np_cosine(n, a[:, None], np.arange(n)[None])
    edge = np_cosine(n, a, np.zeros(n))[:, None]
    w = (base * edge).T if back else base / edge
    return np_halves(np.kron(w, np.eye(SUB, dtype=np.float32)))


def tree(parts):
    while len(parts) > 1:
        parts = [a + b for a, b in zip(parts[::2], parts[1::2])] + (
            [parts[-1]] if len(parts) % 2 else []
        )
    return parts[0]


def split_kernel(nt, q_ref, amp_ref, *refs):
    ins, outs = refs[:nt], refs[nt:]
    steps = amp_ref.shape[0]
    rows = outs[0].shape[0] - steps
    cq = outs[0].shape[1]
    for d in range(nt):
        outs[d][0:rows, :] = ins[d][...].reshape(rows, cq)
        for k in range(steps):
            outs[d][rows + k : rows + k + 1, :] = jnp.full((1, cq), amp_ref[k], F32)


def forward_kernel(q_ref, x_ref, c_ref, kxh_ref, kxl_ref, out_ref):
    nx, _, nz = x_ref.shape
    cq = out_ref.shape[-1]
    xh, xl = cut(x_ref[...].reshape(nx * SUB, nz))
    both = mmt(xh, c_ref[...].reshape(2 * cq, nz))
    z = both[:, :cq] + both[:, cq:] + mmt(xl, c_ref[0])
    zh, zl = cut(z)
    both = mm(kxh_ref[...], jnp.concatenate([zh, zl], axis=1))
    res = both[:, :cq] + both[:, cq:] + mm(kxl_ref[...], zh)
    out_ref[...] = res.reshape(nx, SUB, cq)


def factor_into(f_ref, sx_ref, diff_ref, sy, sz):
    for a in range(f_ref.shape[0]):
        rate = (sx_ref[a] + sy) + sz
        f_ref[a] = 1.0 / (1.0 + diff_ref[0] * rate)


def gather_windows(nt, q, ins, u_s, amp_s):
    steps = amp_s.shape[1]
    rows = ins[0].shape[0] - steps
    for d in range(nt):
        w = jnp.bitwise_xor(q, d)
        u_s[w] = ins[d][0:rows, :].reshape(u_s.shape[1:])
        amp_s[w] = ins[d][rows:, :]


def own_kernel(dims, q_ref, sx_ref, diff_ref, par_ref, *refs):
    nt, steps, nx, hy, cq = dims
    n0, s0, n1, s1 = refs[:4]
    pieces = refs[4 : 4 + nt]
    (tab_ref, sz_ref, kyh_ref, kyl_ref, wv_ref, wd_ref) = refs[4 + nt : 10 + nt]
    ql_ref, qr_ref, clos_ref, mo_ref, so_ref = refs[10 + nt : 15 + nt]
    m_s, s_s, f_s, vd, u_s, amp_s = refs[15 + nt :]
    tiles = hy // SUB
    pack = kyh_ref.shape[0] // (2 * hy)
    half = pack * hy

    gather_windows(nt, q_ref[0], pieces, u_s, amp_s)
    factor_into(f_s, sx_ref, diff_ref, tab_ref[0:hy, :], sz_ref[...])

    def ytrans(ag, _):
        at = pl.ds(ag * pack, pack)
        cols = [
            jnp.concatenate([here[at].reshape(half, cq), there[at].reshape(half, cq)], axis=0)
            for here, there in ((n0, n1), (s0, s1))
        ]
        res = const_times(kyh_ref[...], kyl_ref[...], jnp.concatenate(cols, axis=1))
        for f, own, oth in ((0, m_s, mo_ref), (1, s_s, so_ref)):
            part = res[:, f * cq : (f + 1) * cq]
            own[at] = part[:half].reshape(pack, hy, cq)
            oth[at] = part[half:].reshape(pack, hy, cq)
        return 0

    lax.fori_loop(0, nx // pack, ytrans, 0)
    ha = nx // 2
    chunk = min(SUB, ha)
    for j in range(tiles):
        rows = slice(j * SUB, (j + 1) * SUB)
        for par in range(2):
            for first in range(0, ha, chunk):
                modes = [par * ha + first + i for i in range(chunk)]
                s = [s_s[a, rows, :] for a in modes]
                f = [f_s[a, rows, :] for a in modes]
                wv = [wv_ref[a] for a in modes]
                wd = [wd_ref[a] for a in modes]

                def window(w, cur, j=j, par=par, first=first, rows=rows, modes=modes, s=s, f=f, wv=wv, wd=wd):
                    cur = list(cur)
                    for k in range(steps):
                        r0 = u_s[w, 0, k, pl.ds(j, SUB, stride=tiles), :]
                        r1 = u_s[w, 1, k, pl.ds(j, SUB, stride=tiles), :]
                        u = r0 + r1 if par == 0 else r0 - r1
                        amp = amp_s[w, k : k + 1, :]
                        cur = [(x + (amp * y + u)) * z for x, y, z in zip(cur, s, f)]
                        m = w * steps + k
                        v = tree([x * y for x, y in zip(cur, wv)])
                        d = tree([x * y for x, y in zip(cur, wd)])
                        if first:
                            v = v + vd[par, 0, m, j]
                            d = d + vd[par, 1, m, j]
                        vd[par, 0, m, j] = v
                        vd[par, 1, m, j] = d
                    for a, x in zip(modes, cur):
                        clos_ref[w, a, rows, :] = x
                    return tuple(cur)

                lax.fori_loop(0, nt, window, tuple(m_s[a, rows, :] for a in modes))

    owner, closed = tab_ref.at[hy : 3 * hy], tab_ref.at[3 * hy :]

    def combine(m, _):
        left, right = [], []
        for j in range(tiles):
            ve, vo = vd[0, 0, m, j], vd[1, 0, m, j]
            de, do = vd[0, 1, m, j], vd[1, 1, m, j]
            p = [
                jnp.where(owner[i * hy + j * SUB : i * hy + (j + 1) * SUB, :] < 0.5, par_ref[i], par_ref[i + 1])
                for i in range(2)
            ]
            left.append((de + do) + p[0] * (ve + vo))
            right.append(p[1] * (ve - vo) + (de - do))
        for i in range(tiles - 1):
            rows = slice(i * SUB, (i + 1) * SUB)
            le = [closed[(n * (tiles - 1) + i) * SUB : (n * (tiles - 1) + i + 1) * SUB, :] > 0.5 for n in range(2)]
            ql_ref[m, rows, :] = jnp.where(le[0], left[i + 1], left[i])
            qr_ref[m, rows, :] = jnp.where(le[1], right[i + 1], right[i])
        return 0

    lax.fori_loop(0, nt * steps, combine, 0)


def other_kernel(dims, q_ref, sx_ref, diff_ref, m_ref, s_ref, *refs):
    nt, steps, nx, hy, cq = dims
    pieces = refs[:nt]
    sy_ref, sz_ref, clos_ref, kih_ref, kil_ref, kxh_ref, kxl_ref = refs[nt : nt + 7]
    outs = refs[nt + 7 : 2 * nt + 7]
    f_s, cl, t_s, u_s, amp_s = refs[2 * nt + 7 :]
    tiles = hy // SUB
    gather_windows(nt, q_ref[0], pieces, u_s, amp_s)
    factor_into(f_s, sx_ref, diff_ref, sy_ref[...], sz_ref[...])
    ha = nx // 2
    for j in range(tiles):
        rows = slice(j * SUB, (j + 1) * SUB)
        for par in range(2):
            modes = [par * ha + i for i in range(ha)]
            s = [s_ref[a, rows, :] for a in modes]
            f = [f_s[a, rows, :] for a in modes]

            def window(w, cur, j=j, par=par, rows=rows, modes=modes, s=s, f=f):
                cur = list(cur)
                for k in range(steps):
                    r0 = u_s[w, 0, k, pl.ds(j, SUB, stride=tiles), :]
                    r1 = u_s[w, 1, k, pl.ds(j, SUB, stride=tiles), :]
                    u = r0 + r1 if par == 0 else r0 - r1
                    amp = amp_s[w, k : k + 1, :]
                    cur = [(x + (amp * y + u)) * z for x, y, z in zip(cur, s, f)]
                for a, x in zip(modes, cur):
                    cl[w, a, rows, :] = x
                return tuple(cur)

            lax.fori_loop(0, nt, window, tuple(m_ref[a, rows, :] for a in modes))
    pack = kih_ref.shape[0] // hy
    half = pack * hy
    for e in range(0, nt, 2):
        ws = [jnp.bitwise_xor(q_ref[0], e + i) for i in range(2)]

        def yback(ag, _, ws=ws):
            at = pl.ds(ag * pack, pack)
            cols = [
                jnp.concatenate([clos_ref[w, at].reshape(half, cq), cl[w, at].reshape(half, cq)], axis=0)
                for w in ws
            ]
            res = const_times(kih_ref[...], kil_ref[...], jnp.concatenate(cols, axis=1))
            t_s[at] = res.reshape(pack, hy, 2 * cq)
            return 0

        lax.fori_loop(0, nx // pack, yback, 0)
        for yb in range(tiles):
            x = t_s[:, yb * SUB : (yb + 1) * SUB, :].reshape(nx * SUB, 2 * cq)
            res = const_times(kxh_ref[...], kxl_ref[...], x).reshape(nx, SUB, 2 * cq)
            for i in range(2):
                outs[e + i][:, yb * SUB : (yb + 1) * SUB, :] = res[:, :, i * cq : (i + 1) * cq]


def final_kernel(nt, q_ref, *refs):
    ws, ins, out_ref, wh, wl = refs[:nt], refs[nt : 2 * nt], refs[2 * nt], refs[2 * nt + 1], refs[2 * nt + 2]
    xb, hy, nz = out_ref.shape[1:]
    cq = nz // nt

    @pl.when(pl.program_id(0) == 0)
    def _():
        for d in range(nt):
            wh[d * cq : (d + 1) * cq, :] = ws[d][0]
            wl[d * cq : (d + 1) * cq, :] = ws[d][1]

    xh, xl = cut(jnp.concatenate([x[...].reshape(xb * hy, cq) for x in ins], axis=1))
    res = mm(xh, wh[...]) + mm(xh, wl[...]) + mm(xl, wh[...])
    out_ref[0] = res.reshape(xb, hy, nz)


def deal_kernel(nt, steps, q_ref, f0_ref, f1_ref, *outs):
    for d in range(nt):
        w = jnp.bitwise_xor(q_ref[0], d)
        outs[d][0] = f0_ref[pl.ds(w * steps, steps)]
        outs[d][1] = f1_ref[pl.ds(w * steps, steps)]


def spread_kernel(nt, steps, q_ref, tab_ref, *refs):
    ins, out_ref, slots, line = refs[:nt], refs[nt], refs[nt + 1], refs[nt + 2]
    hy = out_ref.shape[3]
    cq = out_ref.shape[4] // nt
    tiles = hy // SUB
    for d in range(nt):
        slots[jnp.bitwise_xor(q_ref[0], d)] = ins[d][...]
    for face in range(2):
        base = 3 * hy + face * (tiles - 1) * SUB
        le = [tab_ref[base + i * SUB : base + (i + 1) * SUB, :] > 0.5 for i in range(tiles - 1)]
        zero = jnp.zeros((SUB, cq), F32)
        for c in range(nt):

            def step(k, _, face=face, c=c):
                r = [slots[c, face, k, i * SUB : (i + 1) * SUB, :] for i in range(tiles - 1)]
                for j in range(tiles):
                    if j == 0:
                        v = jnp.where(le[0], zero, r[0])
                    elif j < tiles - 1:
                        v = jnp.where(le[j], jnp.where(le[j - 1], r[j - 1], zero), r[j])
                    else:
                        v = jnp.where(le[j - 1], r[j - 1], zero)
                    line[face, k, pl.ds(j, SUB, stride=tiles), :] = v
                out_ref[0, face, k, :, c * cq : (c + 1) * cq] = line[face, k]
                return 0

            lax.fori_loop(0, steps, step, 0)


def sds(*shape):
    return jax.ShapeDtypeStruct(shape, F32)


def cost(flops, nbytes):
    return pl.CostEstimate(flops=int(flops), bytes_accessed=int(nbytes), transcendentals=0)


def grant(mib):
    return pltpu.CompilerParams(vmem_limit_bytes=mib << 20)


def local(
    initial_state,
    heat_source,
    source_amplitude,
    diffusivity,
    robin_param,
    spectrum_x,
    spectrum_y,
    spectrum_z,
    robin_in,
    open_flag,
    owner_side,
):
    nx, hy, nz = initial_state.shape
    nt = lax.axis_size("tm")
    ncores = lax.axis_size("cores")
    assert ncores == 2 and nt & (nt - 1) == 0 and nt >= 2
    ny = hy * ncores
    cq = nz // nt
    steps = source_amplitude.shape[0]
    tiles = hy // SUB
    assert tiles == 4 and nx % 4 == 0
    q = lax.axis_index("tm")
    yc = lax.axis_index("cores")
    space = lax.axis_size("space")
    me = lax.axis_index("space")
    left_index = (me + space - 1) % space
    qv = jnp.reshape(q, (1,)).astype(jnp.int32)
    dims = (nt, steps, nx, hy, cq)
    ha = nx // 2
    tied = lax.optimization_barrier

    def xor_permute(x, d):
        return lax.ppermute(x, "tm", [(i, i ^ d) for i in range(nt)])

    def swap(x):
        return lax.ppermute(x, "cores", [(0, 1), (1, 0)])

    def along(x, by):
        return lax.ppermute(x, "space", [(i, (i + by) % space) for i in range(space)])

    rows = 2 * steps * hy
    block = (None, 2, steps, hy, cq)
    cuts = pl.pallas_call(
        functools.partial(split_kernel, nt),
        out_shape=[sds(rows + steps, cq)] * nt,
        grid_spec=pltpu.PrefetchScalarGridSpec(
            num_scalar_prefetch=1,
            grid=(1,),
            in_specs=[SM]
            + [
                pl.BlockSpec(block, lambda i, q, d=d: (0, 0, 0, 0, jnp.bitwise_xor(q[0], d)))
                for d in range(nt)
            ],
            out_specs=[pl.BlockSpec((rows + steps, cq), lambda i, q: (0, 0))] * nt,
        ),
        compiler_params=grant(8),
        cost_estimate=cost(0, 8 * nt * rows * cq),
        name="split",
    )(qv, source_amplitude, *([robin_in] * nt))
    there = [swap(cuts[0])]
    dealt = [cuts[0]] + [xor_permute(cuts[d], d) for d in range(1, nt)]

    base = np.stack(np_halves(np_cosine(nz, np.arange(nz)[:, None], np.arange(nz)[None])))
    base = jnp.asarray(base.reshape(2, nt, cq, nz).swapaxes(0, 1))
    kxh, kxl = (jnp.asarray(w) for w in np_bar(nx, False))
    kxih, kxil = (jnp.asarray(w) for w in np_bar(nx, True))
    whole = lambda shape: pl.BlockSpec(shape, lambda i, q: (0,) * len(shape))

    def forward(values):
        return pl.pallas_call(
            forward_kernel,
            out_shape=sds(nx, hy, cq),
            grid_spec=pltpu.PrefetchScalarGridSpec(
                num_scalar_prefetch=1,
                grid=(tiles,),
                in_specs=[
                    pl.BlockSpec((nx, SUB, nz), lambda i, q: (0, i, 0)),
                    pl.BlockSpec((None, 2, cq, nz), lambda i, q: (q[0], 0, 0, 0)),
                    whole((nx * SUB, nx * SUB)),
                    whole((nx * SUB, nx * SUB)),
                ],
                out_specs=pl.BlockSpec((nx, SUB, cq), lambda i, q: (0, i, 0)),
            ),
            compiler_params=grant(8),
            cost_estimate=cost(1e9, 3e6),
        )(qv, values, base, kxh, kxl)

    n0 = forward(initial_state)
    n1 = swap(n0)
    s0 = forward(tied((heat_source, n0))[0])
    s1 = swap(s0)
    there += [swap(dealt[d]) for d in range(1, nt)]

    robin_param, spectrum_y, spectrum_x, spectrum_z, open_flag, owner_side, yc, _ = tied(
        (robin_param, spectrum_y, spectrum_x, spectrum_z, open_flag, owner_side, yc, s0)
    )
    right_param = along(robin_param, -1)
    left_param = along(robin_param, 1)
    params = jnp.concatenate([left_param, robin_param, right_param])
    sy_there = swap(spectrum_y)

    pack = 256 // (2 * hy)
    half = pack * hy

    def mode_of(i):
        side = jnp.where(i // half == 0, yc, 1 - yc)
        line = i % hy
        return side * hy + tiles * (line % (hy // tiles)) + line // (hy // tiles)

    def node_of(i):
        return jnp.where(i // half == 0, yc, 1 - yc) * hy + i % hy

    r, c = iotas(2 * half, 2 * half)
    same = (r // hy) % pack == (c // hy) % pack
    kyh, kyl = halves(jnp.where(same, cosine(ny, mode_of(r), node_of(c)), 0.0))
    r, c = iotas(half, 2 * half)
    same = (r // hy) % pack == (c // hy) % pack
    kih, kil = halves(jnp.where(same, cosine(ny, mode_of(c), node_of(r)), 0.0))

    def lanes(v):
        return jnp.broadcast_to(v[:, None], v.shape + (cq,)).astype(F32)

    def modes_by_tile(v):
        return jnp.swapaxes(v.reshape(-1, hy // tiles, tiles), -1, -2).reshape(-1)

    sx = jnp.swapaxes(spectrum_x.reshape(ha, 2), 0, 1).reshape(nx)
    sz = lax.dynamic_slice_in_dim(spectrum_z, q * cq, cq, 0)[None]
    pick = lambda v: jnp.concatenate(
        [lax.dynamic_slice_in_dim(v, left_index, 1, 0), lax.dynamic_slice_in_dim(v, me, 1, 0)]
    )
    opened = pick(open_flag).reshape(2, hy // tiles, tiles)
    closed = jnp.stack(
        [jnp.any(opened[:, :, : i + 1] == 0, axis=2) for i in range(tiles - 1)], axis=1
    )
    flat = jnp.concatenate(
        [
            modes_by_tile(spectrum_y),
            modes_by_tile(pick(owner_side).astype(F32)),
            closed.astype(F32).reshape(-1),
        ]
    )
    tab = lanes(flat)
    sy_there = lanes(modes_by_tile(sy_there))
    a = np_modes(nx)
    first = np_cosine(nx, a, np.zeros(nx))
    second = np_cosine(nx, a, np.ones(nx))
    fill = lambda v: jnp.asarray(np.broadcast_to(v[:, None, None], (nx, SUB, cq)).astype(np.float32))
    wv, wd = fill(first * first), fill(first * (second - first))

    scratch = [pltpu.VMEM((nt, 2, steps, hy, cq), F32), pltpu.VMEM((nt, steps, cq), F32)]
    ql, qr, clos, m_there, s_there = pl.pallas_call(
        functools.partial(own_kernel, dims),
        out_shape=[sds(nt * steps, (tiles - 1) * SUB, cq)] * 2
        + [sds(nt, nx, hy, cq), sds(nx, hy, cq), sds(nx, hy, cq)],
        in_specs=[SM] * 4 + [VM] * (10 + nt),
        out_specs=[VM] * 5,
        scratch_shapes=[pltpu.VMEM((nx, hy, cq), F32)] * 3
        + [pltpu.VMEM((2, 2, nt * steps, tiles, SUB, cq), F32)]
        + scratch,
        compiler_params=grant(20),
        cost_estimate=cost(4e9, 8e6),
        name="own",
    )(qv, sx, diffusivity, params, n0, s0, n1, s1, *dealt, tab, sz, kyh, kyl, wv, wd)
    to_left = along(ql, -1)
    to_right = along(qr, 1)

    other = pl.pallas_call(
        functools.partial(other_kernel, dims),
        out_shape=[sds(nx, hy, cq)] * nt,
        in_specs=[SM] * 3 + [VM] * (9 + nt),
        out_specs=[VM] * nt,
        scratch_shapes=[
            pltpu.VMEM((nx, hy, cq), F32),
            pltpu.VMEM((nt, nx, hy, cq), F32),
            pltpu.VMEM((nx, hy, 2 * cq), F32),
        ]
        + scratch,
        compiler_params=grant(20),
        cost_estimate=cost(6e9, 8e6),
        name="other",
    )
    outs = other(qv, sx, diffusivity, m_there, s_there, *there, sy_there, sz, clos, kih, kil, kxih, kxil)
    ends = [outs[0]] + [xor_permute(outs[d], d) for d in range(1, nt)]

    short = sds(2, steps, (tiles - 1) * SUB, cq)
    hands = pl.pallas_call(
        functools.partial(deal_kernel, nt, steps),
        out_shape=[short] * nt,
        in_specs=[SM, VM, VM],
        out_specs=[VM] * nt,
        compiler_params=grant(8),
        cost_estimate=cost(0, 2e6),
        name="deal",
    )(qv, to_right, to_left)
    hands = [hands[0]] + [xor_permute(hands[d], d) for d in range(1, nt)]

    xb = SUB
    window_end = pl.pallas_call(
        functools.partial(final_kernel, nt),
        out_shape=sds(1, nx, hy, nz),
        grid_spec=pltpu.PrefetchScalarGridSpec(
            num_scalar_prefetch=1,
            grid=(nx // xb,),
            in_specs=[
                pl.BlockSpec((None, 2, cq, nz), lambda i, q, d=d: (jnp.bitwise_xor(q[0], d), 0, 0, 0))
                for d in range(nt)
            ]
            + [pl.BlockSpec((xb, hy, cq), lambda i, q: (i, 0, 0))] * nt,
            out_specs=pl.BlockSpec((1, xb, hy, nz), lambda i, q: (0, i, 0, 0)),
            scratch_shapes=[pltpu.VMEM((nz, nz), BF16)] * 2,
        ),
        compiler_params=grant(16),
        cost_estimate=cost(2e9, 6e6),
        name="final",
    )(qv, *([base] * nt), *ends)

    robin_out = pl.pallas_call(
        functools.partial(spread_kernel, nt, steps),
        out_shape=sds(1, 2, steps, hy, nz),
        in_specs=[SM] + [VM] * (nt + 1),
        out_specs=VM,
        scratch_shapes=[
            pltpu.VMEM((nt,) + short.shape, F32),
            pltpu.VMEM((2, steps, hy, cq), F32),
        ],
        compiler_params=grant(8),
        cost_estimate=cost(0, 2e6),
        name="spread",
    )(qv, tab, *hands)
    return robin_out, window_end


def solution(mesh):
    placed = (
        P("space", "cores", None),
        P("space", "cores", None),
        P("tm"),
        P("space"),
        P("space"),
        P(),
        P("cores"),
        P(),
        P("space", None, "tm", "cores", None),
        P(None, "cores"),
        P(None, "cores"),
    )

    return jax.shard_map(
        local,
        mesh=mesh,
        in_specs=placed,
        out_specs=(P("space", None, "tm", "cores", None), P("tm", "space", "cores", None)),
        check_vma=False,
    )
```

```python
import functools
import jax
import numpy as np
import jax.numpy as jnp
from jax import lax
from jax.experimental import pallas as pl
from jax.experimental.pallas import tpu as pltpu
from jax.sharding import PartitionSpec as P


F32 = jnp.float32
BF16 = jnp.bfloat16
SUB = 8


VM = pl.BlockSpec(memory_space=pltpu.VMEM)
SM = pl.BlockSpec(memory_space=pltpu.SMEM)


def cosine(order, mode, node):
    mode = mode.astype(F32)
    node = node.astype(F32)
    scaling = jnp.where(mode == 0, jnp.sqrt(1.0 / order), jnp.sqrt(2.0 / order))
    return scaling * jnp.cos(jnp.pi * mode * (node + 0.5) / order)


def halves(w):
    hi = lax.reduce_precision(w, exponent_bits=8, mantissa_bits=7)
    return hi.astype(BF16), (w - hi).astype(BF16)


def iotas(rows, cols):
    shape = (rows, cols)
    return lax.broadcasted_iota(jnp.int32, shape, 0), lax.broadcasted_iota(jnp.int32, shape, 1)


def cut(x):
    hi = x.astype(BF16)
    return hi, (x - hi.astype(F32)).astype(BF16)


def mm(a, b):
    return jnp.dot(a, b, preferred_element_type=F32)


def mmt(a, b):
    return lax.dot_general(a, b, (((1,), (1,)), ((), ())), preferred_element_type=F32)


def const_times(wh, wl, x):
    xh, xl = cut(x)
    return mm(wh, xh) + mm(wh, xl) + mm(wl, xh)


def np_cosine(order, mode, node):
    mode = np.asarray(mode, np.float32)
    node = np.asarray(node, np.float32)
    scaling = np.where(mode == 0, np.sqrt(np.float32(1.0 / order)), np.sqrt(np.float32(2.0 / order)))
    angle = np.float32(np.pi) * mode * (node + np.float32(0.5)) / np.float32(order)
    return (scaling * np.cos(angle.astype(np.float64))).astype(np.float32)


def np_halves(w):
    hi = w.astype(BF16)
    return hi, (w - hi.astype(np.float32)).astype(BF16)


def np_modes(n):
    return np.concatenate([np.arange(0, n, 2), np.arange(1, n, 2)])


def np_bar(n, back):
    a = np_modes(n)
    base = np_cosine(n, a[:, None], np.arange(n)[None])
    edge = np_cosine(n, a, np.zeros(n))[:, None]
    w = (base * edge).T if back else base / edge
    return np_halves(np.kron(w, np.eye(SUB, dtype=np.float32)))


def tree(parts):
    while len(parts) > 1:
        parts = [a + b for a, b in zip(parts[::2], parts[1::2])] + (
            [parts[-1]] if len(parts) % 2 else []
        )
    return parts[0]


def split_kernel(nt, q_ref, amp_ref, *refs):
    ins, outs = refs[:nt], refs[nt:]
    steps = amp_ref.shape[0]
    rows = outs[0].shape[0] - steps
    cq = outs[0].shape[1]
    for d in range(nt):
        outs[d][0:rows, :] = ins[d][...].reshape(rows, cq)
        for k in range(steps):
            outs[d][rows + k : rows + k + 1, :] = jnp.full((1, cq), amp_ref[k], F32)


def forward_kernel(q_ref, x_ref, c_ref, kxh_ref, kxl_ref, out_ref):
    nx, _, nz = x_ref.shape
    cq = out_ref.shape[-1]
    xh, xl = cut(x_ref[...].reshape(nx * SUB, nz))
    both = mmt(xh, c_ref[...].reshape(2 * cq, nz))
    z = both[:, :cq] + both[:, cq:] + mmt(xl, c_ref[0])
    zh, zl = cut(z)
    both = mm(kxh_ref[...], jnp.concatenate([zh, zl], axis=1))
    res = both[:, :cq] + both[:, cq:] + mm(kxl_ref[...], zh)
    out_ref[...] = res.reshape(nx, SUB, cq)


def factor_into(f_ref, sx_ref, diff_ref, sy, sz):
    for a in range(f_ref.shape[0]):
        rate = (sx_ref[a] + sy) + sz
        f_ref[a] = 1.0 / (1.0 + diff_ref[0] * rate)


def order_kernel(nt, q_ref, *refs):
    ins, u_ref, amp_ref, outs = refs[:nt], refs[nt], refs[nt + 1], refs[nt + 2 :]
    steps = amp_ref.shape[1]
    rows = ins[0].shape[0] - steps
    for d in range(nt):
        w = jnp.bitwise_xor(q_ref[0], d)
        u_ref[w] = ins[d][0:rows, :].reshape(u_ref.shape[1:])
        amp_ref[w] = ins[d][rows:, :]
    for w in range(nt):
        outs[w][...] = u_ref[w]


def own_kernel(dims, q_ref, sx_ref, diff_ref, par_ref, *refs):
    nt, steps, nx, hy, cq = dims
    n0, s0, n1, s1, u_s, amp_s, tab_ref, sz_ref, kyh_ref, kyl_ref, wv_ref, wd_ref = refs[:12]
    hands, (clos_ref, mo_ref, so_ref) = refs[12 : 12 + nt], refs[12 + nt : 15 + nt]
    m_s, s_s, f_s, vd = refs[15 + nt :]
    tiles = hy // SUB
    pack = kyh_ref.shape[0] // (2 * hy)
    half = pack * hy

    factor_into(f_s, sx_ref, diff_ref, tab_ref[0:hy, :], sz_ref[...])

    def ytrans(ag, _):
        at = pl.ds(ag * pack, pack)
        cols = [
            jnp.concatenate([here[at].reshape(half, cq), there[at].reshape(half, cq)], axis=0)
            for here, there in ((n0, n1), (s0, s1))
        ]
        res = const_times(kyh_ref[...], kyl_ref[...], jnp.concatenate(cols, axis=1))
        for f, own, oth in ((0, m_s, mo_ref), (1, s_s, so_ref)):
            part = res[:, f * cq : (f + 1) * cq]
            own[at] = part[:half].reshape(pack, hy, cq)
            oth[at] = part[half:].reshape(pack, hy, cq)
        return 0

    lax.fori_loop(0, nx // pack, ytrans, 0)
    ha = nx // 2
    chunk = min(SUB, ha)
    for j in range(tiles):
        rows = slice(j * SUB, (j + 1) * SUB)
        for par in range(2):
            for first in range(0, ha, chunk):
                modes = [par * ha + first + i for i in range(chunk)]
                s = [s_s[a, rows, :] for a in modes]
                f = [f_s[a, rows, :] for a in modes]
                wv = [wv_ref[a] for a in modes]
                wd = [wd_ref[a] for a in modes]

                def window(w, cur, j=j, par=par, first=first, rows=rows, modes=modes, s=s, f=f, wv=wv, wd=wd):
                    cur = list(cur)
                    for k in range(steps):
                        r0 = u_s[w, 0, k, pl.ds(j, SUB, stride=tiles), :]
                        r1 = u_s[w, 1, k, pl.ds(j, SUB, stride=tiles), :]
                        u = r0 + r1 if par == 0 else r0 - r1
                        amp = amp_s[w, k : k + 1, :]
                        cur = [(x + (amp * y + u)) * z for x, y, z in zip(cur, s, f)]
                        m = w * steps + k
                        v = tree([x * y for x, y in zip(cur, wv)])
                        d = tree([x * y for x, y in zip(cur, wd)])
                        if first:
                            v = v + vd[par, 0, m, j]
                            d = d + vd[par, 1, m, j]
                        vd[par, 0, m, j] = v
                        vd[par, 1, m, j] = d
                    for a, x in zip(modes, cur):
                        clos_ref[w, a, rows, :] = x
                    return tuple(cur)

                lax.fori_loop(0, nt, window, tuple(m_s[a, rows, :] for a in modes))

    owner, closed = tab_ref.at[hy : 3 * hy], tab_ref.at[3 * hy :]

    for slot in range(nt):
        w = jnp.bitwise_xor(q_ref[0], slot)

        def combine(k, _, slot=slot, w=w):
            m = w * steps + k
            left, right = [], []
            for j in range(tiles):
                ve, vo = vd[0, 0, m, j], vd[1, 0, m, j]
                de, do = vd[0, 1, m, j], vd[1, 1, m, j]
                p = [
                    jnp.where(owner[i * hy + j * SUB : i * hy + (j + 1) * SUB, :] < 0.5, par_ref[i], par_ref[i + 1])
                    for i in range(2)
                ]
                left.append((de + do) + p[0] * (ve + vo))
                right.append(p[1] * (ve - vo) + (de - do))
            for face, line in enumerate((left, right)):
                for i in range(tiles - 1):
                    at = (face * (tiles - 1) + i) * SUB
                    le = closed[at : at + SUB, :] > 0.5
                    hands[slot][face, k, i * SUB : (i + 1) * SUB, :] = jnp.where(le, line[i + 1], line[i])
            return 0

        lax.fori_loop(0, steps, combine, 0)


def other_kernel(dims, first, last, q_ref, sx_ref, diff_ref, m_ref, s_ref, *refs):
    nt, steps, nx, hy, cq = dims
    count = last - first
    us = refs[:count]
    amp_ref, sy_ref, sz_ref, clos_ref, kih_ref, kil_ref, kxh_ref, kxl_ref = refs[count : count + 8]
    nout = nt if count > 1 else 1
    outs = refs[count + 8 : count + 8 + nout]
    st_ref, f_s, cl, t_s, u_s = refs[count + 8 + nout :]
    tiles = hy // SUB
    for i in range(count):
        u_s[i] = us[i][...]
    factor_into(f_s, sx_ref, diff_ref, sy_ref[...], sz_ref[...])
    ha = nx // 2
    for j in range(tiles):
        rows = slice(j * SUB, (j + 1) * SUB)
        for par in range(2):
            modes = [par * ha + i for i in range(ha)]
            s = [s_ref[a, rows, :] for a in modes]
            f = [f_s[a, rows, :] for a in modes]

            def window(w, cur, j=j, par=par, rows=rows, modes=modes, s=s, f=f):
                cur = list(cur)
                for k in range(steps):
                    r0 = u_s[w, 0, k, pl.ds(j, SUB, stride=tiles), :]
                    r1 = u_s[w, 1, k, pl.ds(j, SUB, stride=tiles), :]
                    u = r0 + r1 if par == 0 else r0 - r1
                    amp = amp_ref[w + first, k : k + 1, :]
                    cur = [(x + (amp * y + u)) * z for x, y, z in zip(cur, s, f)]
                for a, x in zip(modes, cur):
                    cl[w, a, rows, :] = x
                return tuple(cur)

            end = lax.fori_loop(0, count, window, tuple(m_ref[a, rows, :] for a in modes))
            for a, x in zip(modes, end):
                st_ref[a, rows, :] = x
    pack = kih_ref.shape[0] // hy
    half = pack * hy
    for e in range(0, nout, 2):
        if count > 1:
            ws = [jnp.minimum(jnp.bitwise_xor(q_ref[0], e + i), last - 1) for i in range(2)]
        else:
            ws = [first]
        width = len(ws) * cq

        def yback(ag, _, ws=ws, width=width):
            at = pl.ds(ag * pack, pack)
            cols = [
                jnp.concatenate(
                    [clos_ref[w, at].reshape(half, cq), cl[w - first, at].reshape(half, cq)], axis=0
                )
                for w in ws
            ]
            res = const_times(kih_ref[...], kil_ref[...], jnp.concatenate(cols, axis=1))
            t_s[at] = res.reshape(pack, hy, width)
            return 0

        lax.fori_loop(0, nx // pack, yback, 0)
        for yb in range(tiles):
            x = t_s[:, yb * SUB : (yb + 1) * SUB, :].reshape(nx * SUB, width)
            res = const_times(kxh_ref[...], kxl_ref[...], x).reshape(nx, SUB, width)
            for i in range(len(ws)):
                outs[e + i][:, yb * SUB : (yb + 1) * SUB, :] = res[:, :, i * cq : (i + 1) * cq]


def final_kernel(nt, q_ref, *refs):
    ws, most, late = refs[:nt], refs[nt : 2 * nt], refs[2 * nt : 3 * nt]
    out_ref, wh, wl = refs[3 * nt :]
    xb, hy, nz = out_ref.shape[1:]
    cq = nz // nt

    @pl.when(pl.program_id(0) == 0)
    def _():
        for d in range(nt):
            wh[d * cq : (d + 1) * cq, :] = ws[d][0]
            wl[d * cq : (d + 1) * cq, :] = ws[d][1]

    is_last = q_ref[0] == nt - 1
    ins = [jnp.where(is_last, b[...], a[...]) for a, b in zip(most, late)]
    xh, xl = cut(jnp.concatenate([x.reshape(xb * hy, cq) for x in ins], axis=1))
    res = mm(xh, wh[...]) + mm(xh, wl[...]) + mm(xl, wh[...])
    out_ref[0] = res.reshape(xb, hy, nz)


def merge_kernel(nt, q_ref, *refs):
    ins, outs = refs[:nt], refs[nt:]
    for d in range(nt):
        for face in range(2):
            outs[face][jnp.bitwise_xor(q_ref[0], d)] = ins[d][face]


def spread_kernel(nt, steps, tab_ref, left_ref, right_ref, out_ref, line):
    hy = out_ref.shape[3]
    cq = out_ref.shape[4] // nt
    tiles = hy // SUB
    zero = jnp.zeros((SUB, cq), F32)
    for face, ref in enumerate((left_ref, right_ref)):
        base = 3 * hy + face * (tiles - 1) * SUB
        le = [tab_ref[base + i * SUB : base + (i + 1) * SUB, :] > 0.5 for i in range(tiles - 1)]
        for c in range(nt):

            def step(k, _, face=face, c=c, ref=ref, le=le):
                r = [ref[c, k, i * SUB : (i + 1) * SUB, :] for i in range(tiles - 1)]
                for j in range(tiles):
                    if j == 0:
                        v = jnp.where(le[0], zero, r[0])
                    elif j < tiles - 1:
                        v = jnp.where(le[j], jnp.where(le[j - 1], r[j - 1], zero), r[j])
                    else:
                        v = jnp.where(le[j - 1], r[j - 1], zero)
                    line[face, k, pl.ds(j, SUB, stride=tiles), :] = v
                out_ref[0, face, k, :, c * cq : (c + 1) * cq] = line[face, k]
                return 0

            lax.fori_loop(0, steps, step, 0)


def sds(*shape):
    return jax.ShapeDtypeStruct(shape, F32)


def cost(flops, nbytes):
    return pl.CostEstimate(flops=int(flops), bytes_accessed=int(nbytes), transcendentals=0)


def grant(mib):
    return pltpu.CompilerParams(vmem_limit_bytes=mib << 20)


def local(
    initial_state,
    heat_source,
    source_amplitude,
    diffusivity,
    robin_param,
    spectrum_x,
    spectrum_y,
    spectrum_z,
    robin_in,
    open_flag,
    owner_side,
):
    nx, hy, nz = initial_state.shape
    nt = lax.axis_size("tm")
    ncores = lax.axis_size("cores")
    assert ncores == 2 and nt & (nt - 1) == 0 and nt >= 2
    ny = hy * ncores
    cq = nz // nt
    steps = source_amplitude.shape[0]
    tiles = hy // SUB
    assert tiles == 4 and nx % 4 == 0
    q = lax.axis_index("tm")
    yc = lax.axis_index("cores")
    space = lax.axis_size("space")
    me = lax.axis_index("space")
    left_index = (me + space - 1) % space
    qv = jnp.reshape(q, (1,)).astype(jnp.int32)
    dims = (nt, steps, nx, hy, cq)
    ha = nx // 2
    tied = lax.optimization_barrier

    def xor_permute(x, d):
        return lax.ppermute(x, "tm", [(i, i ^ d) for i in range(nt)])

    def swap(x):
        return lax.ppermute(x, "cores", [(0, 1), (1, 0)])

    def along(x, by):
        return lax.ppermute(x, "space", [(i, (i + by) % space) for i in range(space)])

    rows = 2 * steps * hy
    block = (None, 2, steps, hy, cq)
    cuts = pl.pallas_call(
        functools.partial(split_kernel, nt),
        out_shape=[sds(rows + steps, cq)] * nt,
        grid_spec=pltpu.PrefetchScalarGridSpec(
            num_scalar_prefetch=1,
            grid=(1,),
            in_specs=[SM]
            + [
                pl.BlockSpec(block, lambda i, q, d=d: (0, 0, 0, 0, jnp.bitwise_xor(q[0], d)))
                for d in range(nt)
            ],
            out_specs=[pl.BlockSpec((rows + steps, cq), lambda i, q: (0, 0))] * nt,
        ),
        compiler_params=grant(8),
        cost_estimate=cost(0, 8 * nt * rows * cq),
        name="split",
    )(qv, source_amplitude, *([robin_in] * nt))
    dealt = [cuts[0]] + [xor_permute(cuts[d], d) for d in range(1, nt)]

    base = np.stack(np_halves(np_cosine(nz, np.arange(nz)[:, None], np.arange(nz)[None])))
    base = jnp.asarray(base.reshape(2, nt, cq, nz).swapaxes(0, 1))
    kxh, kxl = (jnp.asarray(w) for w in np_bar(nx, False))
    kxih, kxil = (jnp.asarray(w) for w in np_bar(nx, True))
    whole = lambda shape: pl.BlockSpec(shape, lambda i, q: (0,) * len(shape))

    def forward(values):
        return pl.pallas_call(
            forward_kernel,
            out_shape=sds(nx, hy, cq),
            grid_spec=pltpu.PrefetchScalarGridSpec(
                num_scalar_prefetch=1,
                grid=(tiles,),
                in_specs=[
                    pl.BlockSpec((nx, SUB, nz), lambda i, q: (0, i, 0)),
                    pl.BlockSpec((None, 2, cq, nz), lambda i, q: (q[0], 0, 0, 0)),
                    whole((nx * SUB, nx * SUB)),
                    whole((nx * SUB, nx * SUB)),
                ],
                out_specs=pl.BlockSpec((nx, SUB, cq), lambda i, q: (0, i, 0)),
            ),
            compiler_params=grant(56),
            cost_estimate=cost(1e9, 3e6),
        )(qv, values, base, kxh, kxl)

    n0 = forward(initial_state)
    n1 = swap(n0)
    s0 = forward(tied((heat_source, n0))[0])
    s1 = swap(s0)
    u_own, amps, *windows = pl.pallas_call(
        functools.partial(order_kernel, nt),
        out_shape=[sds(nt, 2, steps, hy, cq), sds(nt, steps, cq)] + [sds(2, steps, hy, cq)] * nt,
        in_specs=[SM] + [VM] * nt,
        out_specs=[VM] * (nt + 2),
        compiler_params=grant(10),
        cost_estimate=cost(0, 3e6),
        name="order",
    )(qv, *dealt)
    there = [swap(u) for u in windows]

    robin_param, spectrum_y, spectrum_x, spectrum_z, open_flag, owner_side, yc, _ = tied(
        (robin_param, spectrum_y, spectrum_x, spectrum_z, open_flag, owner_side, yc, s0)
    )
    right_param = along(robin_param, -1)
    left_param = along(robin_param, 1)
    params = jnp.concatenate([left_param, robin_param, right_param])
    sy_there = swap(spectrum_y)

    pack = 256 // (2 * hy)
    half = pack * hy

    def mode_of(i):
        side = jnp.where(i // half == 0, yc, 1 - yc)
        line = i % hy
        return side * hy + tiles * (line % (hy // tiles)) + line // (hy // tiles)

    def node_of(i):
        return jnp.where(i // half == 0, yc, 1 - yc) * hy + i % hy

    r, c = iotas(2 * half, 2 * half)
    same = (r // hy) % pack == (c // hy) % pack
    kyh, kyl = halves(jnp.where(same, cosine(ny, mode_of(r), node_of(c)), 0.0))
    r, c = iotas(half, 2 * half)
    same = (r // hy) % pack == (c // hy) % pack
    kih, kil = halves(jnp.where(same, cosine(ny, mode_of(c), node_of(r)), 0.0))

    def lanes(v):
        return jnp.broadcast_to(v[:, None], v.shape + (cq,)).astype(F32)

    def modes_by_tile(v):
        return jnp.swapaxes(v.reshape(-1, hy // tiles, tiles), -1, -2).reshape(-1)

    sx = jnp.swapaxes(spectrum_x.reshape(ha, 2), 0, 1).reshape(nx)
    sz = lax.dynamic_slice_in_dim(spectrum_z, q * cq, cq, 0)[None]
    pick = lambda v: jnp.concatenate(
        [lax.dynamic_slice_in_dim(v, left_index, 1, 0), lax.dynamic_slice_in_dim(v, me, 1, 0)]
    )
    opened = pick(open_flag).reshape(2, hy // tiles, tiles)
    closed = jnp.stack(
        [jnp.any(opened[:, :, : i + 1] == 0, axis=2) for i in range(tiles - 1)], axis=1
    )
    flat = jnp.concatenate(
        [
            modes_by_tile(spectrum_y),
            modes_by_tile(pick(owner_side).astype(F32)),
            closed.astype(F32).reshape(-1),
        ]
    )
    tab = lanes(flat)
    sy_there = lanes(modes_by_tile(sy_there))
    a = np_modes(nx)
    first = np_cosine(nx, a, np.zeros(nx))
    second = np_cosine(nx, a, np.ones(nx))
    fill = lambda v: jnp.asarray(np.broadcast_to(v[:, None, None], (nx, SUB, cq)).astype(np.float32))
    wv, wd = fill(first * first), fill(first * (second - first))

    short = sds(2, steps, (tiles - 1) * SUB, cq)
    *hands, clos, m_there, s_there = pl.pallas_call(
        functools.partial(own_kernel, dims),
        out_shape=[short] * nt + [sds(nt, nx, hy, cq), sds(nx, hy, cq), sds(nx, hy, cq)],
        in_specs=[SM] * 4 + [VM] * 12,
        out_specs=[VM] * (nt + 3),
        scratch_shapes=[pltpu.VMEM((nx, hy, cq), F32)] * 3
        + [pltpu.VMEM((2, 2, nt * steps, tiles, SUB, cq), F32)],
        compiler_params=grant(18),
        cost_estimate=cost(4e9, 8e6),
        name="own",
    )(qv, sx, diffusivity, params, n0, s0, n1, s1, u_own, amps, tab, sz, kyh, kyl, wv, wd)
    for d in range(1, nt):
        hands[d] = xor_permute(hands[d], d)

    def finish(first, last, state):
        count = last - first
        nout = nt if count > 1 else 1
        call = pl.pallas_call(
            functools.partial(other_kernel, dims, first, last),
            out_shape=[sds(nx, hy, cq)] * (nout + 1),
            in_specs=[SM] * 3 + [VM] * (10 + count),
            out_specs=[VM] * (nout + 1),
            scratch_shapes=[
                pltpu.VMEM((nx, hy, cq), F32),
                pltpu.VMEM((count, nx, hy, cq), F32),
                pltpu.VMEM((nx, hy, min(count, 2) * cq), F32),
                pltpu.VMEM((count, 2, steps, hy, cq), F32),
            ],
            compiler_params=grant(18),
            cost_estimate=cost(1.5e9 * count, 2e6 * count),
        )
        return call(
            qv, sx, diffusivity, state, s_there, *there[first:last], amps, sy_there, sz,
            clos, kih, kil, kxih, kxil,
        )

    final = nt - 1
    *most, state = finish(0, final, m_there)
    for d in range(1, nt):
        most[d] = lax.ppermute(most[d], "tm", [(i, i ^ d) for i in range(nt) if i ^ d != final])
    left, right = pl.pallas_call(
        functools.partial(merge_kernel, nt),
        out_shape=[sds(nt, steps, (tiles - 1) * SUB, cq)] * 2,
        in_specs=[SM] + [VM] * nt,
        out_specs=[VM] * 2,
        compiler_params=grant(8),
        cost_estimate=cost(0, 2e6),
        name="merge",
    )(qv, *hands)
    from_right = along(left, -1)
    from_left = along(right, 1)
    late, _ = finish(final, nt, state)
    late = [late]
    for d in range(1, nt):
        late.append(lax.ppermute(late[0], "tm", [(final ^ d, final)]))

    xb = SUB
    window_end = pl.pallas_call(
        functools.partial(final_kernel, nt),
        out_shape=sds(1, nx, hy, nz),
        grid_spec=pltpu.PrefetchScalarGridSpec(
            num_scalar_prefetch=1,
            grid=(nx // xb,),
            in_specs=[
                pl.BlockSpec((None, 2, cq, nz), lambda i, q, d=d: (jnp.bitwise_xor(q[0], d), 0, 0, 0))
                for d in range(nt)
            ]
            + [pl.BlockSpec((xb, hy, cq), lambda i, q: (i, 0, 0))] * (2 * nt),
            out_specs=pl.BlockSpec((1, xb, hy, nz), lambda i, q: (0, i, 0, 0)),
            scratch_shapes=[pltpu.VMEM((nz, nz), BF16)] * 2,
        ),
        compiler_params=grant(16),
        cost_estimate=cost(2e9, 6e6),
        name="final",
    )(qv, *([base] * nt), *most, *late)

    robin_out = pl.pallas_call(
        functools.partial(spread_kernel, nt, steps),
        out_shape=sds(1, 2, steps, hy, nz),
        in_specs=[VM] * 3,
        out_specs=VM,
        scratch_shapes=[pltpu.VMEM((2, steps, hy, cq), F32)],
        compiler_params=grant(8),
        cost_estimate=cost(0, 2e6),
        name="spread",
    )(tab, from_left, from_right)
    return robin_out, window_end


def solution(mesh):
    placed = (
        P("space", "cores", None),
        P("space", "cores", None),
        P("tm"),
        P("space"),
        P("space"),
        P(),
        P("cores"),
        P(),
        P("space", None, "tm", "cores", None),
        P(None, "cores"),
        P(None, "cores"),
    )

    return jax.shard_map(
        local,
        mesh=mesh,
        in_specs=placed,
        out_specs=(P("space", None, "tm", "cores", None), P("tm", "space", "cores", None)),
        check_vma=False,
    )
```

```python
import functools
import jax
import numpy as np
import jax.numpy as jnp
from jax import lax
from jax.experimental import pallas as pl
from jax.experimental.pallas import tpu as pltpu
from jax.sharding import PartitionSpec as P


F32 = jnp.float32
BF16 = jnp.bfloat16
SUB = 8


VM = pl.BlockSpec(memory_space=pltpu.VMEM)
SM = pl.BlockSpec(memory_space=pltpu.SMEM)


def cut(x):
    hi = x.astype(BF16)
    return hi, (x - hi.astype(F32)).astype(BF16)


def mm(a, b):
    return jnp.dot(a, b, preferred_element_type=F32)


def mmt(a, b):
    return lax.dot_general(a, b, (((1,), (1,)), ((), ())), preferred_element_type=F32)


def const_times(wh, wl, x):
    n = x.shape[1]
    xh, xl = cut(x)
    if n > 128:
        return mm(wh, xh) + mm(wh, xl) + mm(wl, xh)
    both = mm(wh, jnp.concatenate([xh, xl], axis=1))
    return both[:, :n] + both[:, n:] + mm(wl, xh)


def np_cosine(order, mode, node):
    mode = np.asarray(mode, np.float32)
    node = np.asarray(node, np.float32)
    scaling = np.where(mode == 0, np.sqrt(np.float32(1.0 / order)), np.sqrt(np.float32(2.0 / order)))
    angle = np.float32(np.pi) * mode * (node + np.float32(0.5)) / np.float32(order)
    return (scaling * np.cos(angle.astype(np.float64))).astype(np.float32)


def np_halves(w):
    hi = w.astype(BF16)
    return hi, (w - hi.astype(np.float32)).astype(BF16)


def np_modes(n):
    return np.concatenate([np.arange(0, n, 2), np.arange(1, n, 2)])


def np_bar(n, back):
    a = np_modes(n)
    base = np_cosine(n, a[:, None], np.arange(n)[None])
    edge = np_cosine(n, a, np.zeros(n))[:, None]
    w = (base * edge).T if back else base / edge
    return np_halves(np.kron(w, np.eye(SUB, dtype=np.float32)))


def np_second(hy):
    ny = 2 * hy
    pack = 256 // ny
    tiles = hy // SUB
    line = np.arange(hy)
    modes = tiles * (line % SUB) + line // SUB
    eye = np.eye(pack, dtype=np.float32)
    there, back = [], []
    for yc in range(2):
        sides = (yc, 1 - yc)
        blocks = [[np_cosine(ny, (m * hy + modes)[:, None], (n * hy + line)[None]) for n in sides] for m in sides]
        there.append(np.block([[np.kron(eye, b) for b in row] for row in blocks]))
        back.append(np.concatenate([np.kron(eye, row[0].T) for row in blocks], axis=1))
    return [np.stack([np_halves(w) for w in ws]) for ws in map(np.stack, (there, back))]


def tree(parts):
    while len(parts) > 1:
        parts = [a + b for a, b in zip(parts[::2], parts[1::2])] + (
            [parts[-1]] if len(parts) % 2 else []
        )
    return parts[0]


def split_kernel(nt, q_ref, amp_ref, *refs):
    ins, outs = refs[:nt], refs[nt:]
    steps = amp_ref.shape[0]
    rows = outs[0].shape[0] - steps
    cq = outs[0].shape[1]
    for d in range(nt):
        outs[d][0:rows, :] = ins[d][...].reshape(rows, cq)
        for k in range(steps):
            outs[d][rows + k : rows + k + 1, :] = jnp.full((1, cq), amp_ref[k], F32)


def forward_block(x, c_ref, kxh_ref, kxl_ref):
    nx, _, nz = x.shape
    cq = c_ref.shape[1]
    xh, xl = cut(x.reshape(nx * SUB, nz))
    both = mmt(xh, c_ref[...].reshape(2 * cq, nz))
    z = both[:, :cq] + both[:, cq:] + mmt(xl, c_ref[0])
    return const_times(kxh_ref[...], kxl_ref[...], z).reshape(nx, SUB, cq)


def forward_first_kernel(q_ref, sy_ref, x_hbm, c_hbm, kxh_hbm, kxl_hbm, out_ref, x_s, c_s, kxh_s, kxl_s, sem):
    tiles, nx, _, _ = x_s.shape
    hy = tiles * SUB
    cq = out_ref.shape[2]
    copies = [
        pltpu.make_async_copy(c_hbm.at[q_ref[0]], c_s, sem.at[0]),
        pltpu.make_async_copy(x_hbm.at[:, 0:SUB, :], x_s.at[0], sem.at[3]),
        pltpu.make_async_copy(kxh_hbm, kxh_s, sem.at[1]),
        pltpu.make_async_copy(kxl_hbm, kxl_s, sem.at[2]),
    ]
    copies += [
        pltpu.make_async_copy(x_hbm.at[:, t * SUB : (t + 1) * SUB, :], x_s.at[t], sem.at[3 + t])
        for t in range(1, tiles)
    ]
    for copy in copies:
        copy.start()
    for r in range(hy):
        b = tiles * (r % SUB) + r // SUB
        out_ref[nx, r : r + 1, :] = jnp.full((1, cq), sy_ref[b], F32)
    for copy in copies[:4]:
        copy.wait()
    for t in range(tiles):
        if t > 0:
            copies[3 + t].wait()
        out_ref[0:nx, t * SUB : (t + 1) * SUB, :] = forward_block(x_s[t], c_s, kxh_s, kxl_s)


def forward_kernel(q_ref, x_ref, c_ref, kxh_ref, kxl_ref, out_ref):
    tiles = x_ref.shape[1] // SUB
    for t in range(tiles):
        at = slice(t * SUB, (t + 1) * SUB)
        out_ref[:, at, :] = forward_block(x_ref[:, at, :], c_ref.at[q_ref[0]], kxh_ref, kxl_ref)


def factor_into(f_ref, sx_ref, diff_ref, sy, sz):
    for i, a in enumerate(np_modes(f_ref.shape[0])):
        rate = (sx_ref[int(a)] + sy) + sz
        f_ref[i] = 1.0 / (1.0 + diff_ref[0] * rate)


def order_kernel(nt, q_ref, faces_ref, sx_ref, sy_ref, diff_ref, open_ref, owner_ref, sz_ref, n1_ref, *refs):
    ins, (u_ref, amp_ref, tab_ref, fo_ref, ft_ref), outs = refs[:nt], refs[nt : nt + 5], refs[nt + 5 :]
    steps = amp_ref.shape[1]
    rows = ins[0].shape[0] - steps
    nx, hy, cq = fo_ref.shape
    tiles = hy // SUB
    for d in range(nt):
        w = jnp.bitwise_xor(q_ref[0], d)
        u_ref[w] = ins[d][0:rows, :].reshape(u_ref.shape[1:])
        amp_ref[w] = ins[d][rows:, :]
    w = 0
    for out in outs:
        out[...] = u_ref[w : w + out.shape[0]]
        w += out.shape[0]
    for face in range(2):
        i = faces_ref[face]
        for g in range(hy // tiles):
            closed = False
            for j in range(tiles):
                b = tiles * g + j
                r = face * hy + j * SUB + g
                tab_ref[r : r + 1, :] = jnp.full((1, cq), owner_ref[i, b], jnp.int32)
                closed = jnp.logical_or(closed, open_ref[i, b] == 0)
                if j < tiles - 1:
                    r = 2 * hy + (face * (tiles - 1) + j) * SUB + g
                    tab_ref[r : r + 1, :] = jnp.full((1, cq), closed.astype(jnp.int32), jnp.int32)
    sz = sz_ref[pl.ds(q_ref[0], 1), :]
    for r in range(hy):
        b = tiles * (r % SUB) + r // SUB
        fo_ref[0, r : r + 1, :] = jnp.full((1, cq), sy_ref[b], F32)
    factor_into(fo_ref, sx_ref, diff_ref, fo_ref[0], sz)
    factor_into(ft_ref, sx_ref, diff_ref, n1_ref[nx], sz)


def closed_rows(tab_ref, face, tiles, hy):
    base = 2 * hy + face * (tiles - 1) * SUB
    return [tab_ref[base + i * SUB : base + (i + 1) * SUB, :] > 0 for i in range(tiles - 1)]


def own_kernel(dims, q_ref, yc_ref, p0_ref, p1_ref, p2_ref, *refs):
    nt, steps, nx, hy, cq = dims
    n0, s0, n1, s1, u_s, amp_s, tab_ref, f_s, ky_ref = refs[:9]
    hands, (clos_ref, mo_ref, so_ref) = refs[9 : 9 + nt], refs[9 + nt : 12 + nt]
    m_s, s_s, vd = refs[12 + nt :]
    tiles = hy // SUB
    pack = ky_ref.shape[2] // (2 * hy)
    half = pack * hy
    yc = yc_ref[0]

    def ytrans(ag, _):
        at = pl.ds(ag * pack, pack)
        cols = [
            jnp.concatenate([here[at].reshape(half, cq), there[at].reshape(half, cq)], axis=0)
            for here, there in ((n0, n1), (s0, s1))
        ]
        res = const_times(ky_ref[yc, 0], ky_ref[yc, 1], jnp.concatenate(cols, axis=1))
        for f, own, oth in ((0, m_s, mo_ref), (1, s_s, so_ref)):
            part = res[:, f * cq : (f + 1) * cq]
            own[at] = part[:half].reshape(pack, hy, cq)
            oth[at] = part[half:].reshape(pack, hy, cq)
        return 0

    lax.fori_loop(0, nx // pack, ytrans, 0)
    ha = nx // 2
    chunk = min(SUB, ha)
    order = np_modes(nx)
    edge = np_cosine(nx, order, np.zeros(nx)).astype(np.float64)
    slope = np_cosine(nx, order, np.ones(nx)).astype(np.float64) - edge
    for j in range(tiles):
        rows = slice(j * SUB, (j + 1) * SUB)
        for par in range(2):
            for first in range(0, ha, chunk):
                modes = [par * ha + first + i for i in range(chunk)]
                s = [s_s[a, rows, :] for a in modes]
                f = [f_s[a, rows, :] for a in modes]
                wv = [float(np.float32(edge[a] * edge[a])) for a in modes]
                wd = [float(np.float32(edge[a] * slope[a])) for a in modes]

                def window(w, cur, j=j, par=par, first=first, rows=rows, modes=modes, s=s, f=f, wv=wv, wd=wd):
                    cur = list(cur)
                    for k in range(steps):
                        r0 = u_s[w, 0, k, pl.ds(j, SUB, stride=tiles), :]
                        r1 = u_s[w, 1, k, pl.ds(j, SUB, stride=tiles), :]
                        u = r0 + r1 if par == 0 else r0 - r1
                        amp = amp_s[w, k : k + 1, :]
                        cur = [(x + (amp * y + u)) * z for x, y, z in zip(cur, s, f)]
                        m = w * steps + k
                        v = tree([x * y for x, y in zip(cur, wv)])
                        d = tree([x * y for x, y in zip(cur, wd)])
                        if first:
                            v = v + vd[par, 0, m, j]
                            d = d + vd[par, 1, m, j]
                        vd[par, 0, m, j] = v
                        vd[par, 1, m, j] = d
                    for a, x in zip(modes, cur):
                        clos_ref[w, a, rows, :] = x
                    return tuple(cur)

                lax.fori_loop(0, nt, window, tuple(m_s[a, rows, :] for a in modes))

    params = (p0_ref[0], p1_ref[0], p2_ref[0])
    for slot in range(nt):
        w = jnp.bitwise_xor(q_ref[0], slot)

        def combine(k, _, slot=slot, w=w):
            m = w * steps + k
            left, right = [], []
            for j in range(tiles):
                ve, vo = vd[0, 0, m, j], vd[1, 0, m, j]
                de, do = vd[0, 1, m, j], vd[1, 1, m, j]
                p = [
                    jnp.where(
                        tab_ref[i * hy + j * SUB : i * hy + (j + 1) * SUB, :] == 0, params[i], params[i + 1]
                    )
                    for i in range(2)
                ]
                left.append((de + do) + p[0] * (ve + vo))
                right.append(p[1] * (ve - vo) + (de - do))
            for face, line in enumerate((left, right)):
                for i, le in enumerate(closed_rows(tab_ref, face, tiles, hy)):
                    hands[slot][face, k, i * SUB : (i + 1) * SUB, :] = jnp.where(le, line[i + 1], line[i])
            return 0

        lax.fori_loop(0, steps, combine, 0)


def other_kernel(dims, first, count, prior, q_ref, yc_ref, m_ref, s_ref, f_ref, u_s, amp_ref, clos_ref, ki_ref, kxh_ref, kxl_ref, *refs):
    nt, steps, nx, hy, cq = dims
    refs = refs[prior:]
    last = first + count == nt
    outs = refs[: 1 if last else nt]
    st_ref, cl, t_s, x_s = refs[len(outs) :]
    tiles = hy // SUB
    ha = nx // 2
    for j in range(tiles):
        rows = slice(j * SUB, (j + 1) * SUB)
        for par in range(2):
            modes = [par * ha + i for i in range(ha)]
            s = [s_ref[a, rows, :] for a in modes]
            f = [f_ref[a, rows, :] for a in modes]

            def window(w, cur, j=j, par=par, rows=rows, modes=modes, s=s, f=f):
                cur = list(cur)
                for k in range(steps):
                    r0 = u_s[w, 0, k, pl.ds(j, SUB, stride=tiles), :]
                    r1 = u_s[w, 1, k, pl.ds(j, SUB, stride=tiles), :]
                    u = r0 + r1 if par == 0 else r0 - r1
                    amp = amp_ref[w + first, k : k + 1, :]
                    cur = [(x + (amp * y + u)) * z for x, y, z in zip(cur, s, f)]
                for a, x in zip(modes, cur):
                    cl[w, a, rows, :] = x
                return tuple(cur)

            end = lax.fori_loop(0, count, window, tuple(m_ref[a, rows, :] for a in modes))
            for a, x in zip(modes, end):
                st_ref[a, rows, :] = x
    pack = ki_ref.shape[2] // hy
    half = pack * hy
    width = count * cq
    yc = yc_ref[0]

    def yback(ag, _):
        at = pl.ds(ag * pack, pack)
        cols = [
            jnp.concatenate([clos_ref[first + w, at].reshape(half, cq), cl[w, at].reshape(half, cq)], axis=0)
            for w in range(count)
        ]
        res = const_times(ki_ref[yc, 0], ki_ref[yc, 1], jnp.concatenate(cols, axis=1))
        t_s[at] = res.reshape(pack, hy, width)
        return 0

    lax.fori_loop(0, nx // pack, yback, 0)
    for yb in range(tiles):
        at = slice(yb * SUB, (yb + 1) * SUB)
        res = const_times(kxh_ref[...], kxl_ref[...], t_s[:, at, :].reshape(nx * SUB, width))
        res = res.reshape(nx, SUB, width)
        for w in range(count):
            (outs[0] if last else x_s.at[w])[:, at, :] = res[:, :, w * cq : (w + 1) * cq]
    if not last:
        for w in range(count):
            for d in range(nt):

                @pl.when(jnp.bitwise_xor(q_ref[0], d) == first + w)
                def _(w=w, d=d):
                    outs[d][...] = x_s[w]


def final_kernel(nt, q_ref, *refs):
    ws, most, late = refs[:nt], refs[nt : 2 * nt], refs[2 * nt : 3 * nt]
    out_ref, wh, wl = refs[3 * nt :]
    xb, hy, nz = out_ref.shape[1:]
    cq = nz // nt

    @pl.when(pl.program_id(0) == 0)
    def _():
        for d in range(nt):
            wh[d * cq : (d + 1) * cq, :] = ws[d][0]
            wl[d * cq : (d + 1) * cq, :] = ws[d][1]

    is_last = q_ref[0] == nt - 1
    ins = [jnp.where(is_last, b[...], a[...]) for a, b in zip(most, late)]
    xh, xl = cut(jnp.concatenate([x.reshape(xb * hy, cq) for x in ins], axis=1))
    res = mm(xh, wh[...]) + mm(xh, wl[...]) + mm(xl, wh[...])
    out_ref[0] = res.reshape(xb, hy, nz)


def merge_kernel(nt, q_ref, *refs):
    ins, outs = refs[:nt], refs[nt:]
    for d in range(nt):
        for face in range(2):
            outs[face][jnp.bitwise_xor(q_ref[0], d)] = ins[d][face]


def spread_kernel(nt, steps, tab_ref, left_ref, right_ref, out_ref, line):
    hy = out_ref.shape[3]
    cq = out_ref.shape[4] // nt
    tiles = hy // SUB
    zero = jnp.zeros((SUB, cq), F32)
    for face, ref in enumerate((left_ref, right_ref)):
        le = closed_rows(tab_ref, face, tiles, hy)
        for c in range(nt):

            def step(k, _, face=face, c=c, ref=ref, le=le):
                r = [ref[c, k, i * SUB : (i + 1) * SUB, :] for i in range(tiles - 1)]
                for j in range(tiles):
                    if j == 0:
                        v = jnp.where(le[0], zero, r[0])
                    elif j < tiles - 1:
                        v = jnp.where(le[j], jnp.where(le[j - 1], r[j - 1], zero), r[j])
                    else:
                        v = jnp.where(le[j - 1], r[j - 1], zero)
                    line[face, k, pl.ds(j, SUB, stride=tiles), :] = v
                out_ref[0, face, k, :, c * cq : (c + 1) * cq] = line[face, k]
                return 0

            lax.fori_loop(0, steps, step, 0)


def sds(*shape):
    return jax.ShapeDtypeStruct(shape, F32)


def cost(flops, nbytes):
    return pl.CostEstimate(flops=int(flops), bytes_accessed=int(nbytes), transcendentals=0)


def grant(mib):
    return pltpu.CompilerParams(vmem_limit_bytes=mib << 20)


def local(
    initial_state,
    heat_source,
    source_amplitude,
    diffusivity,
    robin_param,
    spectrum_x,
    spectrum_y,
    spectrum_z,
    robin_in,
    open_flag,
    owner_side,
):
    nx, hy, nz = initial_state.shape
    nt = lax.axis_size("tm")
    ncores = lax.axis_size("cores")
    assert ncores == 2 and nt & (nt - 1) == 0 and nt >= 2
    cq = nz // nt
    steps = source_amplitude.shape[0]
    tiles = hy // SUB
    assert tiles == 4 and nx % 4 == 0
    q = lax.axis_index("tm")
    yc = lax.axis_index("cores")
    space = lax.axis_size("space")
    me = lax.axis_index("space")
    left_index = (me + space - 1) % space
    qv = jnp.reshape(q, (1,)).astype(jnp.int32)
    dims = (nt, steps, nx, hy, cq)

    def xor_permute(x, d):
        return lax.ppermute(x, "tm", [(i, i ^ d) for i in range(nt)])

    def swap(x):
        return lax.ppermute(x, "cores", [(0, 1), (1, 0)])

    def along(x, by):
        return lax.ppermute(x, "space", [(i, (i + by) % space) for i in range(space)])

    base = np.stack(np_halves(np_cosine(nz, np.arange(nz)[:, None], np.arange(nz)[None])))
    base = jnp.asarray(base.reshape(2, nt, cq, nz).swapaxes(0, 1))
    kxh, kxl = (jnp.asarray(w) for w in np_bar(nx, False))
    kxih, kxil = (jnp.asarray(w) for w in np_bar(nx, True))
    ky, ki = (jnp.asarray(w) for w in np_second(hy))
    HB = pl.BlockSpec(memory_space=pltpu.HBM)
    n0 = pl.pallas_call(
        forward_first_kernel,
        out_shape=sds(nx + 1, hy, cq),
        in_specs=[SM, SM] + [HB] * 4,
        out_specs=VM,
        scratch_shapes=[
            pltpu.VMEM((tiles, nx, SUB, nz), F32),
            pltpu.VMEM((2, cq, nz), BF16),
            pltpu.VMEM((nx * SUB, nx * SUB), BF16),
            pltpu.VMEM((nx * SUB, nx * SUB), BF16),
            pltpu.SemaphoreType.DMA((3 + tiles,)),
        ],
        compiler_params=grant(8),
        cost_estimate=cost(1e9, 3e6),
        name="forward0",
    )(qv, spectrum_y, initial_state, base, kxh, kxl)
    n1 = swap(n0)

    rows = 2 * steps * hy
    block = (None, 2, steps, hy, cq)
    cutting = pl.pallas_call(
        functools.partial(split_kernel, nt),
        out_shape=[sds(rows + steps, cq)] * nt,
        grid_spec=pltpu.PrefetchScalarGridSpec(
            num_scalar_prefetch=1,
            grid=(1,),
            in_specs=[SM]
            + [
                pl.BlockSpec(block, lambda i, q, d=d: (0, 0, 0, 0, jnp.bitwise_xor(q[0], d)))
                for d in range(nt)
            ],
            out_specs=[pl.BlockSpec((rows + steps, cq), lambda i, q: (0, 0))] * nt,
        ),
        compiler_params=grant(8),
        cost_estimate=cost(0, 8 * nt * rows * cq),
        name="split",
    )
    dealt = list(cutting(qv, source_amplitude, *([robin_in] * nt)))
    for d in range(1, nt):
        dealt[d] = xor_permute(dealt[d], d)

    s0 = pl.pallas_call(
        forward_kernel,
        out_shape=sds(nx, hy, cq),
        in_specs=[SM] + [VM] * 4,
        out_specs=VM,
        compiler_params=grant(10),
        cost_estimate=cost(1e9, 3e6),
        name="forward1",
    )(qv, heat_source, base, kxh, kxl)
    s1 = swap(s0)
    right_param = along(robin_param, -1)
    left_param = along(robin_param, 1)

    faces = jnp.stack([left_index, me]).astype(jnp.int32)
    ycv = jnp.reshape(yc, (1,)).astype(jnp.int32)
    counts = [nt - 2] + [1, 1]
    counts = [c for c in counts if c > 0]
    table = jax.ShapeDtypeStruct((2 * hy + 2 * (tiles - 1) * SUB, cq), jnp.int32)
    u_own, amps, tab, f_own, f_there, *windows = pl.pallas_call(
        functools.partial(order_kernel, nt),
        out_shape=[sds(nt, 2, steps, hy, cq), sds(nt, steps, cq), table]
        + [sds(nx, hy, cq)] * 2
        + [sds(c, 2, steps, hy, cq) for c in counts],
        in_specs=[SM] * 7 + [VM] * (2 + nt),
        out_specs=[VM] * (5 + len(counts)),
        compiler_params=grant(12),
        cost_estimate=cost(0, 3e6),
        name="order",
    )(
        qv, faces, spectrum_x, spectrum_y, diffusivity, open_flag, owner_side,
        spectrum_z.reshape(nt, cq), n1, *dealt,
    )
    there = []
    for u in windows:
        there.append(swap(u))

    short = sds(2, steps, (tiles - 1) * SUB, cq)
    *hands, clos, m_there, s_there = pl.pallas_call(
        functools.partial(own_kernel, dims),
        out_shape=[short] * nt + [sds(nt, nx, hy, cq), sds(nx, hy, cq), sds(nx, hy, cq)],
        in_specs=[SM] * 5 + [VM] * 9,
        out_specs=[VM] * (nt + 3),
        scratch_shapes=[pltpu.VMEM((nx, hy, cq), F32)] * 2
        + [pltpu.VMEM((2, 2, nt * steps, tiles, SUB, cq), F32)],
        compiler_params=grant(18),
        cost_estimate=cost(4e9, 8e6),
        name="own",
    )(qv, ycv, left_param, robin_param, right_param, n0, s0, n1, s1, u_own, amps, tab, f_own, ky)
    for d in range(1, nt):
        hands[d] = xor_permute(hands[d], d)

    state, most, first = m_there, [], 0
    final = nt - 1
    for i, count in enumerate(counts):
        last = first + count == nt
        nout = 1 if last else nt
        operands = (
            qv, ycv, state, s_there, f_there, there[i], amps, clos, ki, kxih, kxil, *([] if last else most),
        )
        prior = 0 if last else len(most)
        *outs, state = pl.pallas_call(
            functools.partial(other_kernel, dims, first, count, prior),
            out_shape=[sds(nx, hy, cq)] * (nout + 1),
            in_specs=[SM] * 2 + [VM] * (9 + prior),
            out_specs=[VM] * (nout + 1),
            scratch_shapes=[
                pltpu.VMEM((count, nx, hy, cq), F32),
                pltpu.VMEM((nx, hy, count * cq), F32),
                pltpu.VMEM((count, nx, hy, cq), F32),
            ],
            input_output_aliases={11 + d: d for d in range(prior)},
            compiler_params=grant(18),
            cost_estimate=cost(1.5e9 * count, 2e6 * count),
        )(*operands)
        first += count
        if not last:
            most = list(outs)
            continue
        late = list(outs)
    for d in range(1, nt):
        most[d] = lax.ppermute(most[d], "tm", [(i, i ^ d) for i in range(nt) if i ^ d != final])
    left, right = pl.pallas_call(
        functools.partial(merge_kernel, nt),
        out_shape=[sds(nt, steps, (tiles - 1) * SUB, cq)] * 2,
        in_specs=[SM] + [VM] * nt,
        out_specs=[VM] * 2,
        compiler_params=grant(8),
        cost_estimate=cost(0, 2e6),
        name="merge",
    )(qv, *hands)
    from_right = along(left, -1)
    from_left = along(right, 1)
    for d in range(1, nt):
        late.append(lax.ppermute(late[0], "tm", [(final ^ d, final)]))

    xb = SUB
    window_end = pl.pallas_call(
        functools.partial(final_kernel, nt),
        out_shape=sds(1, nx, hy, nz),
        grid_spec=pltpu.PrefetchScalarGridSpec(
            num_scalar_prefetch=1,
            grid=(nx // xb,),
            in_specs=[
                pl.BlockSpec((None, 2, cq, nz), lambda i, q, d=d: (jnp.bitwise_xor(q[0], d), 0, 0, 0))
                for d in range(nt)
            ]
            + [pl.BlockSpec((xb, hy, cq), lambda i, q: (i, 0, 0))] * (2 * nt),
            out_specs=pl.BlockSpec((1, xb, hy, nz), lambda i, q: (0, i, 0, 0)),
            scratch_shapes=[pltpu.VMEM((nz, nz), BF16)] * 2,
        ),
        compiler_params=grant(16),
        cost_estimate=cost(2e9, 6e6),
        name="final",
    )(qv, *([base] * nt), *most, *late)

    robin_out = pl.pallas_call(
        functools.partial(spread_kernel, nt, steps),
        out_shape=sds(1, 2, steps, hy, nz),
        in_specs=[VM] * 3,
        out_specs=VM,
        scratch_shapes=[pltpu.VMEM((2, steps, hy, cq), F32)],
        compiler_params=grant(8),
        cost_estimate=cost(0, 2e6),
        name="spread",
    )(tab, from_left, from_right)
    return robin_out, window_end


def solution(mesh):
    placed = (
        P("space", "cores", None),
        P("space", "cores", None),
        P("tm"),
        P("space"),
        P("space"),
        P(),
        P("cores"),
        P(),
        P("space", None, "tm", "cores", None),
        P(None, "cores"),
        P(None, "cores"),
    )

    return jax.shard_map(
        local,
        mesh=mesh,
        in_specs=placed,
        out_specs=(P("space", None, "tm", "cores", None), P("tm", "space", "cores", None)),
        check_vma=False,
    )
```

```python
import functools
import jax
import numpy as np
import jax.numpy as jnp
from jax import lax
from jax.experimental import pallas as pl
from jax.experimental.pallas import tpu as pltpu
from jax.sharding import PartitionSpec as P


F32 = jnp.float32
BF16 = jnp.bfloat16
SUB = 8


VM = pl.BlockSpec(memory_space=pltpu.VMEM)
SM = pl.BlockSpec(memory_space=pltpu.SMEM)


def cut(x):
    hi = x.astype(BF16)
    return hi, (x - hi.astype(F32)).astype(BF16)


def mm(a, b):
    return jnp.dot(a, b, preferred_element_type=F32)


def mmt(a, b):
    return lax.dot_general(a, b, (((1,), (1,)), ((), ())), preferred_element_type=F32)


def const_times(wh, wl, x):
    n = x.shape[1]
    xh, xl = cut(x)
    if n > 128:
        return mm(wh, xh) + mm(wh, xl) + mm(wl, xh)
    both = mm(wh, jnp.concatenate([xh, xl], axis=1))
    return both[:, :n] + both[:, n:] + mm(wl, xh)


def np_cosine(order, mode, node):
    mode = np.asarray(mode, np.float32)
    node = np.asarray(node, np.float32)
    scaling = np.where(mode == 0, np.sqrt(np.float32(1.0 / order)), np.sqrt(np.float32(2.0 / order)))
    angle = np.float32(np.pi) * mode * (node + np.float32(0.5)) / np.float32(order)
    return (scaling * np.cos(angle.astype(np.float64))).astype(np.float32)


def np_halves(w):
    hi = w.astype(BF16)
    return hi, (w - hi.astype(np.float32)).astype(BF16)


def np_modes(n):
    return np.concatenate([np.arange(0, n, 2), np.arange(1, n, 2)])


def np_bar(n, back):
    a = np_modes(n)
    base = np_cosine(n, a[:, None], np.arange(n)[None])
    edge = np_cosine(n, a, np.zeros(n))[:, None]
    w = (base * edge).T if back else base / edge
    return np_halves(np.kron(w, np.eye(SUB, dtype=np.float32)))


def np_second(hy):
    ny = 2 * hy
    pack = 256 // ny
    tiles = hy // SUB
    line = np.arange(hy)
    modes = tiles * (line % SUB) + line // SUB
    eye = np.eye(pack, dtype=np.float32)
    there, back = [], []
    for yc in range(2):
        sides = (yc, 1 - yc)
        blocks = [[np_cosine(ny, (m * hy + modes)[:, None], (n * hy + line)[None]) for n in sides] for m in sides]
        there.append(np.block([[np.kron(eye, b) for b in row] for row in blocks]))
        back.append(np.concatenate([np.kron(eye, row[0].T) for row in blocks], axis=1))
    return [np.stack([np_halves(w) for w in ws]) for ws in map(np.stack, (there, back))]


def tree(parts):
    while len(parts) > 1:
        parts = [a + b for a, b in zip(parts[::2], parts[1::2])] + (
            [parts[-1]] if len(parts) % 2 else []
        )
    return parts[0]


def split_kernel(nt, q_ref, amp_ref, *refs):
    ins, outs = refs[:nt], refs[nt:]
    steps = amp_ref.shape[0]
    rows = outs[0].shape[0] - steps
    cq = outs[0].shape[1]
    for d in range(nt):
        outs[d][0:rows, :] = ins[d][...].reshape(rows, cq)
        for k in range(steps):
            outs[d][rows + k : rows + k + 1, :] = jnp.full((1, cq), amp_ref[k], F32)


def forward_block(x, c_ref, kxh_ref, kxl_ref):
    nx, _, nz = x.shape
    cq = c_ref.shape[1]
    xh, xl = cut(x.reshape(nx * SUB, nz))
    both = mmt(xh, c_ref[...].reshape(2 * cq, nz))
    z = both[:, :cq] + both[:, cq:] + mmt(xl, c_ref[0])
    return const_times(kxh_ref[...], kxl_ref[...], z).reshape(nx, SUB, cq)


def forward_first_kernel(
    q_ref, yc_ref, me_ref, sy_ref, diff_ref, par_ref, x_hbm, c_hbm, kxh_hbm, kxl_hbm,
    out_ref, diff_out, par_out, x_s, c_s, kxh_s, kxl_s, sem,
):
    tiles, nx, _, _ = x_s.shape
    hy = tiles * SUB
    cq = out_ref.shape[2]
    copies = [
        pltpu.make_async_copy(c_hbm.at[q_ref[0]], c_s, sem.at[0]),
        pltpu.make_async_copy(x_hbm.at[:, 0:SUB, :], x_s.at[0], sem.at[3]),
        pltpu.make_async_copy(kxh_hbm, kxh_s, sem.at[1]),
        pltpu.make_async_copy(kxl_hbm, kxl_s, sem.at[2]),
    ]
    copies += [
        pltpu.make_async_copy(x_hbm.at[:, t * SUB : (t + 1) * SUB, :], x_s.at[t], sem.at[3 + t])
        for t in range(1, tiles)
    ]
    for copy in copies:
        copy.start()
    for r in range(hy):
        b = tiles * (r % SUB) + r // SUB
        out_ref[nx, r : r + 1, :] = jnp.full((1, cq), sy_ref[b], F32)
    diff_out[...] = jnp.full(diff_out.shape, diff_ref[0], F32)
    par_out[...] = jnp.full(par_out.shape, par_ref[0], F32)
    for copy in copies[:4]:
        copy.wait()
    for t in range(tiles):
        if t > 0:
            copies[3 + t].wait()
        out_ref[0:nx, t * SUB : (t + 1) * SUB, :] = forward_block(x_s[t], c_s, kxh_s, kxl_s)


def forward_kernel(q_ref, x_ref, c_ref, kxh_ref, kxl_ref, out_ref):
    tiles = x_ref.shape[1] // SUB
    for t in range(tiles):
        at = slice(t * SUB, (t + 1) * SUB)
        out_ref[:, at, :] = forward_block(x_ref[:, at, :], c_ref.at[q_ref[0]], kxh_ref, kxl_ref)


def factor_into(f_ref, sx_ref, diff_ref, sy, sz):
    for i, a in enumerate(np_modes(f_ref.shape[0])):
        rate = (sx_ref[int(a)] + sy) + sz
        f_ref[i] = 1.0 / (1.0 + diff_ref[0:1, :] * rate)


def order_kernel(nt, space, q_ref, me_ref, sx_ref, sy_ref, open_ref, owner_ref, diff_ref, sz_ref, n1_ref, *refs):
    ins, (u_ref, amp_ref, tab_ref, fo_ref, ft_ref), outs = refs[:nt], refs[nt : nt + 5], refs[nt + 5 :]
    steps = amp_ref.shape[1]
    rows = ins[0].shape[0] - steps
    nx, hy, cq = fo_ref.shape
    tiles = hy // SUB
    for d in range(nt):
        w = jnp.bitwise_xor(q_ref[0], d)
        u_ref[w] = ins[d][0:rows, :].reshape(u_ref.shape[1:])
        amp_ref[w] = ins[d][rows:, :]
    w = 0
    for out in outs:
        out[...] = u_ref[w : w + out.shape[0]]
        w += out.shape[0]
    for face in range(2):
        i = lax.rem(me_ref[0] + space - 1, space) if face == 0 else me_ref[0]
        for g in range(hy // tiles):
            closed = False
            for j in range(tiles):
                b = tiles * g + j
                r = face * hy + j * SUB + g
                tab_ref[r : r + 1, :] = jnp.full((1, cq), owner_ref[i, b], jnp.int32)
                closed = jnp.logical_or(closed, open_ref[i, b] == 0)
                if j < tiles - 1:
                    r = 2 * hy + (face * (tiles - 1) + j) * SUB + g
                    tab_ref[r : r + 1, :] = jnp.full((1, cq), closed.astype(jnp.int32), jnp.int32)
    sz = sz_ref[pl.ds(q_ref[0], 1), :]
    for r in range(hy):
        b = tiles * (r % SUB) + r // SUB
        fo_ref[0, r : r + 1, :] = jnp.full((1, cq), sy_ref[b], F32)
    factor_into(fo_ref, sx_ref, diff_ref, fo_ref[0], sz)
    factor_into(ft_ref, sx_ref, diff_ref, n1_ref[nx], sz)


def closed_rows(tab_ref, face, tiles, hy):
    base = 2 * hy + face * (tiles - 1) * SUB
    return [tab_ref[base + i * SUB : base + (i + 1) * SUB, :] > 0 for i in range(tiles - 1)]


def own_kernel(dims, q_ref, yc_ref, *refs):
    nt, steps, nx, hy, cq = dims
    params, (n0, s0, n1, s1, u_s, amp_s, tab_ref, f_s, ky_ref) = refs[:3], refs[3:12]
    hands, (clos_ref, mo_ref, so_ref) = refs[12 : 12 + nt], refs[12 + nt : 15 + nt]
    m_s, s_s, vd = refs[15 + nt :]
    tiles = hy // SUB
    pack = ky_ref.shape[2] // (2 * hy)
    half = pack * hy
    yc = yc_ref[0]

    def ytrans(ag, _):
        at = pl.ds(ag * pack, pack)
        cols = [
            jnp.concatenate([here[at].reshape(half, cq), there[at].reshape(half, cq)], axis=0)
            for here, there in ((n0, n1), (s0, s1))
        ]
        res = const_times(ky_ref[yc, 0], ky_ref[yc, 1], jnp.concatenate(cols, axis=1))
        for f, own, oth in ((0, m_s, mo_ref), (1, s_s, so_ref)):
            part = res[:, f * cq : (f + 1) * cq]
            own[at] = part[:half].reshape(pack, hy, cq)
            oth[at] = part[half:].reshape(pack, hy, cq)
        return 0

    lax.fori_loop(0, nx // pack, ytrans, 0)
    ha = nx // 2
    chunk = min(SUB, ha)
    order = np_modes(nx)
    edge = np_cosine(nx, order, np.zeros(nx)).astype(np.float64)
    slope = np_cosine(nx, order, np.ones(nx)).astype(np.float64) - edge
    for j in range(tiles):
        rows = slice(j * SUB, (j + 1) * SUB)
        for par in range(2):
            for first in range(0, ha, chunk):
                modes = [par * ha + first + i for i in range(chunk)]
                s = [s_s[a, rows, :] for a in modes]
                f = [f_s[a, rows, :] for a in modes]
                wv = [float(np.float32(edge[a] * edge[a])) for a in modes]
                wd = [float(np.float32(edge[a] * slope[a])) for a in modes]

                def window(w, cur, j=j, par=par, first=first, rows=rows, modes=modes, s=s, f=f, wv=wv, wd=wd):
                    cur = list(cur)
                    for k in range(steps):
                        r0 = u_s[w, 0, k, pl.ds(j, SUB, stride=tiles), :]
                        r1 = u_s[w, 1, k, pl.ds(j, SUB, stride=tiles), :]
                        u = r0 + r1 if par == 0 else r0 - r1
                        amp = amp_s[w, k : k + 1, :]
                        cur = [(x + (amp * y + u)) * z for x, y, z in zip(cur, s, f)]
                        m = w * steps + k
                        v = tree([x * y for x, y in zip(cur, wv)])
                        d = tree([x * y for x, y in zip(cur, wd)])
                        if first:
                            v = v + vd[par, 0, m, j]
                            d = d + vd[par, 1, m, j]
                        vd[par, 0, m, j] = v
                        vd[par, 1, m, j] = d
                    for a, x in zip(modes, cur):
                        clos_ref[w, a, rows, :] = x
                    return tuple(cur)

                lax.fori_loop(0, nt, window, tuple(m_s[a, rows, :] for a in modes))

    params = [ref[...] for ref in params]
    for slot in range(nt):
        w = jnp.bitwise_xor(q_ref[0], slot)

        def combine(k, _, slot=slot, w=w):
            m = w * steps + k
            left, right = [], []
            for j in range(tiles):
                ve, vo = vd[0, 0, m, j], vd[1, 0, m, j]
                de, do = vd[0, 1, m, j], vd[1, 1, m, j]
                p = [
                    jnp.where(
                        tab_ref[i * hy + j * SUB : i * hy + (j + 1) * SUB, :] == 0, params[i], params[i + 1]
                    )
                    for i in range(2)
                ]
                left.append((de + do) + p[0] * (ve + vo))
                right.append(p[1] * (ve - vo) + (de - do))
            for face, line in enumerate((left, right)):
                for i, le in enumerate(closed_rows(tab_ref, face, tiles, hy)):
                    hands[slot][face, k, i * SUB : (i + 1) * SUB, :] = jnp.where(le, line[i + 1], line[i])
            return 0

        lax.fori_loop(0, steps, combine, 0)


def other_kernel(dims, first, count, prior, q_ref, yc_ref, m_ref, s_ref, f_ref, u_s, amp_ref, clos_ref, ki_ref, kxh_ref, kxl_ref, *refs):
    nt, steps, nx, hy, cq = dims
    refs = refs[prior:]
    outs = refs[:nt]
    st_ref, cl, t_s, x_s = refs[nt:]
    tiles = hy // SUB
    ha = nx // 2
    for j in range(tiles):
        rows = slice(j * SUB, (j + 1) * SUB)
        for par in range(2):
            modes = [par * ha + i for i in range(ha)]
            s = [s_ref[a, rows, :] for a in modes]
            f = [f_ref[a, rows, :] for a in modes]

            def window(w, cur, j=j, par=par, rows=rows, modes=modes, s=s, f=f):
                cur = list(cur)
                for k in range(steps):
                    r0 = u_s[w, 0, k, pl.ds(j, SUB, stride=tiles), :]
                    r1 = u_s[w, 1, k, pl.ds(j, SUB, stride=tiles), :]
                    u = r0 + r1 if par == 0 else r0 - r1
                    amp = amp_ref[w + first, k : k + 1, :]
                    cur = [(x + (amp * y + u)) * z for x, y, z in zip(cur, s, f)]
                for a, x in zip(modes, cur):
                    cl[w, a, rows, :] = x
                return tuple(cur)

            end = lax.fori_loop(0, count, window, tuple(m_ref[a, rows, :] for a in modes))
            for a, x in zip(modes, end):
                st_ref[a, rows, :] = x
    pack = ki_ref.shape[2] // hy
    half = pack * hy
    width = count * cq
    yc = yc_ref[0]

    def yback(ag, _):
        at = pl.ds(ag * pack, pack)
        cols = [
            jnp.concatenate([clos_ref[first + w, at].reshape(half, cq), cl[w, at].reshape(half, cq)], axis=0)
            for w in range(count)
        ]
        res = const_times(ki_ref[yc, 0], ki_ref[yc, 1], jnp.concatenate(cols, axis=1))
        t_s[at] = res.reshape(pack, hy, width)
        return 0

    lax.fori_loop(0, nx // pack, yback, 0)
    for yb in range(tiles):
        at = slice(yb * SUB, (yb + 1) * SUB)
        res = const_times(kxh_ref[...], kxl_ref[...], t_s[:, at, :].reshape(nx * SUB, width))
        res = res.reshape(nx, SUB, width)
        for w in range(count):
            x_s[w, :, at, :] = res[:, :, w * cq : (w + 1) * cq]
    for w in range(count):
        for d in range(nt):

            @pl.when(jnp.bitwise_xor(q_ref[0], d) == first + w)
            def _(w=w, d=d):
                outs[d][...] = x_s[w]


def final_kernel(nt, q_ref, *refs):
    ws, ins, (out_ref, wh, wl) = refs[:nt], refs[nt : 2 * nt], refs[2 * nt :]
    xb, hy, nz = out_ref.shape[1:]
    cq = nz // nt

    @pl.when(pl.program_id(0) == 0)
    def _():
        for d in range(nt):
            wh[d * cq : (d + 1) * cq, :] = ws[d][0]
            wl[d * cq : (d + 1) * cq, :] = ws[d][1]

    xh, xl = cut(jnp.concatenate([x[...].reshape(xb * hy, cq) for x in ins], axis=1))
    res = mm(xh, wh[...]) + mm(xh, wl[...]) + mm(xl, wh[...])
    out_ref[0] = res.reshape(xb, hy, nz)


def merge_kernel(nt, q_ref, *refs):
    ins, outs = refs[:nt], refs[nt:]
    for d in range(nt):
        for face in range(2):
            outs[face][jnp.bitwise_xor(q_ref[0], d)] = ins[d][face]


def spread_kernel(nt, steps, tab_ref, left_ref, right_ref, out_ref, line):
    hy = out_ref.shape[3]
    cq = out_ref.shape[4] // nt
    tiles = hy // SUB
    zero = jnp.zeros((SUB, cq), F32)
    for face, ref in enumerate((left_ref, right_ref)):
        le = closed_rows(tab_ref, face, tiles, hy)
        for c in range(nt):

            def step(k, _, face=face, c=c, ref=ref, le=le):
                r = [ref[c, k, i * SUB : (i + 1) * SUB, :] for i in range(tiles - 1)]
                for j in range(tiles):
                    if j == 0:
                        v = jnp.where(le[0], zero, r[0])
                    elif j < tiles - 1:
                        v = jnp.where(le[j], jnp.where(le[j - 1], r[j - 1], zero), r[j])
                    else:
                        v = jnp.where(le[j - 1], r[j - 1], zero)
                    line[face, k, pl.ds(j, SUB, stride=tiles), :] = v
                out_ref[0, face, k, :, c * cq : (c + 1) * cq] = line[face, k]
                return 0

            lax.fori_loop(0, steps, step, 0)


def sds(*shape):
    return jax.ShapeDtypeStruct(shape, F32)


def cost(flops, nbytes):
    return pl.CostEstimate(flops=int(flops), bytes_accessed=int(nbytes), transcendentals=0)


def grant(mib):
    return pltpu.CompilerParams(vmem_limit_bytes=mib << 20)


def local(
    initial_state,
    heat_source,
    source_amplitude,
    diffusivity,
    robin_param,
    spectrum_x,
    spectrum_y,
    spectrum_z,
    robin_in,
    open_flag,
    owner_side,
):
    nx, hy, nz = initial_state.shape
    nt = lax.axis_size("tm")
    ncores = lax.axis_size("cores")
    assert ncores == 2 and nt & (nt - 1) == 0 and nt >= 2
    cq = nz // nt
    steps = source_amplitude.shape[0]
    tiles = hy // SUB
    assert tiles == 4 and nx % 4 == 0
    q = lax.axis_index("tm")
    yc = lax.axis_index("cores")
    space = lax.axis_size("space")
    me = lax.axis_index("space")
    qv, ycv, mev = (jnp.reshape(i, (1,)).astype(jnp.int32) for i in (q, yc, me))
    dims = (nt, steps, nx, hy, cq)

    def xor_permute(x, d):
        return lax.ppermute(x, "tm", [(i, i ^ d) for i in range(nt)])

    def swap(x):
        return lax.ppermute(x, "cores", [(0, 1), (1, 0)])

    def along(x, by):
        return lax.ppermute(x, "space", [(i, (i + by) % space) for i in range(space)])

    base = np.stack(np_halves(np_cosine(nz, np.arange(nz)[:, None], np.arange(nz)[None])))
    base = jnp.asarray(base.reshape(2, nt, cq, nz).swapaxes(0, 1))
    kxh, kxl = (jnp.asarray(w) for w in np_bar(nx, False))
    kxih, kxil = (jnp.asarray(w) for w in np_bar(nx, True))
    ky, ki = (jnp.asarray(w) for w in np_second(hy))
    HB = pl.BlockSpec(memory_space=pltpu.HBM)
    n0, diff_rows, robin_param = pl.pallas_call(
        forward_first_kernel,
        out_shape=[sds(nx + 1, hy, cq), sds(SUB, cq), sds(SUB, cq)],
        in_specs=[SM] * 6 + [HB] * 4,
        out_specs=[VM] * 3,
        scratch_shapes=[
            pltpu.VMEM((tiles, nx, SUB, nz), F32),
            pltpu.VMEM((2, cq, nz), BF16),
            pltpu.VMEM((nx * SUB, nx * SUB), BF16),
            pltpu.VMEM((nx * SUB, nx * SUB), BF16),
            pltpu.SemaphoreType.DMA((3 + tiles,)),
        ],
        compiler_params=grant(60),
        cost_estimate=cost(1e9, 3e6),
        name="forward0",
    )(qv, ycv, mev, spectrum_y, diffusivity, robin_param, initial_state, base, kxh, kxl)
    n1 = swap(n0)

    rows = 2 * steps * hy
    block = (None, 2, steps, hy, cq)
    cutting = pl.pallas_call(
        functools.partial(split_kernel, nt),
        out_shape=[sds(rows + steps, cq)] * nt,
        grid_spec=pltpu.PrefetchScalarGridSpec(
            num_scalar_prefetch=1,
            grid=(1,),
            in_specs=[SM]
            + [
                pl.BlockSpec(block, lambda i, q, d=d: (0, 0, 0, 0, jnp.bitwise_xor(q[0], d)))
                for d in range(nt)
            ],
            out_specs=[pl.BlockSpec((rows + steps, cq), lambda i, q: (0, 0))] * nt,
        ),
        compiler_params=grant(18),
        cost_estimate=cost(0, 8 * nt * rows * cq),
        name="split",
    )
    dealt = list(cutting(qv, source_amplitude, *([robin_in] * nt)))
    for d in range(1, nt):
        dealt[d] = xor_permute(dealt[d], d)

    s0 = pl.pallas_call(
        forward_kernel,
        out_shape=sds(nx, hy, cq),
        in_specs=[SM] + [VM] * 4,
        out_specs=VM,
        compiler_params=grant(18),
        cost_estimate=cost(1e9, 3e6),
        name="forward1",
    )(qv, heat_source, base, kxh, kxl)
    s1 = swap(s0)
    right_param = along(robin_param, -1)
    left_param = along(robin_param, 1)

    counts = [nt - 2] + [1, 1]
    counts = [c for c in counts if c > 0]
    table = jax.ShapeDtypeStruct((2 * hy + 2 * (tiles - 1) * SUB, cq), jnp.int32)
    u_own, amps, tab, f_own, f_there, *windows = pl.pallas_call(
        functools.partial(order_kernel, nt, space),
        out_shape=[sds(nt, 2, steps, hy, cq), sds(nt, steps, cq), table]
        + [sds(nx, hy, cq)] * 2
        + [sds(c, 2, steps, hy, cq) for c in counts],
        in_specs=[SM] * 6 + [VM] * (3 + nt),
        out_specs=[VM] * (5 + len(counts)),
        compiler_params=grant(18),
        cost_estimate=cost(0, 3e6),
        name="order",
    )(
        qv, mev, spectrum_x, spectrum_y, open_flag, owner_side, diff_rows,
        spectrum_z.reshape(nt, cq), n1, *dealt,
    )
    there = []
    for u in windows:
        there.append(swap(u))

    short = sds(2, steps, (tiles - 1) * SUB, cq)
    *hands, clos, m_there, s_there = pl.pallas_call(
        functools.partial(own_kernel, dims),
        out_shape=[short] * nt + [sds(nt, nx, hy, cq), sds(nx, hy, cq), sds(nx, hy, cq)],
        in_specs=[SM] * 2 + [VM] * 12,
        out_specs=[VM] * (nt + 3),
        scratch_shapes=[pltpu.VMEM((nx, hy, cq), F32)] * 2
        + [pltpu.VMEM((2, 2, nt * steps, tiles, SUB, cq), F32)],
        compiler_params=grant(18),
        cost_estimate=cost(4e9, 8e6),
        name="own",
    )(qv, ycv, left_param, robin_param, right_param, n0, s0, n1, s1, u_own, amps, tab, f_own, ky)
    for d in range(1, nt):
        hands[d] = xor_permute(hands[d], d)

    state, ends, first = m_there, [], 0
    for i, count in enumerate(counts):
        *ends, state = pl.pallas_call(
            functools.partial(other_kernel, dims, first, count, len(ends)),
            out_shape=[sds(nx, hy, cq)] * (nt + 1),
            in_specs=[SM] * 2 + [VM] * (9 + len(ends)),
            out_specs=[VM] * (nt + 1),
            scratch_shapes=[
                pltpu.VMEM((count, nx, hy, cq), F32),
                pltpu.VMEM((nx, hy, count * cq), F32),
                pltpu.VMEM((count, nx, hy, cq), F32),
            ],
            input_output_aliases={11 + d: d for d in range(len(ends))},
            compiler_params=grant(18),
            cost_estimate=cost(1.5e9 * count, 2e6 * count),
        )(qv, ycv, state, s_there, f_there, there[i], amps, clos, ki, kxih, kxil, *ends)
        first += count
    for d in range(1, nt):
        ends[d] = xor_permute(ends[d], d)
    left, right = pl.pallas_call(
        functools.partial(merge_kernel, nt),
        out_shape=[sds(nt, steps, (tiles - 1) * SUB, cq)] * 2,
        in_specs=[SM] + [VM] * nt,
        out_specs=[VM] * 2,
        compiler_params=grant(18),
        cost_estimate=cost(0, 2e6),
        name="merge",
    )(qv, *hands)
    from_right = along(left, -1)
    from_left = along(right, 1)
    xb = SUB
    window_end = pl.pallas_call(
        functools.partial(final_kernel, nt),
        out_shape=sds(1, nx, hy, nz),
        grid_spec=pltpu.PrefetchScalarGridSpec(
            num_scalar_prefetch=1,
            grid=(nx // xb,),
            in_specs=[
                pl.BlockSpec((None, 2, cq, nz), lambda i, q, d=d: (jnp.bitwise_xor(q[0], d), 0, 0, 0))
                for d in range(nt)
            ]
            + [pl.BlockSpec((xb, hy, cq), lambda i, q: (i, 0, 0))] * nt,
            out_specs=pl.BlockSpec((1, xb, hy, nz), lambda i, q: (0, i, 0, 0)),
            scratch_shapes=[pltpu.VMEM((nz, nz), BF16)] * 2,
        ),
        compiler_params=grant(18),
        cost_estimate=cost(2e9, 6e6),
        name="final",
    )(qv, *([base] * nt), *ends)

    robin_out = pl.pallas_call(
        functools.partial(spread_kernel, nt, steps),
        out_shape=sds(1, 2, steps, hy, nz),
        in_specs=[VM] * 3,
        out_specs=VM,
        scratch_shapes=[pltpu.VMEM((2, steps, hy, cq), F32)],
        compiler_params=grant(18),
        cost_estimate=cost(0, 2e6),
        name="spread",
    )(tab, from_left, from_right)
    return robin_out, window_end


def solution(mesh):
    placed = (
        P("space", "cores", None),
        P("space", "cores", None),
        P("tm"),
        P("space"),
        P("space"),
        P(),
        P("cores"),
        P(),
        P("space", None, "tm", "cores", None),
        P(None, "cores"),
        P(None, "cores"),
    )

    return jax.shard_map(
        local,
        mesh=mesh,
        in_specs=placed,
        out_specs=(P("space", None, "tm", "cores", None), P("tm", "space", "cores", None)),
        check_vma=False,
    )
```

```python
import functools
import jax
import numpy as np
import jax.numpy as jnp
from jax import lax
from jax.experimental import pallas as pl
from jax.experimental.pallas import tpu as pltpu
from jax.sharding import PartitionSpec as P


F32 = jnp.float32
BF16 = jnp.bfloat16
SUB = 8


VM = pl.BlockSpec(memory_space=pltpu.VMEM)
SM = pl.BlockSpec(memory_space=pltpu.SMEM)


def cut(x):
    hi = x.astype(BF16)
    return hi, (x - hi.astype(F32)).astype(BF16)


def mm(a, b):
    return jnp.dot(a, b, preferred_element_type=F32)


def mmt(a, b):
    return lax.dot_general(a, b, (((1,), (1,)), ((), ())), preferred_element_type=F32)


def const_times(wh, wl, x):
    n = x.shape[1]
    xh, xl = cut(x)
    if n > 128:
        return mm(wh, xh) + mm(wh, xl) + mm(wl, xh)
    both = mm(wh, jnp.concatenate([xh, xl], axis=1))
    return both[:, :n] + both[:, n:] + mm(wl, xh)


def np_cosine(order, mode, node):
    mode = np.asarray(mode, np.float32)
    node = np.asarray(node, np.float32)
    scaling = np.where(mode == 0, np.sqrt(np.float32(1.0 / order)), np.sqrt(np.float32(2.0 / order)))
    angle = np.float32(np.pi) * mode * (node + np.float32(0.5)) / np.float32(order)
    return (scaling * np.cos(angle.astype(np.float64))).astype(np.float32)


def np_halves(w):
    hi = w.astype(BF16)
    return hi, (w - hi.astype(np.float32)).astype(BF16)


def np_modes(n):
    return np.concatenate([np.arange(0, n, 2), np.arange(1, n, 2)])


def np_bar(n, back):
    a = np_modes(n)
    base = np_cosine(n, a[:, None], np.arange(n)[None])
    edge = np_cosine(n, a, np.zeros(n))[:, None]
    w = (base * edge).T if back else base / edge
    return np_halves(np.kron(w, np.eye(SUB, dtype=np.float32)))


def np_second(hy):
    ny = 2 * hy
    pack = 256 // ny
    tiles = hy // SUB
    line = np.arange(hy)
    modes = tiles * (line % SUB) + line // SUB
    eye = np.eye(pack, dtype=np.float32)
    there, back = [], []
    for yc in range(2):
        sides = (yc, 1 - yc)
        blocks = [[np_cosine(ny, (m * hy + modes)[:, None], (n * hy + line)[None]) for n in sides] for m in sides]
        there.append(np.block([[np.kron(eye, b) for b in row] for row in blocks]))
        back.append(np.concatenate([np.kron(eye, row[0].T) for row in blocks], axis=1))
    return [np.stack([np_halves(w) for w in ws]) for ws in map(np.stack, (there, back))]


def tree(parts):
    while len(parts) > 1:
        parts = [a + b for a, b in zip(parts[::2], parts[1::2])] + (
            [parts[-1]] if len(parts) % 2 else []
        )
    return parts[0]


def split_kernel(nt, q_ref, yc_ref, me_ref, amp_ref, diff_ref, par_ref, *refs):
    ins, outs, diff_out, par_out = refs[:nt], refs[nt : 2 * nt], refs[2 * nt], refs[2 * nt + 1]
    steps = amp_ref.shape[0]
    rows = outs[0].shape[0] - steps
    cq = outs[0].shape[1]
    for d in range(nt):
        outs[d][0:rows, :] = ins[d][...].reshape(rows, cq)
        for k in range(steps):
            outs[d][rows + k : rows + k + 1, :] = jnp.full((1, cq), amp_ref[k], F32)
    diff_out[...] = jnp.full(diff_out.shape, diff_ref[0], F32)
    par_out[...] = jnp.full(par_out.shape, par_ref[0], F32)


def forward_block(x, c_ref, kxh_ref, kxl_ref):
    nx, _, nz = x.shape
    cq = c_ref.shape[1]
    xh, xl = cut(x.reshape(nx * SUB, nz))
    both = mmt(xh, c_ref[...].reshape(2 * cq, nz))
    z = both[:, :cq] + both[:, cq:] + mmt(xl, c_ref[0])
    return const_times(kxh_ref[...], kxl_ref[...], z).reshape(nx, SUB, cq)


def forward_kernel(with_sy, q_ref, sy_ref, x_ref, c_ref, kxh_ref, kxl_ref, out_ref):
    nx, hy, _ = x_ref.shape
    cq = out_ref.shape[2]
    tiles = hy // SUB
    if with_sy:
        for r in range(hy):
            b = tiles * (r % SUB) + r // SUB
            out_ref[nx, r : r + 1, :] = jnp.full((1, cq), sy_ref[b], F32)
    for t in range(tiles):
        at = slice(t * SUB, (t + 1) * SUB)
        out_ref[0:nx, at, :] = forward_block(x_ref[:, at, :], c_ref.at[q_ref[0]], kxh_ref, kxl_ref)


def factor_into(f_ref, sx_ref, diff_ref, sy, sz):
    for i, a in enumerate(np_modes(f_ref.shape[0])):
        rate = (sx_ref[int(a)] + sy) + sz
        f_ref[i] = 1.0 / (1.0 + diff_ref[0:1, :] * rate)


def order_kernel(nt, space, q_ref, me_ref, sx_ref, sy_ref, open_ref, owner_ref, diff_ref, sz_ref, n1_ref, *refs):
    ins, (u_ref, amp_ref, tab_ref, fo_ref, ft_ref), outs = refs[:nt], refs[nt : nt + 5], refs[nt + 5 :]
    steps = amp_ref.shape[1]
    rows = ins[0].shape[0] - steps
    nx, hy, cq = fo_ref.shape
    tiles = hy // SUB
    for d in range(nt):
        w = jnp.bitwise_xor(q_ref[0], d)
        u_ref[w] = ins[d][0:rows, :].reshape(u_ref.shape[1:])
        amp_ref[w] = ins[d][rows:, :]
    for i, out in enumerate(outs):
        out[...] = u_ref[jnp.where(i < q_ref[0], i, i + 1)]
    for face in range(2):
        i = lax.rem(me_ref[0] + space - 1, space) if face == 0 else me_ref[0]
        for g in range(hy // tiles):
            closed = False
            for j in range(tiles):
                b = tiles * g + j
                r = face * hy + j * SUB + g
                tab_ref[r : r + 1, :] = jnp.full((1, cq), owner_ref[i, b], jnp.int32)
                closed = jnp.logical_or(closed, open_ref[i, b] == 0)
                if j < tiles - 1:
                    r = 2 * hy + (face * (tiles - 1) + j) * SUB + g
                    tab_ref[r : r + 1, :] = jnp.full((1, cq), closed.astype(jnp.int32), jnp.int32)
    sz = sz_ref[pl.ds(q_ref[0], 1), :]
    for r in range(hy):
        b = tiles * (r % SUB) + r // SUB
        fo_ref[0, r : r + 1, :] = jnp.full((1, cq), sy_ref[b], F32)
    factor_into(fo_ref, sx_ref, diff_ref, fo_ref[0], sz)
    factor_into(ft_ref, sx_ref, diff_ref, n1_ref[nx], sz)


def closed_rows(tab_ref, face, tiles, hy):
    base = 2 * hy + face * (tiles - 1) * SUB
    return [tab_ref[base + i * SUB : base + (i + 1) * SUB, :] > 0 for i in range(tiles - 1)]


def own_kernel(dims, q_ref, yc_ref, *refs):
    nt, steps, nx, hy, cq = dims
    params, (n0, s0, n1, s1, u_s, amp_s, tab_ref, f_s, ky_ref) = refs[:3], refs[3:12]
    hands, (clos_ref, mo_ref, so_ref) = refs[12 : 12 + nt], refs[12 + nt : 15 + nt]
    m_s, s_s, vd = refs[15 + nt :]
    tiles = hy // SUB
    pack = ky_ref.shape[2] // (2 * hy)
    half = pack * hy
    yc = yc_ref[0]

    def ytrans(ag, _):
        at = pl.ds(ag * pack, pack)
        cols = [
            jnp.concatenate([here[at].reshape(half, cq), there[at].reshape(half, cq)], axis=0)
            for here, there in ((n0, n1), (s0, s1))
        ]
        res = const_times(ky_ref[yc, 0], ky_ref[yc, 1], jnp.concatenate(cols, axis=1))
        for f, own, oth in ((0, m_s, mo_ref), (1, s_s, so_ref)):
            part = res[:, f * cq : (f + 1) * cq]
            own[at] = part[:half].reshape(pack, hy, cq)
            oth[at] = part[half:].reshape(pack, hy, cq)
        return 0

    lax.fori_loop(0, nx // pack, ytrans, 0)
    ha = nx // 2
    chunk = min(SUB, ha)
    order = np_modes(nx)
    edge = np_cosine(nx, order, np.zeros(nx)).astype(np.float64)
    slope = np_cosine(nx, order, np.ones(nx)).astype(np.float64) - edge
    for j in range(tiles):
        rows = slice(j * SUB, (j + 1) * SUB)
        for par in range(2):
            for first in range(0, ha, chunk):
                modes = [par * ha + first + i for i in range(chunk)]
                s = [s_s[a, rows, :] for a in modes]
                f = [f_s[a, rows, :] for a in modes]
                wv = [float(np.float32(edge[a] * edge[a])) for a in modes]
                wd = [float(np.float32(edge[a] * slope[a])) for a in modes]

                def window(w, cur, j=j, par=par, first=first, rows=rows, modes=modes, s=s, f=f, wv=wv, wd=wd):
                    cur = list(cur)
                    for k in range(steps):
                        r0 = u_s[w, 0, k, pl.ds(j, SUB, stride=tiles), :]
                        r1 = u_s[w, 1, k, pl.ds(j, SUB, stride=tiles), :]
                        u = r0 + r1 if par == 0 else r0 - r1
                        amp = amp_s[w, k : k + 1, :]
                        cur = [(x + (amp * y + u)) * z for x, y, z in zip(cur, s, f)]
                        m = w * steps + k
                        v = tree([x * y for x, y in zip(cur, wv)])
                        d = tree([x * y for x, y in zip(cur, wd)])
                        if first:
                            v = v + vd[par, 0, m, j]
                            d = d + vd[par, 1, m, j]
                        vd[par, 0, m, j] = v
                        vd[par, 1, m, j] = d
                    for a, x in zip(modes, cur):
                        clos_ref[w, a, rows, :] = x
                    return tuple(cur)

                lax.fori_loop(0, nt, window, tuple(m_s[a, rows, :] for a in modes))

    params = [ref[...] for ref in params]
    for slot in range(nt):
        w = jnp.bitwise_xor(q_ref[0], slot)

        def combine(k, _, slot=slot, w=w):
            m = w * steps + k
            left, right = [], []
            for j in range(tiles):
                ve, vo = vd[0, 0, m, j], vd[1, 0, m, j]
                de, do = vd[0, 1, m, j], vd[1, 1, m, j]
                p = [
                    jnp.where(
                        tab_ref[i * hy + j * SUB : i * hy + (j + 1) * SUB, :] == 0, params[i], params[i + 1]
                    )
                    for i in range(2)
                ]
                left.append((de + do) + p[0] * (ve + vo))
                right.append(p[1] * (ve - vo) + (de - do))
            for face, line in enumerate((left, right)):
                for i, le in enumerate(closed_rows(tab_ref, face, tiles, hy)):
                    hands[slot][face, k, i * SUB : (i + 1) * SUB, :] = jnp.where(le, line[i + 1], line[i])
            return 0

        lax.fori_loop(0, steps, combine, 0)


def window_of(nt, q, slot):
    if nt == 4 and slot >= 2:
        return jnp.bitwise_xor(q, jnp.where(q == 1, 5 - slot, slot))
    return jnp.bitwise_xor(q, slot)


def late_slots(nt):
    return [0, 1, 3] if nt == 4 else list(range(nt))


def other_kernel(
    dims, late, q_ref, yc_ref, m_ref, s_ref, f_ref, amp_ref, clos_ref, ki_ref, kxh_ref, kxl_ref, own_ref, *refs
):
    nt, steps, nx, hy, cq = dims
    slots = late_slots(nt) if late else range(nt)
    chunks, refs = (refs[:1], refs[1 + len(slots) :]) if late else (refs[: nt - 2], refs[nt - 2 :])
    outs = refs[: len(slots)]
    st_ref, cl, t_s, x_s, u_s = refs[len(slots) :]
    q = q_ref[0]
    edge = jnp.where(q == nt - 1, nt - 2, nt - 1)
    lo, hi, base = (edge, nt, nt - 2) if late else (0, edge, 0)

    def put(when, w, ref):
        @pl.when(when)
        def _():
            u_s[w - base] = ref[...]

    if late:
        put(q == nt - 1, nt - 1, own_ref)
        put(q < nt - 1, nt - 1, chunks[0])
        put(q == nt - 1, nt - 2, chunks[0])
    else:
        for w in range(nt - 1):
            put(q == w, w, own_ref)
            if w < nt - 2:
                put(q > w, w, chunks[w])
            if w > 0:
                put(q < w, w, chunks[w - 1])
    tiles = hy // SUB
    ha = nx // 2
    for j in range(tiles):
        rows = slice(j * SUB, (j + 1) * SUB)
        for par in range(2):
            modes = [par * ha + i for i in range(ha)]
            s = [s_ref[a, rows, :] for a in modes]
            f = [f_ref[a, rows, :] for a in modes]

            def window(w, cur, j=j, par=par, rows=rows, modes=modes, s=s, f=f):
                cur = list(cur)
                for k in range(steps):
                    r0 = u_s[w - base, 0, k, pl.ds(j, SUB, stride=tiles), :]
                    r1 = u_s[w - base, 1, k, pl.ds(j, SUB, stride=tiles), :]
                    u = r0 + r1 if par == 0 else r0 - r1
                    amp = amp_ref[w, k : k + 1, :]
                    cur = [(x + (amp * y + u)) * z for x, y, z in zip(cur, s, f)]
                for a, x in zip(modes, cur):
                    cl[w - base, a, rows, :] = x
                return tuple(cur)

            end = lax.fori_loop(lo, hi, window, tuple(m_ref[a, rows, :] for a in modes))
            for a, x in zip(modes, end):
                st_ref[a, rows, :] = x
    pack = ki_ref.shape[2] // hy
    half = pack * hy
    yc = yc_ref[0]

    def back(w, _):
        def yback(ag, _):
            at = pl.ds(ag * pack, pack)
            col = [clos_ref[w, at].reshape(half, cq), cl[w - base, at].reshape(half, cq)]
            res = const_times(ki_ref[yc, 0], ki_ref[yc, 1], jnp.concatenate(col, axis=0))
            t_s[at] = res.reshape(pack, hy, cq)
            return 0

        lax.fori_loop(0, nx // pack, yback, 0, unroll=2)
        for yb in range(tiles):
            at = slice(yb * SUB, (yb + 1) * SUB)
            res = const_times(kxh_ref[...], kxl_ref[...], t_s[:, at, :].reshape(nx * SUB, cq))
            x_s[:, at, :] = res.reshape(nx, SUB, cq)
        for slot, out in zip(slots, outs):

            @pl.when(window_of(nt, q, slot) == w)
            def _(out=out):
                out[...] = x_s[...]

        return 0

    lax.fori_loop(lo, hi, back, 0)


def relay_kernel(nt, q_ref, early_ref, late_ref, out_ref):
    @pl.when(q_ref[0] == nt - 1)
    def _():
        out_ref[...] = early_ref[...]

    @pl.when(q_ref[0] != nt - 1)
    def _():
        out_ref[...] = late_ref[...]


def final_kernel(nt, q_ref, *refs):
    ws, ins, (out_ref, wh, wl) = refs[:nt], refs[nt:-3], refs[-3:]
    xb, hy, nz = out_ref.shape[1:]
    cq = nz // nt

    @pl.when(pl.program_id(0) == 0)
    def _():
        for d in range(nt):
            wh[d * cq : (d + 1) * cq, :] = ws[d][0]
            wl[d * cq : (d + 1) * cq, :] = ws[d][1]

    parts = [x[...].reshape(xb * hy, cq) for x in ins]
    if nt == 4:
        relayed = parts.pop()
        parts[2] = jnp.where(q_ref[0] == 3, relayed, parts[2])
        parts[3] = jnp.where(q_ref[0] == 2, relayed, parts[3])
    xh, xl = cut(jnp.concatenate(parts, axis=1))
    res = mm(xh, wh[...]) + mm(xh, wl[...]) + mm(xl, wh[...])
    out_ref[0] = res.reshape(xb, hy, nz)


def merge_kernel(nt, q_ref, *refs):
    ins, outs = refs[:nt], refs[nt:]
    for d in range(nt):
        for face in range(2):
            outs[face][jnp.bitwise_xor(q_ref[0], d)] = ins[d][face]


def spread_kernel(nt, steps, tab_ref, left_ref, right_ref, out_ref, line):
    hy = out_ref.shape[3]
    cq = out_ref.shape[4] // nt
    tiles = hy // SUB
    zero = jnp.zeros((SUB, cq), F32)
    for face, ref in enumerate((left_ref, right_ref)):
        le = closed_rows(tab_ref, face, tiles, hy)
        for c in range(nt):

            def step(k, _, face=face, c=c, ref=ref, le=le):
                r = [ref[c, k, i * SUB : (i + 1) * SUB, :] for i in range(tiles - 1)]
                for j in range(tiles):
                    if j == 0:
                        v = jnp.where(le[0], zero, r[0])
                    elif j < tiles - 1:
                        v = jnp.where(le[j], jnp.where(le[j - 1], r[j - 1], zero), r[j])
                    else:
                        v = jnp.where(le[j - 1], r[j - 1], zero)
                    line[face, k, pl.ds(j, SUB, stride=tiles), :] = v
                out_ref[0, face, k, :, c * cq : (c + 1) * cq] = line[face, k]
                return 0

            lax.fori_loop(0, steps, step, 0)


def sds(*shape):
    return jax.ShapeDtypeStruct(shape, F32)


def cost(flops, nbytes):
    return pl.CostEstimate(flops=int(flops), bytes_accessed=int(nbytes), transcendentals=0)


def grant(mib):
    return pltpu.CompilerParams(vmem_limit_bytes=mib << 20)


def local(
    initial_state,
    heat_source,
    source_amplitude,
    diffusivity,
    robin_param,
    spectrum_x,
    spectrum_y,
    spectrum_z,
    robin_in,
    open_flag,
    owner_side,
):
    nx, hy, nz = initial_state.shape
    nt = lax.axis_size("tm")
    ncores = lax.axis_size("cores")
    assert ncores == 2 and nt & (nt - 1) == 0 and nt >= 2
    cq = nz // nt
    steps = source_amplitude.shape[0]
    tiles = hy // SUB
    assert tiles == 4 and nx % 4 == 0
    q = lax.axis_index("tm")
    yc = lax.axis_index("cores")
    space = lax.axis_size("space")
    me = lax.axis_index("space")
    qv, ycv, mev = (jnp.reshape(i, (1,)).astype(jnp.int32) for i in (q, yc, me))
    dims = (nt, steps, nx, hy, cq)

    def xor_permute(x, d):
        return lax.ppermute(x, "tm", [(i, i ^ d) for i in range(nt)])

    def swap(x):
        return lax.ppermute(x, "cores", [(0, 1), (1, 0)])

    def along(x, by):
        return lax.ppermute(x, "space", [(i, (i + by) % space) for i in range(space)])

    base = np.stack(np_halves(np_cosine(nz, np.arange(nz)[:, None], np.arange(nz)[None])))
    base = jnp.asarray(base.reshape(2, nt, cq, nz).swapaxes(0, 1))
    kxh, kxl = (jnp.asarray(w) for w in np_bar(nx, False))
    kxih, kxil = (jnp.asarray(w) for w in np_bar(nx, True))
    ky, ki = (jnp.asarray(w) for w in np_second(hy))

    rows = 2 * steps * hy
    block = (None, 2, steps, hy, cq)
    cutting = pl.pallas_call(
        functools.partial(split_kernel, nt),
        out_shape=[sds(rows + steps, cq)] * nt + [sds(SUB, cq)] * 2,
        grid_spec=pltpu.PrefetchScalarGridSpec(
            num_scalar_prefetch=3,
            grid=(1,),
            in_specs=[SM] * 3
            + [
                pl.BlockSpec(block, lambda i, q, y, z, d=d: (0, 0, 0, 0, jnp.bitwise_xor(q[0], d)))
                for d in range(nt)
            ],
            out_specs=[pl.BlockSpec((rows + steps, cq), lambda i, q, y, z: (0, 0))] * nt
            + [pl.BlockSpec((SUB, cq), lambda i, q, y, z: (0, 0))] * 2,
        ),
        compiler_params=grant(18),
        cost_estimate=cost(0, 8 * nt * rows * cq),
        name="split",
    )
    *dealt, diff_rows, robin_param = cutting(
        qv, ycv, mev, source_amplitude, diffusivity, robin_param, *([robin_in] * nt)
    )
    piece = swap(dealt[0])

    def forward(values, planes):
        return pl.pallas_call(
            functools.partial(forward_kernel, planes > 0),
            out_shape=sds(nx + planes, hy, cq),
            in_specs=[SM] * 2 + [VM] * 4,
            out_specs=VM,
            compiler_params=grant(18),
            cost_estimate=cost(1e9, 3e6),
        )(qv, spectrum_y, values, base, kxh, kxl)

    n0 = forward(initial_state, 1)
    n1 = swap(n0)
    for d in range(1, nt):
        dealt[d] = xor_permute(dealt[d], d)
    s0 = forward(heat_source, 0)
    s1 = swap(s0)
    right_param = along(robin_param, -1)
    left_param = along(robin_param, 1)

    table = jax.ShapeDtypeStruct((2 * hy + 2 * (tiles - 1) * SUB, cq), jnp.int32)
    u_own, amps, tab, f_own, f_there, *chunks = pl.pallas_call(
        functools.partial(order_kernel, nt, space),
        out_shape=[sds(nt, 2, steps, hy, cq), sds(nt, steps, cq), table]
        + [sds(nx, hy, cq)] * 2
        + [sds(2, steps, hy, cq)] * (nt - 1),
        in_specs=[SM] * 6 + [VM] * (3 + nt),
        out_specs=[VM] * (4 + nt),
        compiler_params=grant(18),
        cost_estimate=cost(0, 3e6),
        name="order",
    )(
        qv, mev, spectrum_x, spectrum_y, open_flag, owner_side, diff_rows,
        spectrum_z.reshape(nt, cq), n1, *dealt,
    )
    for i in range(nt - 1):
        chunks[i] = swap(chunks[i])

    short = sds(2, steps, (tiles - 1) * SUB, cq)
    *hands, clos, m_there, s_there = pl.pallas_call(
        functools.partial(own_kernel, dims),
        out_shape=[short] * nt + [sds(nt, nx, hy, cq), sds(nx, hy, cq), sds(nx, hy, cq)],
        in_specs=[SM] * 2 + [VM] * 12,
        out_specs=[VM] * (nt + 3),
        scratch_shapes=[pltpu.VMEM((nx, hy, cq), F32)] * 2
        + [pltpu.VMEM((2, 2, nt * steps, tiles, SUB, cq), F32)],
        compiler_params=grant(18),
        cost_estimate=cost(4e9, 8e6),
        name="own",
    )(qv, ycv, left_param, robin_param, right_param, n0, s0, n1, s1, u_own, amps, tab, f_own, ky)
    for d in range(1, nt):
        hands[d] = xor_permute(hands[d], d)

    state, ends = m_there, [None] * nt
    piece = piece[:rows].reshape(2, steps, hy, cq)
    for late, got in ((False, chunks[:-1]), (True, chunks[-1:])):
        span = 2 if late else nt - 1
        slots = late_slots(nt) if late else list(range(nt))
        prior = [ends[d] for d in slots] if late else []
        *outs, state = pl.pallas_call(
            functools.partial(other_kernel, dims, late),
            out_shape=[sds(nx, hy, cq)] * (len(slots) + 1),
            in_specs=[SM] * 2 + [VM] * (9 + len(got) + len(prior)),
            out_specs=[VM] * (len(slots) + 1),
            scratch_shapes=[
                pltpu.VMEM((span, nx, hy, cq), F32),
                pltpu.VMEM((nx, hy, cq), F32),
                pltpu.VMEM((nx, hy, cq), F32),
                pltpu.VMEM((span, 2, steps, hy, cq), F32),
            ],
            input_output_aliases={11 + len(got) + d: d for d in range(len(prior))},
            compiler_params=grant(18),
            cost_estimate=cost(4e9, 4e6),
            name="other1" if late else "other0",
        )(qv, ycv, state, s_there, f_there, amps, clos, ki, kxih, kxil, piece, *got, *prior)
        for d, out in zip(slots, outs):
            ends[d] = out
        for d in range(1, nt):
            if late and d in slots or not late and d not in late_slots(nt):
                ends[d] = xor_permute(ends[d], d)
    if nt == 4:
        passing = pl.pallas_call(
            functools.partial(relay_kernel, nt),
            out_shape=sds(nx, hy, cq),
            in_specs=[SM] + [VM] * 2,
            out_specs=VM,
            compiler_params=grant(18),
            cost_estimate=cost(0, 1e6),
            name="relay",
        )(qv, ends[2], ends[3])
        ends.append(xor_permute(passing, 1))
    left, right = pl.pallas_call(
        functools.partial(merge_kernel, nt),
        out_shape=[sds(nt, steps, (tiles - 1) * SUB, cq)] * 2,
        in_specs=[SM] + [VM] * nt,
        out_specs=[VM] * 2,
        compiler_params=grant(18),
        cost_estimate=cost(0, 2e6),
        name="merge",
    )(qv, *hands)
    from_right = along(left, -1)
    from_left = along(right, 1)
    xb = SUB
    window_end = pl.pallas_call(
        functools.partial(final_kernel, nt),
        out_shape=sds(1, nx, hy, nz),
        grid_spec=pltpu.PrefetchScalarGridSpec(
            num_scalar_prefetch=1,
            grid=(nx // xb,),
            in_specs=[
                pl.BlockSpec((None, 2, cq, nz), lambda i, q, d=d: (jnp.bitwise_xor(q[0], d), 0, 0, 0))
                for d in range(nt)
            ]
            + [pl.BlockSpec((xb, hy, cq), lambda i, q: (i, 0, 0))] * len(ends),
            out_specs=pl.BlockSpec((1, xb, hy, nz), lambda i, q: (0, i, 0, 0)),
            scratch_shapes=[pltpu.VMEM((nz, nz), BF16)] * 2,
        ),
        compiler_params=grant(18),
        cost_estimate=cost(2e9, 6e6),
        name="final",
    )(qv, *([base] * nt), *ends)

    robin_out = pl.pallas_call(
        functools.partial(spread_kernel, nt, steps),
        out_shape=sds(1, 2, steps, hy, nz),
        in_specs=[VM] * 3,
        out_specs=VM,
        scratch_shapes=[pltpu.VMEM((2, steps, hy, cq), F32)],
        compiler_params=grant(18),
        cost_estimate=cost(0, 2e6),
        name="spread",
    )(tab, from_left, from_right)
    return robin_out, window_end


def solution(mesh):
    placed = (
        P("space", "cores", None),
        P("space", "cores", None),
        P("tm"),
        P("space"),
        P("space"),
        P(),
        P("cores"),
        P(),
        P("space", None, "tm", "cores", None),
        P(None, "cores"),
        P(None, "cores"),
    )

    return jax.shard_map(
        local,
        mesh=mesh,
        in_specs=placed,
        out_specs=(P("space", None, "tm", "cores", None), P("tm", "space", "cores", None)),
        check_vma=False,
    )
```

```python
import functools
import jax
import numpy as np
import jax.numpy as jnp
from jax import lax
from jax.experimental import pallas as pl
from jax.experimental.pallas import tpu as pltpu
from jax.sharding import PartitionSpec as P


F32 = jnp.float32
BF16 = jnp.bfloat16
SUB = 8


VM = pl.BlockSpec(memory_space=pltpu.VMEM)
SM = pl.BlockSpec(memory_space=pltpu.SMEM)


def cut(x):
    hi = x.astype(BF16)
    return hi, (x - hi.astype(F32)).astype(BF16)


def mm(a, b):
    return jnp.dot(a, b, preferred_element_type=F32)


def mmt(a, b):
    return lax.dot_general(a, b, (((1,), (1,)), ((), ())), preferred_element_type=F32)


def const_times(wh, wl, x):
    n = x.shape[1]
    xh, xl = cut(x)
    if n > 128:
        return mm(wh, xh) + mm(wh, xl) + mm(wl, xh)
    both = mm(wh, jnp.concatenate([xh, xl], axis=1))
    return both[:, :n] + both[:, n:] + mm(wl, xh)


def np_cosine(order, mode, node):
    mode = np.asarray(mode, np.float32)
    node = np.asarray(node, np.float32)
    scaling = np.where(mode == 0, np.sqrt(np.float32(1.0 / order)), np.sqrt(np.float32(2.0 / order)))
    angle = np.float32(np.pi) * mode * (node + np.float32(0.5)) / np.float32(order)
    return (scaling * np.cos(angle.astype(np.float64))).astype(np.float32)


def np_halves(w):
    hi = w.astype(BF16)
    return hi, (w - hi.astype(np.float32)).astype(BF16)


def np_modes(n):
    return np.concatenate([np.arange(0, n, 2), np.arange(1, n, 2)])


def np_bar(n, back):
    a = np_modes(n)
    base = np_cosine(n, a[:, None], np.arange(n)[None])
    edge = np_cosine(n, a, np.zeros(n))[:, None]
    w = (base * edge).T if back else base / edge
    return np_halves(np.kron(w, np.eye(SUB, dtype=np.float32)))


def np_second(hy):
    ny = 2 * hy
    pack = 256 // ny
    tiles = hy // SUB
    line = np.arange(hy)
    modes = tiles * (line % SUB) + line // SUB
    eye = np.eye(pack, dtype=np.float32)
    there, back = [], []
    for yc in range(2):
        sides = (yc, 1 - yc)
        blocks = [[np_cosine(ny, (m * hy + modes)[:, None], (n * hy + line)[None]) for n in sides] for m in sides]
        there.append(np.block([[np.kron(eye, b) for b in row] for row in blocks]))
        back.append(np.concatenate([np.kron(eye, row[0].T) for row in blocks], axis=1))
    return [np.stack([np_halves(w) for w in ws]) for ws in map(np.stack, (there, back))]


def tree(parts):
    while len(parts) > 1:
        parts = [a + b for a, b in zip(parts[::2], parts[1::2])] + (
            [parts[-1]] if len(parts) % 2 else []
        )
    return parts[0]


def split_kernel(nt, q_ref, yc_ref, me_ref, amp_ref, diff_ref, par_ref, *refs):
    ins, outs, diff_out, par_out = refs[:nt], refs[nt : 2 * nt], refs[2 * nt], refs[2 * nt + 1]
    steps = amp_ref.shape[0]
    rows = outs[0].shape[0] - steps
    cq = outs[0].shape[1]
    for d in range(nt):
        outs[d][0:rows, :] = ins[d][...].reshape(rows, cq)
        for k in range(steps):
            outs[d][rows + k : rows + k + 1, :] = jnp.full((1, cq), amp_ref[k], F32)
    diff_out[...] = jnp.full(diff_out.shape, diff_ref[0], F32)
    par_out[...] = jnp.full(par_out.shape, par_ref[0], F32)


def forward_block(x, c_ref, kxh_ref, kxl_ref):
    nx, _, nz = x.shape
    cq = c_ref.shape[1]
    xh, xl = cut(x.reshape(nx * SUB, nz))
    both = mmt(xh, c_ref[...].reshape(2 * cq, nz))
    z = both[:, :cq] + both[:, cq:] + mmt(xl, c_ref[0])
    return const_times(kxh_ref[...], kxl_ref[...], z).reshape(nx, SUB, cq)


def forward_kernel(with_sy, q_ref, sy_ref, x_ref, c_ref, kxh_ref, kxl_ref, out_ref):
    nx, hy, _ = x_ref.shape
    cq = out_ref.shape[2]
    tiles = hy // SUB
    if with_sy:
        for r in range(hy):
            b = tiles * (r % SUB) + r // SUB
            out_ref[nx, r : r + 1, :] = jnp.full((1, cq), sy_ref[b], F32)
    for t in range(tiles):
        at = slice(t * SUB, (t + 1) * SUB)
        out_ref[0:nx, at, :] = forward_block(x_ref[:, at, :], c_ref.at[q_ref[0]], kxh_ref, kxl_ref)


def factor_into(f_ref, sx_ref, diff_ref, sy, sz):
    for i, a in enumerate(np_modes(f_ref.shape[0])):
        rate = (sx_ref[int(a)] + sy) + sz
        f_ref[i] = 1.0 / (1.0 + diff_ref[0:1, :] * rate)


def order_kernel(nt, space, q_ref, me_ref, sx_ref, sy_ref, open_ref, owner_ref, diff_ref, sz_ref, there_ref, *refs):
    ins, (u_ref, amp_ref, tab_ref, fo_ref, ft_ref), outs = refs[:nt], refs[nt : nt + 5], refs[nt + 5 :]
    steps = amp_ref.shape[1]
    rows = ins[0].shape[0] - steps
    nx, hy, cq = fo_ref.shape
    tiles = hy // SUB
    for d in range(nt):
        w = jnp.bitwise_xor(q_ref[0], d)
        u_ref[w] = ins[d][0:rows, :].reshape(u_ref.shape[1:])
        amp_ref[w] = ins[d][rows:, :]
    for i, out in enumerate(outs):
        out[...] = u_ref[jnp.where(i < q_ref[0], i, i + 1)]
    for face in range(2):
        i = lax.rem(me_ref[0] + space - 1, space) if face == 0 else me_ref[0]
        for g in range(hy // tiles):
            closed = False
            for j in range(tiles):
                b = tiles * g + j
                r = face * hy + j * SUB + g
                tab_ref[r : r + 1, :] = jnp.full((1, cq), owner_ref[i, b], jnp.int32)
                closed = jnp.logical_or(closed, open_ref[i, b] == 0)
                if j < tiles - 1:
                    r = 2 * hy + (face * (tiles - 1) + j) * SUB + g
                    tab_ref[r : r + 1, :] = jnp.full((1, cq), closed.astype(jnp.int32), jnp.int32)
    sz = sz_ref[pl.ds(q_ref[0], 1), :]
    for r in range(hy):
        b = tiles * (r % SUB) + r // SUB
        fo_ref[0, r : r + 1, :] = jnp.full((1, cq), sy_ref[b], F32)
    factor_into(fo_ref, sx_ref, diff_ref, fo_ref[0], sz)
    factor_into(ft_ref, sx_ref, diff_ref, there_ref[nx], sz)


def closed_rows(tab_ref, face, tiles, hy):
    base = 2 * hy + face * (tiles - 1) * SUB
    return [tab_ref[base + i * SUB : base + (i + 1) * SUB, :] > 0 for i in range(tiles - 1)]


def transform_second(ky_ref, yc, here, there, own, oth):
    nx, hy, cq = own.shape
    pack = ky_ref.shape[2] // (2 * hy)
    half = pack * hy

    def step(ag, _):
        ats = [pl.ds((2 * ag + i) * pack, pack) for i in range(2)]
        cols = [
            jnp.concatenate([here[at].reshape(half, cq), there[at].reshape(half, cq)], axis=0) for at in ats
        ]
        res = const_times(ky_ref[yc, 0], ky_ref[yc, 1], jnp.concatenate(cols, axis=1))
        for i, at in enumerate(ats):
            part = res[:, i * cq : (i + 1) * cq]
            own[at] = part[:half].reshape(pack, hy, cq)
            oth[at] = part[half:].reshape(pack, hy, cq)
        return 0

    lax.fori_loop(0, nx // (2 * pack), step, 0)


def np_edges(nx):
    order = np_modes(nx)
    edge = np_cosine(nx, order, np.zeros(nx)).astype(np.float64)
    return edge, np_cosine(nx, order, np.ones(nx)).astype(np.float64) - edge


def driven_kernel(dims, yc_ref, s0, s1, u_s, amp_s, f_s, ky_ref, vd, clos_ref, so_ref, s_s):
    nt, steps, nx, hy, cq = dims
    tiles = hy // SUB
    transform_second(ky_ref, yc_ref[0], s0, s1, s_s, so_ref)
    ha = nx // 2
    chunk = min(SUB, ha)
    edge, slope = np_edges(nx)
    for j in range(tiles):
        rows = slice(j * SUB, (j + 1) * SUB)
        for par in range(2):
            for first in range(0, ha, chunk):
                modes = [par * ha + first + i for i in range(chunk)]
                s = [s_s[a, rows, :] for a in modes]
                f = [f_s[a, rows, :] for a in modes]
                wv = [float(np.float32(edge[a] * edge[a])) for a in modes]
                wd = [float(np.float32(edge[a] * slope[a])) for a in modes]

                def window(w, cur, j=j, par=par, first=first, rows=rows, modes=modes, s=s, f=f, wv=wv, wd=wd):
                    cur = list(cur)
                    for k in range(steps):
                        r0 = u_s[w, 0, k, pl.ds(j, SUB, stride=tiles), :]
                        r1 = u_s[w, 1, k, pl.ds(j, SUB, stride=tiles), :]
                        u = r0 + r1 if par == 0 else r0 - r1
                        amp = amp_s[w, k : k + 1, :]
                        cur = [(x + (amp * y + u)) * z for x, y, z in zip(cur, s, f)]
                        m = w * steps + k
                        v = tree([x * y for x, y in zip(cur, wv)])
                        d = tree([x * y for x, y in zip(cur, wd)])
                        if first:
                            v = v + vd[par, 0, m, j]
                            d = d + vd[par, 1, m, j]
                        vd[par, 0, m, j] = v
                        vd[par, 1, m, j] = d
                    for a, x in zip(modes, cur):
                        clos_ref[w, a, rows, :] = x
                    return tuple(cur)

                lax.fori_loop(0, nt, window, (jnp.zeros((SUB, cq), F32),) * chunk)


def own_kernel(dims, q_ref, yc_ref, *refs):
    nt, steps, nx, hy, _ = dims
    params, (n0, n1, driven, clos_in, tab_ref, f_s, ky_ref) = refs[:3], refs[3:10]
    hands, (clos_ref, mo_ref) = refs[10 : 10 + nt], refs[10 + nt : 12 + nt]
    m_s, vd = refs[12 + nt :]
    tiles = hy // SUB
    transform_second(ky_ref, yc_ref[0], n0, n1, m_s, mo_ref)
    ha = nx // 2
    edge, slope = np_edges(nx)
    for j in range(tiles):
        rows = slice(j * SUB, (j + 1) * SUB)
        for par in range(2):
            modes = [par * ha + i for i in range(ha)]
            f = [f_s[a, rows, :] for a in modes]
            ratio = [float(np.float32(slope[a] / edge[a])) for a in modes]

            def window(w, cur, j=j, par=par, rows=rows, modes=modes, f=f, ratio=ratio):
                cur = list(cur)
                for k in range(steps):
                    cur = [x * z for x, z in zip(cur, f)]
                    m = w * steps + k
                    vd[par, 0, m, j] = tree(cur)
                    vd[par, 1, m, j] = tree([x * y for x, y in zip(cur, ratio)])
                for a, x in zip(modes, cur):
                    clos_ref[w, a, rows, :] = clos_in[w, a, rows, :] + x * float(np.float32(edge[a] ** -2))
                return tuple(cur)

            start = tuple(m_s[a, rows, :] * float(np.float32(edge[a] ** 2)) for a in modes)
            lax.fori_loop(0, nt, window, start)

    params = [ref[...] for ref in params]
    for slot in range(nt):
        w = jnp.bitwise_xor(q_ref[0], slot)

        def combine(k, _, slot=slot, w=w):
            m = w * steps + k
            left, right = [], []
            for j in range(tiles):
                ve, vo, de, do = (
                    driven[par, kind, m, j] + vd[par, kind, m, j] for kind in range(2) for par in range(2)
                )
                p = [
                    jnp.where(
                        tab_ref[i * hy + j * SUB : i * hy + (j + 1) * SUB, :] == 0, params[i], params[i + 1]
                    )
                    for i in range(2)
                ]
                left.append((de + do) + p[0] * (ve + vo))
                right.append(p[1] * (ve - vo) + (de - do))
            for face, line in enumerate((left, right)):
                for i, le in enumerate(closed_rows(tab_ref, face, tiles, hy)):
                    hands[slot][face, k, i * SUB : (i + 1) * SUB, :] = jnp.where(le, line[i + 1], line[i])
            return 0

        lax.fori_loop(0, steps, combine, 0)


def window_of(nt, q, slot):
    if nt == 4 and slot >= 2:
        return jnp.bitwise_xor(q, jnp.where(q == 1, 5 - slot, slot))
    return jnp.bitwise_xor(q, slot)


def late_slots(nt):
    return [0, 1, 3] if nt == 4 else list(range(nt))


def other_kernel(
    dims, stage, q_ref, yc_ref, m_ref, s_ref, f_ref, amp_ref, clos_ref, ki_ref, kxh_ref, kxl_ref, own_ref, *refs
):
    nt, steps, nx, hy, cq = dims
    slots = late_slots(nt) if stage == 2 else range(nt)
    given = nt - 3 if stage == 0 else 1
    prior = 0 if stage == 0 else len(slots)
    chunks, refs = refs[:given], refs[given + prior :]
    outs = refs[: len(slots)]
    st_ref, cl, t_s, x_s, u_s = refs[len(slots) :]
    q = q_ref[0]
    edge = jnp.where(q < nt - 2, nt - 2, nt - 3)
    lo, hi = ((0, edge), (edge, edge + 1), (edge + 1, nt))[stage]

    def put(when, at, ref):
        @pl.when(when)
        def _():
            u_s[at] = ref[...]

    if stage == 0:
        for w in range(nt - 2):
            put(q == w, w, own_ref)
            if w < nt - 3:
                put(q > w, w, chunks[w])
            if w > 0:
                put(q < w, w, chunks[w - 1])
    elif stage == 1:
        u_s[0] = chunks[0][...]
    else:
        put(q != nt - 2, 0, chunks[0])
        put(q == nt - 2, 0, own_ref)
        put(q == nt - 2, 1, chunks[0])
        put(q == nt - 1, 1, own_ref)
    base = lo
    tiles = hy // SUB
    ha = nx // 2
    for j in range(tiles):
        rows = slice(j * SUB, (j + 1) * SUB)
        for par in range(2):
            modes = [par * ha + i for i in range(ha)]
            s = [s_ref[a, rows, :] for a in modes]
            f = [f_ref[a, rows, :] for a in modes]

            def window(w, cur, j=j, par=par, rows=rows, modes=modes, s=s, f=f):
                cur = list(cur)
                for k in range(steps):
                    r0 = u_s[w - base, 0, k, pl.ds(j, SUB, stride=tiles), :]
                    r1 = u_s[w - base, 1, k, pl.ds(j, SUB, stride=tiles), :]
                    u = r0 + r1 if par == 0 else r0 - r1
                    amp = amp_ref[w, k : k + 1, :]
                    cur = [(x + (amp * y + u)) * z for x, y, z in zip(cur, s, f)]
                for a, x in zip(modes, cur):
                    cl[w - base, a, rows, :] = x
                return tuple(cur)

            end = lax.fori_loop(lo, hi, window, tuple(m_ref[a, rows, :] for a in modes))
            for a, x in zip(modes, end):
                st_ref[a, rows, :] = x
    pack = ki_ref.shape[2] // hy
    half = pack * hy
    yc = yc_ref[0]

    def back(w, _):
        def yback(ag, _):
            at = pl.ds(ag * pack, pack)
            col = [clos_ref[w, at].reshape(half, cq), cl[w - base, at].reshape(half, cq)]
            res = const_times(ki_ref[yc, 0], ki_ref[yc, 1], jnp.concatenate(col, axis=0))
            t_s[at] = res.reshape(pack, hy, cq)
            return 0

        lax.fori_loop(0, nx // pack, yback, 0, unroll=2)
        for yb in range(tiles):
            at = slice(yb * SUB, (yb + 1) * SUB)
            res = const_times(kxh_ref[...], kxl_ref[...], t_s[:, at, :].reshape(nx * SUB, cq))
            x_s[:, at, :] = res.reshape(nx, SUB, cq)
        for slot, out in zip(slots, outs):

            @pl.when(window_of(nt, q, slot) == w)
            def _(out=out):
                out[...] = x_s[...]

        return 0

    lax.fori_loop(lo, hi, back, 0)


def relay_kernel(nt, q_ref, early_ref, late_ref, out_ref):
    @pl.when(q_ref[0] == nt - 1)
    def _():
        out_ref[...] = early_ref[...]

    @pl.when(q_ref[0] != nt - 1)
    def _():
        out_ref[...] = late_ref[...]


def half_kernel(nt, q_ref, c_ref, *refs):
    ins, (acc_ref, wh_ref, wl_ref) = refs[:2], refs[2:]
    nx, hy, nz = acc_ref.shape
    cq = nz // nt
    q = q_ref[0]
    for d in range(2, nt):
        at = slice((d - 2) * cq, (d - 1) * cq)
        wh_ref[at, :] = c_ref[jnp.bitwise_xor(q, d), 0]
        wl_ref[at, :] = c_ref[jnp.bitwise_xor(q, d), 1]
    wh, wl = (jnp.concatenate([c_ref[jnp.bitwise_xor(q, d), i] for d in range(2)], axis=0) for i in range(2))
    for x in range(0, nx, SUB):
        part = [ref[x : x + SUB].reshape(SUB * hy, cq) for ref in ins]
        xh, xl = cut(jnp.concatenate(part, axis=1))
        res = mm(xh, wh) + mm(xh, wl) + mm(xl, wh)
        acc_ref[x : x + SUB] = res.reshape(SUB, hy, nz)


def final_kernel(nt, q_ref, acc_ref, wh_ref, wl_ref, *refs):
    ins, out_ref = refs[:-1], refs[-1]
    xb, hy, nz = out_ref.shape[1:]
    cq = nz // nt
    parts = [x[...].reshape(xb * hy, cq) for x in ins]
    if nt == 4:
        relayed = parts.pop()
        parts[0] = jnp.where(q_ref[0] == 3, relayed, parts[0])
        parts[1] = jnp.where(q_ref[0] == 2, relayed, parts[1])
    xh, xl = cut(jnp.concatenate(parts, axis=1))
    res = mm(xh, wh_ref[...]) + mm(xh, wl_ref[...]) + mm(xl, wh_ref[...])
    out_ref[0] = acc_ref[...] + res.reshape(xb, hy, nz)


def merge_kernel(nt, q_ref, *refs):
    ins, outs = refs[:nt], refs[nt:]
    for d in range(nt):
        for face in range(2):
            outs[face][jnp.bitwise_xor(q_ref[0], d)] = ins[d][face]


def spread_kernel(nt, steps, tab_ref, left_ref, right_ref, out_ref, line):
    hy = out_ref.shape[3]
    cq = out_ref.shape[4] // nt
    tiles = hy // SUB
    zero = jnp.zeros((SUB, cq), F32)
    for face, ref in enumerate((left_ref, right_ref)):
        le = closed_rows(tab_ref, face, tiles, hy)
        for c in range(nt):

            def step(k, _, face=face, c=c, ref=ref, le=le):
                r = [ref[c, k, i * SUB : (i + 1) * SUB, :] for i in range(tiles - 1)]
                for j in range(tiles):
                    if j == 0:
                        v = jnp.where(le[0], zero, r[0])
                    elif j < tiles - 1:
                        v = jnp.where(le[j], jnp.where(le[j - 1], r[j - 1], zero), r[j])
                    else:
                        v = jnp.where(le[j - 1], r[j - 1], zero)
                    line[face, k, pl.ds(j, SUB, stride=tiles), :] = v
                out_ref[0, face, k, :, c * cq : (c + 1) * cq] = line[face, k]
                return 0

            lax.fori_loop(0, steps, step, 0)


def sds(*shape):
    return jax.ShapeDtypeStruct(shape, F32)


def cost(flops, nbytes):
    return pl.CostEstimate(flops=int(flops), bytes_accessed=int(nbytes), transcendentals=0)


def grant(mib):
    return pltpu.CompilerParams(vmem_limit_bytes=mib << 20)


def local(
    initial_state,
    heat_source,
    source_amplitude,
    diffusivity,
    robin_param,
    spectrum_x,
    spectrum_y,
    spectrum_z,
    robin_in,
    open_flag,
    owner_side,
):
    nx, hy, nz = initial_state.shape
    nt = lax.axis_size("tm")
    ncores = lax.axis_size("cores")
    assert ncores == 2 and nt & (nt - 1) == 0 and nt >= 4
    cq = nz // nt
    steps = source_amplitude.shape[0]
    tiles = hy // SUB
    assert tiles == 4 and nx % 4 == 0
    q = lax.axis_index("tm")
    yc = lax.axis_index("cores")
    space = lax.axis_size("space")
    me = lax.axis_index("space")
    qv, ycv, mev = (jnp.reshape(i, (1,)).astype(jnp.int32) for i in (q, yc, me))
    dims = (nt, steps, nx, hy, cq)

    def xor_permute(x, d):
        return lax.ppermute(x, "tm", [(i, i ^ d) for i in range(nt)])

    def swap(x):
        return lax.ppermute(x, "cores", [(0, 1), (1, 0)])

    def along(x, by):
        return lax.ppermute(x, "space", [(i, (i + by) % space) for i in range(space)])

    base = np.stack(np_halves(np_cosine(nz, np.arange(nz)[:, None], np.arange(nz)[None])))
    base = jnp.asarray(base.reshape(2, nt, cq, nz).swapaxes(0, 1))
    kxh, kxl = (jnp.asarray(w) for w in np_bar(nx, False))
    kxih, kxil = (jnp.asarray(w) for w in np_bar(nx, True))
    ky, ki = (jnp.asarray(w) for w in np_second(hy))

    rows = 2 * steps * hy
    block = (None, 2, steps, hy, cq)
    cutting = pl.pallas_call(
        functools.partial(split_kernel, nt),
        out_shape=[sds(rows + steps, cq)] * nt + [sds(SUB, cq)] * 2,
        grid_spec=pltpu.PrefetchScalarGridSpec(
            num_scalar_prefetch=3,
            grid=(1,),
            in_specs=[SM] * 3
            + [
                pl.BlockSpec(block, lambda i, q, y, z, d=d: (0, 0, 0, 0, jnp.bitwise_xor(q[0], d)))
                for d in range(nt)
            ],
            out_specs=[pl.BlockSpec((rows + steps, cq), lambda i, q, y, z: (0, 0))] * nt
            + [pl.BlockSpec((SUB, cq), lambda i, q, y, z: (0, 0))] * 2,
        ),
        compiler_params=grant(18),
        cost_estimate=cost(0, 8 * nt * rows * cq),
        name="split",
    )
    *dealt, diff_rows, robin_param = cutting(
        qv, ycv, mev, source_amplitude, diffusivity, robin_param, *([robin_in] * nt)
    )
    piece = swap(dealt[0])

    def forward(values, planes):
        return pl.pallas_call(
            functools.partial(forward_kernel, planes > 0),
            out_shape=sds(nx + planes, hy, cq),
            in_specs=[SM] * 2 + [VM] * 4,
            out_specs=VM,
            compiler_params=grant(18),
            cost_estimate=cost(1e9, 3e6),
        )(qv, spectrum_y, values, base, kxh, kxl)

    s0 = forward(heat_source, 1)
    s1 = swap(s0)
    for d in range(1, nt):
        dealt[d] = xor_permute(dealt[d], d)
    n0 = forward(initial_state, 0)
    n1 = swap(n0)
    right_param = along(robin_param, -1)
    left_param = along(robin_param, 1)

    table = jax.ShapeDtypeStruct((2 * hy + 2 * (tiles - 1) * SUB, cq), jnp.int32)
    u_own, amps, tab, f_own, f_there, *chunks = pl.pallas_call(
        functools.partial(order_kernel, nt, space),
        out_shape=[sds(nt, 2, steps, hy, cq), sds(nt, steps, cq), table]
        + [sds(nx, hy, cq)] * 2
        + [sds(2, steps, hy, cq)] * (nt - 1),
        in_specs=[SM] * 6 + [VM] * (3 + nt),
        out_specs=[VM] * (4 + nt),
        compiler_params=grant(18),
        cost_estimate=cost(0, 3e6),
        name="order",
    )(
        qv, mev, spectrum_x, spectrum_y, open_flag, owner_side, diff_rows,
        spectrum_z.reshape(nt, cq), s1, *dealt,
    )
    for i in range(nt - 1):
        chunks[i] = swap(chunks[i])

    ends_shape, traces = sds(nt, nx, hy, cq), sds(2, 2, nt * steps, tiles, SUB, cq)
    driven, clos, s_there = pl.pallas_call(
        functools.partial(driven_kernel, dims),
        out_shape=[traces, ends_shape, sds(nx, hy, cq)],
        in_specs=[SM] + [VM] * 6,
        out_specs=[VM] * 3,
        scratch_shapes=[pltpu.VMEM((nx, hy, cq), F32)],
        compiler_params=grant(18),
        cost_estimate=cost(3e9, 6e6),
        name="driven",
    )(ycv, s0, s1, u_own, amps, f_own, ky)
    short = sds(2, steps, (tiles - 1) * SUB, cq)
    *hands, clos, m_there = pl.pallas_call(
        functools.partial(own_kernel, dims),
        out_shape=[short] * nt + [ends_shape, sds(nx, hy, cq)],
        in_specs=[SM] * 2 + [VM] * 10,
        out_specs=[VM] * (nt + 2),
        scratch_shapes=[pltpu.VMEM((nx, hy, cq), F32), pltpu.VMEM(traces.shape, F32)],
        compiler_params=grant(18),
        cost_estimate=cost(3e9, 8e6),
        name="own",
    )(qv, ycv, left_param, robin_param, right_param, n0, n1, driven, clos, tab, f_own, ky)
    for d in range(1, nt):
        hands[d] = xor_permute(hands[d], d)

    state, ends = m_there, [None] * nt
    piece = piece[:rows].reshape(2, steps, hy, cq)
    for stage, got in enumerate((chunks[:-2], chunks[-2:-1], chunks[-1:])):
        span = (nt - 2, 1, 2)[stage]
        slots = late_slots(nt) if stage == 2 else list(range(nt))
        prior = [ends[d] for d in slots] if stage else []
        *outs, state = pl.pallas_call(
            functools.partial(other_kernel, dims, stage),
            out_shape=[sds(nx, hy, cq)] * (len(slots) + 1),
            in_specs=[SM] * 2 + [VM] * (9 + len(got) + len(prior)),
            out_specs=[VM] * (len(slots) + 1),
            scratch_shapes=[
                pltpu.VMEM((span, nx, hy, cq), F32),
                pltpu.VMEM((nx, hy, cq), F32),
                pltpu.VMEM((nx, hy, cq), F32),
                pltpu.VMEM((span, 2, steps, hy, cq), F32),
            ],
            input_output_aliases={11 + len(got) + d: d for d in range(len(prior))},
            compiler_params=grant(18),
            cost_estimate=cost(2e9 * span, 2e6 * span),
        )(qv, ycv, state, s_there, f_there, amps, clos, ki, kxih, kxil, piece, *got, *prior)
        for d, out in zip(slots, outs):
            ends[d] = out
        for d in range(1, nt):
            if stage == 2 and d in slots or stage == 1 and d not in late_slots(nt):
                ends[d] = xor_permute(ends[d], d)
    if nt == 4:
        passing = pl.pallas_call(
            functools.partial(relay_kernel, nt),
            out_shape=sds(nx, hy, cq),
            in_specs=[SM] + [VM] * 2,
            out_specs=VM,
            compiler_params=grant(18),
            cost_estimate=cost(0, 1e6),
            name="relay",
        )(qv, ends[2], ends[3])
        ends.append(xor_permute(passing, 1))
    left, right = pl.pallas_call(
        functools.partial(merge_kernel, nt),
        out_shape=[sds(nt, steps, (tiles - 1) * SUB, cq)] * 2,
        in_specs=[SM] + [VM] * nt,
        out_specs=[VM] * 2,
        compiler_params=grant(18),
        cost_estimate=cost(0, 2e6),
        name="merge",
    )(qv, *hands)
    from_right = along(left, -1)
    from_left = along(right, 1)
    acc, wh, wl = pl.pallas_call(
        functools.partial(half_kernel, nt),
        out_shape=[sds(nx, hy, nz)] + [jax.ShapeDtypeStruct(((nt - 2) * cq, nz), BF16)] * 2,
        in_specs=[SM] + [VM] * 3,
        out_specs=[VM] * 3,
        compiler_params=grant(18),
        cost_estimate=cost(1e9, 4e6),
        name="half",
    )(qv, base, ends[0], ends[1])
    xb = SUB
    window_end = pl.pallas_call(
        functools.partial(final_kernel, nt),
        out_shape=sds(1, nx, hy, nz),
        grid_spec=pltpu.PrefetchScalarGridSpec(
            num_scalar_prefetch=1,
            grid=(nx // xb,),
            in_specs=[pl.BlockSpec((xb, hy, nz), lambda i, q: (i, 0, 0))]
            + [pl.BlockSpec(wh.shape, lambda i, q: (0, 0))] * 2
            + [pl.BlockSpec((xb, hy, cq), lambda i, q: (i, 0, 0))] * (len(ends) - 2),
            out_specs=pl.BlockSpec((1, xb, hy, nz), lambda i, q: (0, i, 0, 0)),
        ),
        compiler_params=grant(18),
        cost_estimate=cost(1e9, 6e6),
        name="final",
    )(qv, acc, wh, wl, *ends[2:])

    robin_out = pl.pallas_call(
        functools.partial(spread_kernel, nt, steps),
        out_shape=sds(1, 2, steps, hy, nz),
        in_specs=[VM] * 3,
        out_specs=VM,
        scratch_shapes=[pltpu.VMEM((2, steps, hy, cq), F32)],
        compiler_params=grant(18),
        cost_estimate=cost(0, 2e6),
        name="spread",
    )(tab, from_left, from_right)
    return robin_out, window_end


def solution(mesh):
    placed = (
        P("space", "cores", None),
        P("space", "cores", None),
        P("tm"),
        P("space"),
        P("space"),
        P(),
        P("cores"),
        P(),
        P("space", None, "tm", "cores", None),
        P(None, "cores"),
        P(None, "cores"),
    )

    return jax.shard_map(
        local,
        mesh=mesh,
        in_specs=placed,
        out_specs=(P("space", None, "tm", "cores", None), P("tm", "space", "cores", None)),
        check_vma=False,
    )
```

```python
import functools
import jax
import numpy as np
import jax.numpy as jnp
from jax import lax
from jax.experimental import pallas as pl
from jax.experimental.pallas import tpu as pltpu
from jax.sharding import PartitionSpec as P


F32 = jnp.float32
BF16 = jnp.bfloat16
SUB = 8


VM = pl.BlockSpec(memory_space=pltpu.VMEM)
SM = pl.BlockSpec(memory_space=pltpu.SMEM)


def cut(x):
    hi = x.astype(BF16)
    return hi, (x - hi.astype(F32)).astype(BF16)


def mm(a, b):
    return jnp.dot(a, b, preferred_element_type=F32)


def mmt(a, b):
    return lax.dot_general(a, b, (((1,), (1,)), ((), ())), preferred_element_type=F32)


def const_times(wh, wl, x):
    n = x.shape[1]
    xh, xl = cut(x)
    if n > 128:
        return mm(wh, xh) + mm(wh, xl) + mm(wl, xh)
    both = mm(wh, jnp.concatenate([xh, xl], axis=1))
    return both[:, :n] + both[:, n:] + mm(wl, xh)


def np_cosine(order, mode, node):
    mode = np.asarray(mode, np.float32)
    node = np.asarray(node, np.float32)
    scaling = np.where(mode == 0, np.sqrt(np.float32(1.0 / order)), np.sqrt(np.float32(2.0 / order)))
    angle = np.float32(np.pi) * mode * (node + np.float32(0.5)) / np.float32(order)
    return (scaling * np.cos(angle.astype(np.float64))).astype(np.float32)


def np_halves(w):
    hi = w.astype(BF16)
    return hi, (w - hi.astype(np.float32)).astype(BF16)


def np_modes(n):
    return np.concatenate([np.arange(0, n, 2), np.arange(1, n, 2)])


def np_bar(n, back):
    a = np_modes(n)
    base = np_cosine(n, a[:, None], np.arange(n)[None])
    edge = np_cosine(n, a, np.zeros(n))[:, None]
    w = (base * edge).T if back else base / edge
    return np_halves(np.kron(w, np.eye(SUB, dtype=np.float32)))


def np_second(hy):
    ny = 2 * hy
    pack = 256 // ny
    tiles = hy // SUB
    line = np.arange(hy)
    modes = tiles * (line % SUB) + line // SUB
    eye = np.eye(pack, dtype=np.float32)
    there, back = [], []
    for yc in range(2):
        sides = (yc, 1 - yc)
        blocks = [[np_cosine(ny, (m * hy + modes)[:, None], (n * hy + line)[None]) for n in sides] for m in sides]
        there.append(np.block([[np.kron(eye, b) for b in row] for row in blocks]))
        back.append(np.concatenate([np.kron(eye, row[0].T) for row in blocks], axis=1))
    return [np.stack([np_halves(w) for w in ws]) for ws in map(np.stack, (there, back))]


def tree(parts):
    while len(parts) > 1:
        parts = [a + b for a, b in zip(parts[::2], parts[1::2])] + (
            [parts[-1]] if len(parts) % 2 else []
        )
    return parts[0]


def piece_kernel(q_ref, yc_ref, me_ref, robin_ref, out_ref, sem):
    cq = out_ref.shape[3]
    at = pl.ds(pl.multiple_of(q_ref[0] * cq, cq), cq)
    copies = [
        pltpu.make_async_copy(robin_ref.at[0, face, :, :, at], out_ref.at[face], sem.at[face]) for face in range(2)
    ]
    for copy in copies:
        copy.start()
    for copy in copies:
        copy.wait()


def split_kernel(nt, q_ref, amp_ref, *refs):
    ins, (diff_ref, par_ref), refs = refs[:nt], refs[nt : nt + 2], refs[nt + 2 :]
    outs, (diff_out, par_out, diff_s, par_s, sem) = refs[:nt], refs[nt:]
    copies = [pltpu.make_async_copy(diff_ref, diff_s, sem.at[0]), pltpu.make_async_copy(par_ref, par_s, sem.at[1])]
    for copy in copies:
        copy.start()
    steps = amp_ref.shape[0]
    rows = outs[0].shape[0] - steps
    cq = outs[0].shape[1]
    for d in range(nt):
        outs[d][0:rows, :] = ins[d][...].reshape(rows, cq)
        for k in range(steps):
            outs[d][rows + k : rows + k + 1, :] = jnp.full((1, cq), amp_ref[k], F32)
    for copy in copies:
        copy.wait()
    diff_out[...] = jnp.full(diff_out.shape, diff_s[0], F32)
    par_out[...] = jnp.full(par_out.shape, par_s[0], F32)


def forward_block(x, c_ref, kxh_ref, kxl_ref):
    nx, _, nz = x.shape
    cq = c_ref.shape[1]
    xh, xl = cut(x.reshape(nx * SUB, nz))
    both = mmt(xh, c_ref[...].reshape(2 * cq, nz))
    z = both[:, :cq] + both[:, cq:] + mmt(xl, c_ref[0])
    return const_times(kxh_ref[...], kxl_ref[...], z).reshape(nx, SUB, cq)


def forward_kernel(with_sy, q_ref, sy_ref, x_ref, c_ref, kxh_ref, kxl_ref, out_ref):
    nx, hy, _ = x_ref.shape
    cq = out_ref.shape[2]
    tiles = hy // SUB
    if with_sy:
        for r in range(hy):
            b = tiles * (r % SUB) + r // SUB
            out_ref[nx, r : r + 1, :] = jnp.full((1, cq), sy_ref[b], F32)
    for t in range(tiles):
        at = slice(t * SUB, (t + 1) * SUB)
        out_ref[0:nx, at, :] = forward_block(x_ref[:, at, :], c_ref.at[q_ref[0]], kxh_ref, kxl_ref)


def factor_into(f_ref, sx_ref, diff_ref, sy, sz):
    for i, a in enumerate(np_modes(f_ref.shape[0])):
        rate = (sx_ref[int(a)] + sy) + sz
        f_ref[i] = 1.0 / (1.0 + diff_ref[0:1, :] * rate)


def order_kernel(nt, space, q_ref, me_ref, sx_ref, sy_ref, open_ref, owner_ref, diff_ref, sz_ref, there_ref, *refs):
    ins, (u_ref, amp_ref, tab_ref, fo_ref, ft_ref), outs = refs[:nt], refs[nt : nt + 5], refs[nt + 5 :]
    steps = amp_ref.shape[1]
    rows = ins[0].shape[0] - steps
    nx, hy, cq = fo_ref.shape
    tiles = hy // SUB
    for d in range(nt):
        w = jnp.bitwise_xor(q_ref[0], d)
        u_ref[w] = ins[d][0:rows, :].reshape(u_ref.shape[1:])
        amp_ref[w] = ins[d][rows:, :]
    for i, out in enumerate(outs):
        out[...] = u_ref[jnp.where(i < q_ref[0], i, i + 1)]
    for face in range(2):
        i = lax.rem(me_ref[0] + space - 1, space) if face == 0 else me_ref[0]
        for g in range(hy // tiles):
            closed = False
            for j in range(tiles):
                b = tiles * g + j
                r = face * hy + j * SUB + g
                tab_ref[r : r + 1, :] = jnp.full((1, cq), owner_ref[i, b], jnp.int32)
                closed = jnp.logical_or(closed, open_ref[i, b] == 0)
                if j < tiles - 1:
                    r = 2 * hy + (face * (tiles - 1) + j) * SUB + g
                    tab_ref[r : r + 1, :] = jnp.full((1, cq), closed.astype(jnp.int32), jnp.int32)
    sz = sz_ref[pl.ds(q_ref[0], 1), :]
    for r in range(hy):
        b = tiles * (r % SUB) + r // SUB
        fo_ref[0, r : r + 1, :] = jnp.full((1, cq), sy_ref[b], F32)
    factor_into(fo_ref, sx_ref, diff_ref, fo_ref[0], sz)
    factor_into(ft_ref, sx_ref, diff_ref, there_ref[nx], sz)


def closed_rows(tab_ref, face, tiles, hy):
    base = 2 * hy + face * (tiles - 1) * SUB
    return [tab_ref[base + i * SUB : base + (i + 1) * SUB, :] > 0 for i in range(tiles - 1)]


def transform_second(ky_ref, yc, here, there, own, oth):
    nx, hy, cq = own.shape
    pack = ky_ref.shape[2] // (2 * hy)
    half = pack * hy

    def step(ag, _):
        ats = [pl.ds((2 * ag + i) * pack, pack) for i in range(2)]
        cols = [
            jnp.concatenate([here[at].reshape(half, cq), there[at].reshape(half, cq)], axis=0) for at in ats
        ]
        res = const_times(ky_ref[yc, 0], ky_ref[yc, 1], jnp.concatenate(cols, axis=1))
        for i, at in enumerate(ats):
            part = res[:, i * cq : (i + 1) * cq]
            own[at] = part[:half].reshape(pack, hy, cq)
            oth[at] = part[half:].reshape(pack, hy, cq)
        return 0

    lax.fori_loop(0, nx // (2 * pack), step, 0)


def np_edges(nx):
    order = np_modes(nx)
    edge = np_cosine(nx, order, np.zeros(nx)).astype(np.float64)
    return edge, np_cosine(nx, order, np.ones(nx)).astype(np.float64) - edge


def driven_kernel(dims, yc_ref, s0, s1, u_s, amp_s, f_s, ky_ref, vd, clos_ref, so_ref, s_s):
    nt, steps, nx, hy, cq = dims
    tiles = hy // SUB
    transform_second(ky_ref, yc_ref[0], s0, s1, s_s, so_ref)
    ha = nx // 2
    chunk = min(SUB, ha)
    edge, slope = np_edges(nx)
    for j in range(tiles):
        rows = slice(j * SUB, (j + 1) * SUB)
        for par in range(2):
            for first in range(0, ha, chunk):
                modes = [par * ha + first + i for i in range(chunk)]
                s = [s_s[a, rows, :] for a in modes]
                f = [f_s[a, rows, :] for a in modes]
                wv = [float(np.float32(edge[a] * edge[a])) for a in modes]
                wd = [float(np.float32(edge[a] * slope[a])) for a in modes]

                def window(w, cur, j=j, par=par, first=first, rows=rows, modes=modes, s=s, f=f, wv=wv, wd=wd):
                    cur = list(cur)
                    for k in range(steps):
                        r0 = u_s[w, 0, k, pl.ds(j, SUB, stride=tiles), :]
                        r1 = u_s[w, 1, k, pl.ds(j, SUB, stride=tiles), :]
                        u = r0 + r1 if par == 0 else r0 - r1
                        amp = amp_s[w, k : k + 1, :]
                        cur = [(x + (amp * y + u)) * z for x, y, z in zip(cur, s, f)]
                        m = w * steps + k
                        v = tree([x * y for x, y in zip(cur, wv)])
                        d = tree([x * y for x, y in zip(cur, wd)])
                        if first:
                            v = v + vd[par, 0, m, j]
                            d = d + vd[par, 1, m, j]
                        vd[par, 0, m, j] = v
                        vd[par, 1, m, j] = d
                    for a, x in zip(modes, cur):
                        clos_ref[w, a, rows, :] = x
                    return tuple(cur)

                lax.fori_loop(0, nt, window, (jnp.zeros((SUB, cq), F32),) * chunk)


def own_kernel(dims, q_ref, yc_ref, *refs):
    nt, steps, nx, hy, _ = dims
    params, (n0, n1, driven, clos_in, tab_ref, f_s, ky_ref) = refs[:3], refs[3:10]
    hands, (clos_ref, mo_ref) = refs[10 : 10 + nt], refs[10 + nt : 12 + nt]
    m_s, vd = refs[12 + nt :]
    tiles = hy // SUB
    transform_second(ky_ref, yc_ref[0], n0, n1, m_s, mo_ref)
    ha = nx // 2
    edge, slope = np_edges(nx)
    for j in range(tiles):
        rows = slice(j * SUB, (j + 1) * SUB)
        for par in range(2):
            modes = [par * ha + i for i in range(ha)]
            f = [f_s[a, rows, :] for a in modes]
            ratio = [float(np.float32(slope[a] / edge[a])) for a in modes]

            def window(w, cur, j=j, par=par, rows=rows, modes=modes, f=f, ratio=ratio):
                cur = list(cur)
                for k in range(steps):
                    cur = [x * z for x, z in zip(cur, f)]
                    m = w * steps + k
                    vd[par, 0, m, j] = tree(cur)
                    vd[par, 1, m, j] = tree([x * y for x, y in zip(cur, ratio)])
                for a, x in zip(modes, cur):
                    clos_ref[w, a, rows, :] = clos_in[w, a, rows, :] + x * float(np.float32(edge[a] ** -2))
                return tuple(cur)

            start = tuple(m_s[a, rows, :] * float(np.float32(edge[a] ** 2)) for a in modes)
            lax.fori_loop(0, nt, window, start)

    params = [ref[...] for ref in params]
    for slot in range(nt):
        w = jnp.bitwise_xor(q_ref[0], slot)

        def combine(k, _, slot=slot, w=w):
            m = w * steps + k
            left, right = [], []
            for j in range(tiles):
                ve, vo, de, do = (
                    driven[par, kind, m, j] + vd[par, kind, m, j] for kind in range(2) for par in range(2)
                )
                p = [
                    jnp.where(
                        tab_ref[i * hy + j * SUB : i * hy + (j + 1) * SUB, :] == 0, params[i], params[i + 1]
                    )
                    for i in range(2)
                ]
                left.append((de + do) + p[0] * (ve + vo))
                right.append(p[1] * (ve - vo) + (de - do))
            for face, line in enumerate((left, right)):
                for i, le in enumerate(closed_rows(tab_ref, face, tiles, hy)):
                    hands[slot][face, k, i * SUB : (i + 1) * SUB, :] = jnp.where(le, line[i + 1], line[i])
            return 0

        lax.fori_loop(0, steps, combine, 0)


def window_of(nt, q, slot):
    if nt == 4 and slot >= 2:
        return jnp.bitwise_xor(q, jnp.where(q == 1, 5 - slot, slot))
    return jnp.bitwise_xor(q, slot)


def late_slots(nt):
    return [0, 1, 3] if nt == 4 else list(range(nt))


def slot_parts(slots, nt, nx):
    parts = []
    for slot in slots:
        cuts = (0, nx // 2, nx) if slot == nt - 1 else (0, nx)
        parts += [(slot, lo, hi) for lo, hi in zip(cuts[:-1], cuts[1:])]
    return parts


def other_kernel(
    dims, stage, q_ref, yc_ref, m_ref, s_ref, f_ref, amp_ref, clos_ref, ki_ref, kxh_ref, kxl_ref, own_ref, *refs
):
    nt, steps, nx, hy, cq = dims
    parts = slot_parts(late_slots(nt) if stage == 2 else range(nt), nt, nx)
    given = nt - 3 if stage == 0 else 1
    prior = 0 if stage == 0 else len(parts)
    chunks, refs = refs[:given], refs[given + prior :]
    outs = refs[: len(parts)]
    st_ref, cl, t_s, x_s, u_s = refs[len(parts) :]
    q = q_ref[0]
    edge = jnp.where(q < nt - 2, nt - 2, nt - 3)
    lo, hi = ((0, edge), (edge, edge + 1), (edge + 1, nt))[stage]

    def put(when, at, ref):
        @pl.when(when)
        def _():
            u_s[at] = ref[...]

    if stage == 0:
        for w in range(nt - 2):
            put(q == w, w, own_ref)
            if w < nt - 3:
                put(q > w, w, chunks[w])
            if w > 0:
                put(q < w, w, chunks[w - 1])
    elif stage == 1:
        u_s[0] = chunks[0][...]
    else:
        put(q != nt - 2, 0, chunks[0])
        put(q == nt - 2, 0, own_ref)
        put(q == nt - 2, 1, chunks[0])
        put(q == nt - 1, 1, own_ref)
    base = lo
    tiles = hy // SUB
    ha = nx // 2
    for j in range(tiles):
        rows = slice(j * SUB, (j + 1) * SUB)
        for par in range(2):
            modes = [par * ha + i for i in range(ha)]
            s = [s_ref[a, rows, :] for a in modes]
            f = [f_ref[a, rows, :] for a in modes]

            def window(w, cur, j=j, par=par, rows=rows, modes=modes, s=s, f=f):
                cur = list(cur)
                for k in range(steps):
                    r0 = u_s[w - base, 0, k, pl.ds(j, SUB, stride=tiles), :]
                    r1 = u_s[w - base, 1, k, pl.ds(j, SUB, stride=tiles), :]
                    u = r0 + r1 if par == 0 else r0 - r1
                    amp = amp_ref[w, k : k + 1, :]
                    cur = [(x + (amp * y + u)) * z for x, y, z in zip(cur, s, f)]
                for a, x in zip(modes, cur):
                    cl[w - base, a, rows, :] = x
                return tuple(cur)

            end = lax.fori_loop(lo, hi, window, tuple(m_ref[a, rows, :] for a in modes))
            for a, x in zip(modes, end):
                st_ref[a, rows, :] = x
    pack = ki_ref.shape[2] // hy
    half = pack * hy
    yc = yc_ref[0]

    def back(w, _):
        def yback(ag, _):
            at = pl.ds(ag * pack, pack)
            col = [clos_ref[w, at].reshape(half, cq), cl[w - base, at].reshape(half, cq)]
            res = const_times(ki_ref[yc, 0], ki_ref[yc, 1], jnp.concatenate(col, axis=0))
            t_s[at] = res.reshape(pack, hy, cq)
            return 0

        lax.fori_loop(0, nx // pack, yback, 0, unroll=2)
        for yb in range(tiles):
            at = slice(yb * SUB, (yb + 1) * SUB)
            res = const_times(kxh_ref[...], kxl_ref[...], t_s[:, at, :].reshape(nx * SUB, cq))
            x_s[:, at, :] = res.reshape(nx, SUB, cq)
        for (slot, r0, r1), out in zip(parts, outs):

            @pl.when(window_of(nt, q, slot) == w)
            def _(out=out, r0=r0, r1=r1):
                out[...] = x_s[r0:r1]

        return 0

    lax.fori_loop(lo, hi, back, 0)


def relay_kernel(nt, at, q_ref, early_ref, late_ref, out_ref):
    @pl.when(q_ref[0] == nt - 1)
    def _():
        out_ref[...] = early_ref[at : at + out_ref.shape[0]]

    @pl.when(q_ref[0] != nt - 1)
    def _():
        out_ref[...] = late_ref[...]


def half_kernel(nt, q_ref, c_ref, *refs):
    ins, (acc_ref, wh_ref, wl_ref) = refs[:2], refs[2:]
    nx, hy, nz = acc_ref.shape
    cq = nz // nt
    q = q_ref[0]
    for d in range(2, nt):
        at = slice((d - 2) * cq, (d - 1) * cq)
        wh_ref[at, :] = c_ref[jnp.bitwise_xor(q, d), 0]
        wl_ref[at, :] = c_ref[jnp.bitwise_xor(q, d), 1]
    wh, wl = (jnp.concatenate([c_ref[jnp.bitwise_xor(q, d), i] for d in range(2)], axis=0) for i in range(2))
    for x in range(0, nx, SUB):
        part = [ref[x : x + SUB].reshape(SUB * hy, cq) for ref in ins]
        xh, xl = cut(jnp.concatenate(part, axis=1))
        res = mm(xh, wh) + mm(xh, wl) + mm(xl, wh)
        acc_ref[x : x + SUB] = res.reshape(SUB, hy, nz)


def final_kernel(nt, at, q_ref, acc_ref, wh_ref, wl_ref, *refs):
    count = nt - 2 + (nt == 4)
    ins, (out_ref, blocks, sem) = refs[:count], refs[-3:]
    n, xb, hy, nz = blocks.shape
    cq = nz // nt
    copies = []
    for i in range(n):
        rows = slice(i * xb, (i + 1) * xb)
        whole = slice(at + i * xb, at + (i + 1) * xb)
        parts = [x[whole if d < nt - 3 else rows].reshape(xb * hy, cq) for d, x in enumerate(ins)]
        if nt == 4:
            relayed = parts.pop()
            parts[0] = jnp.where(q_ref[0] == 3, relayed, parts[0])
            parts[1] = jnp.where(q_ref[0] == 2, relayed, parts[1])
        xh, xl = cut(jnp.concatenate(parts, axis=1))
        res = mm(xh, wh_ref[...]) + mm(xh, wl_ref[...]) + mm(xl, wh_ref[...])
        blocks[i] = acc_ref[whole] + res.reshape(xb, hy, nz)
        copies.append(pltpu.make_async_copy(blocks.at[i], out_ref.at[0, whole], sem.at[i]))
        copies[-1].start()
    for copy in copies:
        copy.wait()


def merge_kernel(nt, q_ref, *refs):
    ins, outs = refs[:nt], refs[nt:]
    for d in range(nt):
        for face in range(2):
            outs[face][jnp.bitwise_xor(q_ref[0], d)] = ins[d][face]


def spread_kernel(nt, steps, tab_ref, left_ref, right_ref, out_ref, line, lanes, sem):
    hy = out_ref.shape[3]
    cq = out_ref.shape[4] // nt
    copies = []
    tiles = hy // SUB
    zero = jnp.zeros((SUB, cq), F32)
    for face, ref in enumerate((left_ref, right_ref)):
        le = closed_rows(tab_ref, face, tiles, hy)
        for c in range(nt):

            def step(k, _, face=face, c=c, ref=ref, le=le):
                r = [ref[c, k, i * SUB : (i + 1) * SUB, :] for i in range(tiles - 1)]
                for j in range(tiles):
                    if j == 0:
                        v = jnp.where(le[0], zero, r[0])
                    elif j < tiles - 1:
                        v = jnp.where(le[j], jnp.where(le[j - 1], r[j - 1], zero), r[j])
                    else:
                        v = jnp.where(le[j - 1], r[j - 1], zero)
                    line[face, k, pl.ds(j, SUB, stride=tiles), :] = v
                lanes[face, k, :, c * cq : (c + 1) * cq] = line[face, k]
                return 0

            lax.fori_loop(0, steps, step, 0)
        for part in range(2):
            ks = slice(part * steps // 2, (part + 1) * steps // 2)
            copy = pltpu.make_async_copy(lanes.at[face, ks], out_ref.at[0, face, ks], sem.at[2 * face + part])
            copy.start()
            copies.append(copy)
    for copy in copies:
        copy.wait()


def sds(*shape):
    return jax.ShapeDtypeStruct(shape, F32)


def cost(flops, nbytes):
    return pl.CostEstimate(flops=int(flops), bytes_accessed=int(nbytes), transcendentals=0)


def grant(mib):
    return pltpu.CompilerParams(vmem_limit_bytes=mib << 20)


def local(
    initial_state,
    heat_source,
    source_amplitude,
    diffusivity,
    robin_param,
    spectrum_x,
    spectrum_y,
    spectrum_z,
    robin_in,
    open_flag,
    owner_side,
):
    nx, hy, nz = initial_state.shape
    nt = lax.axis_size("tm")
    ncores = lax.axis_size("cores")
    assert ncores == 2 and nt & (nt - 1) == 0 and nt >= 4
    cq = nz // nt
    steps = source_amplitude.shape[0]
    tiles = hy // SUB
    assert tiles == 4 and nx % 4 == 0
    q = lax.axis_index("tm")
    yc = lax.axis_index("cores")
    space = lax.axis_size("space")
    me = lax.axis_index("space")
    qv, ycv, mev = (jnp.reshape(i, (1,)).astype(jnp.int32) for i in (q, yc, me))
    dims = (nt, steps, nx, hy, cq)

    def xor_permute(x, d):
        return lax.ppermute(x, "tm", [(i, i ^ d) for i in range(nt)])

    def swap(x):
        return lax.ppermute(x, "cores", [(0, 1), (1, 0)])

    def along(x, by):
        return lax.ppermute(x, "space", [(i, (i + by) % space) for i in range(space)])

    base = np.stack(np_halves(np_cosine(nz, np.arange(nz)[:, None], np.arange(nz)[None])))
    base = jnp.asarray(base.reshape(2, nt, cq, nz).swapaxes(0, 1))
    kxh, kxl = (jnp.asarray(w) for w in np_bar(nx, False))
    kxih, kxil = (jnp.asarray(w) for w in np_bar(nx, True))
    ky, ki = (jnp.asarray(w) for w in np_second(hy))

    rows = 2 * steps * hy
    block = (None, 2, steps, hy, cq)
    AN = pl.BlockSpec(memory_space=pl.ANY)
    piece = pl.pallas_call(
        piece_kernel,
        out_shape=sds(2, steps, hy, cq),
        in_specs=[SM] * 3 + [AN],
        out_specs=VM,
        scratch_shapes=[pltpu.SemaphoreType.DMA((2,))],
        compiler_params=grant(60),
        cost_estimate=cost(0, 5e5),
        name="piece",
    )(qv, ycv, mev, robin_in)
    piece = swap(piece)
    cutting = pl.pallas_call(
        functools.partial(split_kernel, nt),
        out_shape=[sds(rows + steps, cq)] * nt + [sds(SUB, cq)] * 2,
        grid_spec=pltpu.PrefetchScalarGridSpec(
            num_scalar_prefetch=1,
            grid=(1,),
            in_specs=[SM]
            + [
                pl.BlockSpec(block, lambda i, q, d=d: (0, 0, 0, 0, jnp.bitwise_xor(q[0], d)))
                for d in range(nt)
            ]
            + [AN] * 2,
            out_specs=[pl.BlockSpec((rows + steps, cq), lambda i, q: (0, 0))] * nt
            + [pl.BlockSpec((SUB, cq), lambda i, q: (0, 0))] * 2,
            scratch_shapes=[pltpu.SMEM((1,), F32)] * 2 + [pltpu.SemaphoreType.DMA((2,))],
        ),
        compiler_params=grant(18),
        cost_estimate=cost(0, 8 * nt * rows * cq),
        name="split",
    )
    *dealt, diff_rows, robin_param = cutting(
        qv, source_amplitude, *([robin_in] * nt), diffusivity, robin_param
    )

    def forward(values, planes):
        return pl.pallas_call(
            functools.partial(forward_kernel, planes > 0),
            out_shape=sds(nx + planes, hy, cq),
            in_specs=[SM] * 2 + [VM] * 4,
            out_specs=VM,
            compiler_params=grant(18),
            cost_estimate=cost(1e9, 3e6),
        )(qv, spectrum_y, values, base, kxh, kxl)

    s0 = forward(heat_source, 1)
    s1 = swap(s0)
    for d in range(1, nt):
        dealt[d] = xor_permute(dealt[d], d)
    n0 = forward(initial_state, 0)
    n1 = swap(n0)
    right_param = along(robin_param, -1)
    left_param = along(robin_param, 1)

    table = jax.ShapeDtypeStruct((2 * hy + 2 * (tiles - 1) * SUB, cq), jnp.int32)
    u_own, amps, tab, f_own, f_there, *chunks = pl.pallas_call(
        functools.partial(order_kernel, nt, space),
        out_shape=[sds(nt, 2, steps, hy, cq), sds(nt, steps, cq), table]
        + [sds(nx, hy, cq)] * 2
        + [sds(2, steps, hy, cq)] * (nt - 1),
        in_specs=[SM] * 6 + [VM] * (3 + nt),
        out_specs=[VM] * (4 + nt),
        compiler_params=grant(18),
        cost_estimate=cost(0, 3e6),
        name="order",
    )(
        qv, mev, spectrum_x, spectrum_y, open_flag, owner_side, diff_rows,
        spectrum_z.reshape(nt, cq), s1, *dealt,
    )
    for i in range(nt - 1):
        chunks[i] = swap(chunks[i])

    ends_shape, traces = sds(nt, nx, hy, cq), sds(2, 2, nt * steps, tiles, SUB, cq)
    driven, clos, s_there = pl.pallas_call(
        functools.partial(driven_kernel, dims),
        out_shape=[traces, ends_shape, sds(nx, hy, cq)],
        in_specs=[SM] + [VM] * 6,
        out_specs=[VM] * 3,
        scratch_shapes=[pltpu.VMEM((nx, hy, cq), F32)],
        compiler_params=grant(18),
        cost_estimate=cost(3e9, 6e6),
        name="driven",
    )(ycv, s0, s1, u_own, amps, f_own, ky)
    short = sds(2, steps, (tiles - 1) * SUB, cq)
    *hands, clos, m_there = pl.pallas_call(
        functools.partial(own_kernel, dims),
        out_shape=[short] * nt + [ends_shape, sds(nx, hy, cq)],
        in_specs=[SM] * 2 + [VM] * 10,
        out_specs=[VM] * (nt + 2),
        scratch_shapes=[pltpu.VMEM((nx, hy, cq), F32), pltpu.VMEM(traces.shape, F32)],
        compiler_params=grant(18),
        cost_estimate=cost(3e9, 8e6),
        name="own",
    )(qv, ycv, left_param, robin_param, right_param, n0, n1, driven, clos, tab, f_own, ky)
    for d in range(1, nt):
        hands[d] = xor_permute(hands[d], d)

    state, ends = m_there, {}
    for stage, got in enumerate((chunks[:-2], chunks[-2:-1], chunks[-1:])):
        span = (nt - 2, 1, 2)[stage]
        parts = slot_parts(late_slots(nt) if stage == 2 else range(nt), nt, nx)
        prior = [ends[part] for part in parts] if stage else []
        *outs, state = pl.pallas_call(
            functools.partial(other_kernel, dims, stage),
            out_shape=[sds(r1 - r0, hy, cq) for _, r0, r1 in parts] + [sds(nx, hy, cq)],
            in_specs=[SM] * 2 + [VM] * (9 + len(got) + len(prior)),
            out_specs=[VM] * (len(parts) + 1),
            scratch_shapes=[
                pltpu.VMEM((span, nx, hy, cq), F32),
                pltpu.VMEM((nx, hy, cq), F32),
                pltpu.VMEM((nx, hy, cq), F32),
                pltpu.VMEM((span, 2, steps, hy, cq), F32),
            ],
            input_output_aliases={11 + len(got) + d: d for d in range(len(prior))},
            compiler_params=grant(18),
            cost_estimate=cost(2e9 * span, 2e6 * span),
        )(qv, ycv, state, s_there, f_there, amps, clos, ki, kxih, kxil, piece, *got, *prior)
        for part, out in zip(parts, outs):
            ends[part] = out
        early = slot_parts([d for d in range(1, nt) if d not in late_slots(nt)], nt, nx)
        for d, r0, r1 in (early, parts)[stage - 1] if stage else ():
            if d:
                ends[d, r0, r1] = xor_permute(ends[d, r0, r1], d)
    middle = [ends[d, 0, nx] for d in range(nt - 1)]
    lasts = [ends[nt - 1, r0, r1] for r0, r1 in ((0, nx // 2), (nx // 2, nx))]
    passed = []
    for h, last in enumerate(lasts if nt == 4 else []):
        passing = pl.pallas_call(
            functools.partial(relay_kernel, nt, h * nx // 2),
            out_shape=sds(nx // 2, hy, cq),
            in_specs=[SM] + [VM] * 2,
            out_specs=VM,
            compiler_params=grant(18),
            cost_estimate=cost(0, 1e6),
        )(qv, middle[2], last)
        passed.append(xor_permute(passing, 1))
    left, right = pl.pallas_call(
        functools.partial(merge_kernel, nt),
        out_shape=[sds(nt, steps, (tiles - 1) * SUB, cq)] * 2,
        in_specs=[SM] + [VM] * nt,
        out_specs=[VM] * 2,
        compiler_params=grant(18),
        cost_estimate=cost(0, 2e6),
        name="merge",
    )(qv, *hands)
    from_right = along(left, -1)
    from_left = along(right, 1)
    acc, wh, wl = pl.pallas_call(
        functools.partial(half_kernel, nt),
        out_shape=[sds(nx, hy, nz)] + [jax.ShapeDtypeStruct(((nt - 2) * cq, nz), BF16)] * 2,
        in_specs=[SM] + [VM] * 3,
        out_specs=[VM] * 3,
        compiler_params=grant(18),
        cost_estimate=cost(1e9, 4e6),
        name="half",
    )(qv, base, *middle[:2])
    xb = 4
    window_end = []
    for h, last in enumerate(lasts):
        operands = (qv, acc, wh, wl, *middle[2:], last, *passed[h : h + 1])
        window_end = [
            pl.pallas_call(
                functools.partial(final_kernel, nt, h * nx // 2),
                out_shape=sds(1, nx, hy, nz),
                in_specs=[SM] + [VM] * (len(operands) - 1) + [AN] * len(window_end),
                out_specs=AN,
                scratch_shapes=[
                    pltpu.VMEM((nx // 2 // xb, xb, hy, nz), F32),
                    pltpu.SemaphoreType.DMA((nx // 2 // xb,)),
                ],
                input_output_aliases={len(operands): 0} if window_end else {},
                compiler_params=grant(18),
                cost_estimate=cost(1e9, 3e6),
            )(*operands, *window_end)
        ]

    robin_out = pl.pallas_call(
        functools.partial(spread_kernel, nt, steps),
        out_shape=sds(1, 2, steps, hy, nz),
        in_specs=[VM] * 3,
        out_specs=AN,
        scratch_shapes=[
            pltpu.VMEM((2, steps, hy, cq), F32),
            pltpu.VMEM((2, steps, hy, nz), F32),
            pltpu.SemaphoreType.DMA((4,)),
        ],
        compiler_params=grant(18),
        cost_estimate=cost(0, 2e6),
        name="spread",
    )(tab, from_left, from_right)
    return robin_out, window_end[0]


def solution(mesh):
    placed = (
        P("space", "cores", None),
        P("space", "cores", None),
        P("tm"),
        P("space"),
        P("space"),
        P(),
        P("cores"),
        P(),
        P("space", None, "tm", "cores", None),
        P(None, "cores"),
        P(None, "cores"),
    )

    return jax.shard_map(
        local,
        mesh=mesh,
        in_specs=placed,
        out_specs=(P("space", None, "tm", "cores", None), P("tm", "space", "cores", None)),
        check_vma=False,
    )
```

```python
import functools
import jax
import numpy as np
import jax.numpy as jnp
from jax import lax
from jax.experimental import pallas as pl
from jax.experimental.pallas import tpu as pltpu
from jax.sharding import PartitionSpec as P


F32 = jnp.float32
BF16 = jnp.bfloat16
SUB = 8


VM = pl.BlockSpec(memory_space=pltpu.VMEM)
SM = pl.BlockSpec(memory_space=pltpu.SMEM)


def cut(x):
    hi = x.astype(BF16)
    return hi, (x - hi.astype(F32)).astype(BF16)


def mm(a, b):
    return jnp.dot(a, b, preferred_element_type=F32)


def mmt(a, b):
    return lax.dot_general(a, b, (((1,), (1,)), ((), ())), preferred_element_type=F32)


def const_times(wh, wl, x):
    n = x.shape[1]
    xh, xl = cut(x)
    if n > 128:
        return mm(wh, xh) + mm(wh, xl) + mm(wl, xh)
    both = mm(wh, jnp.concatenate([xh, xl], axis=1))
    return both[:, :n] + both[:, n:] + mm(wl, xh)


def np_cosine(order, mode, node):
    mode = np.asarray(mode, np.float32)
    node = np.asarray(node, np.float32)
    scaling = np.where(mode == 0, np.sqrt(np.float32(1.0 / order)), np.sqrt(np.float32(2.0 / order)))
    angle = np.float32(np.pi) * mode * (node + np.float32(0.5)) / np.float32(order)
    return (scaling * np.cos(angle.astype(np.float64))).astype(np.float32)


def np_halves(w):
    hi = w.astype(BF16)
    return hi, (w - hi.astype(np.float32)).astype(BF16)


def np_modes(n):
    return np.concatenate([np.arange(0, n, 2), np.arange(1, n, 2)])


def np_bar(n, back):
    a = np_modes(n)
    base = np_cosine(n, a[:, None], np.arange(n)[None])
    edge = np_cosine(n, a, np.zeros(n))[:, None]
    w = (base * edge).T if back else base / edge
    return np_halves(np.kron(w, np.eye(SUB, dtype=np.float32)))


def np_second(hy):
    ny = 2 * hy
    pack = 256 // ny
    tiles = hy // SUB
    line = np.arange(hy)
    modes = tiles * (line % SUB) + line // SUB
    eye = np.eye(pack, dtype=np.float32)
    there, back = [], []
    for yc in range(2):
        sides = (yc, 1 - yc)
        blocks = [[np_cosine(ny, (m * hy + modes)[:, None], (n * hy + line)[None]) for n in sides] for m in sides]
        there.append(np.block([[np.kron(eye, b) for b in row] for row in blocks]))
        back.append(np.concatenate([np.kron(eye, row[0].T) for row in blocks], axis=1))
    return [np.stack([np_halves(w) for w in ws]) for ws in map(np.stack, (there, back))]


def tree(parts):
    while len(parts) > 1:
        parts = [a + b for a, b in zip(parts[::2], parts[1::2])] + (
            [parts[-1]] if len(parts) % 2 else []
        )
    return parts[0]


def split_kernel(nt, q_ref, yc_ref, me_ref, amp_ref, *refs):
    ins, outs, piece_ref = refs[:nt], refs[nt : 2 * nt], refs[2 * nt]
    steps = amp_ref.shape[0]
    rows = outs[0].shape[0] - steps
    cq = outs[0].shape[1]
    piece_ref[...] = ins[0][...]
    for d in range(nt):
        outs[d][0:rows, :] = ins[d][...].reshape(rows, cq)
        for k in range(steps):
            outs[d][rows + k : rows + k + 1, :] = jnp.full((1, cq), amp_ref[k], F32)


def forward_block(x, c_ref, kxh_ref, kxl_ref):
    nx, _, nz = x.shape
    cq = c_ref.shape[1]
    xh, xl = cut(x.reshape(nx * SUB, nz))
    both = mmt(xh, c_ref[...].reshape(2 * cq, nz))
    z = both[:, :cq] + both[:, cq:] + mmt(xl, c_ref[0])
    return const_times(kxh_ref[...], kxl_ref[...], z).reshape(nx, SUB, cq)


def forward_kernel(with_sy, q_ref, sy_ref, x_ref, c_ref, kxh_ref, kxl_ref, out_ref):
    nx, hy, _ = x_ref.shape
    cq = out_ref.shape[2]
    tiles = hy // SUB
    if with_sy:
        for r in range(hy):
            b = tiles * (r % SUB) + r // SUB
            out_ref[nx, r : r + 1, :] = jnp.full((1, cq), sy_ref[b], F32)
    for t in range(tiles):
        at = slice(t * SUB, (t + 1) * SUB)
        out_ref[0:nx, at, :] = forward_block(x_ref[:, at, :], c_ref.at[q_ref[0]], kxh_ref, kxl_ref)


def forward_second_kernel(q_ref, diff_ref, par_ref, x_ref, c_ref, kxh_ref, kxl_ref, out_ref, diff_out, par_out):
    diff_out[...] = jnp.full(diff_out.shape, diff_ref[0], F32)
    par_out[...] = jnp.full(par_out.shape, par_ref[0], F32)
    forward_kernel(False, q_ref, None, x_ref, c_ref, kxh_ref, kxl_ref, out_ref)


def factor_into(f_ref, sx_ref, diff_ref, sy, sz):
    for i, a in enumerate(np_modes(f_ref.shape[0])):
        rate = (sx_ref[int(a)] + sy) + sz
        f_ref[i] = 1.0 / (1.0 + diff_ref[0:1, :] * rate)


def order_kernel(nt, space, q_ref, me_ref, sx_ref, sy_ref, open_ref, owner_ref, diff_ref, sz_ref, there_ref, *refs):
    ins, (u_ref, amp_ref, tab_ref, fo_ref, ft_ref), outs = refs[:nt], refs[nt : nt + 5], refs[nt + 5 :]
    steps = amp_ref.shape[1]
    rows = ins[0].shape[0] - steps
    nx, hy, cq = fo_ref.shape
    tiles = hy // SUB
    for d in range(nt):
        w = jnp.bitwise_xor(q_ref[0], d)
        u_ref[w] = ins[d][0:rows, :].reshape(u_ref.shape[1:])
        amp_ref[w] = ins[d][rows:, :]
    for i, out in enumerate(outs):
        out[...] = u_ref[jnp.where(i < q_ref[0], i, i + 1)]
    for face in range(2):
        i = lax.rem(me_ref[0] + space - 1, space) if face == 0 else me_ref[0]
        for g in range(hy // tiles):
            closed = False
            for j in range(tiles):
                b = tiles * g + j
                r = face * hy + j * SUB + g
                tab_ref[r : r + 1, :] = jnp.full((1, cq), owner_ref[i, b], jnp.int32)
                closed = jnp.logical_or(closed, open_ref[i, b] == 0)
                if j < tiles - 1:
                    r = 2 * hy + (face * (tiles - 1) + j) * SUB + g
                    tab_ref[r : r + 1, :] = jnp.full((1, cq), closed.astype(jnp.int32), jnp.int32)
    sz = sz_ref[pl.ds(q_ref[0], 1), :]
    for r in range(hy):
        b = tiles * (r % SUB) + r // SUB
        fo_ref[0, r : r + 1, :] = jnp.full((1, cq), sy_ref[b], F32)
    factor_into(fo_ref, sx_ref, diff_ref, fo_ref[0], sz)
    factor_into(ft_ref, sx_ref, diff_ref, there_ref[nx], sz)


def closed_rows(tab_ref, face, tiles, hy):
    base = 2 * hy + face * (tiles - 1) * SUB
    return [tab_ref[base + i * SUB : base + (i + 1) * SUB, :] > 0 for i in range(tiles - 1)]


def transform_second(ky_ref, yc, here, there, own, oth):
    nx, hy, cq = own.shape
    pack = ky_ref.shape[2] // (2 * hy)
    half = pack * hy

    def step(ag, _):
        ats = [pl.ds((2 * ag + i) * pack, pack) for i in range(2)]
        cols = [
            jnp.concatenate([here[at].reshape(half, cq), there[at].reshape(half, cq)], axis=0) for at in ats
        ]
        res = const_times(ky_ref[yc, 0], ky_ref[yc, 1], jnp.concatenate(cols, axis=1))
        for i, at in enumerate(ats):
            part = res[:, i * cq : (i + 1) * cq]
            own[at] = part[:half].reshape(pack, hy, cq)
            oth[at] = part[half:].reshape(pack, hy, cq)
        return 0

    lax.fori_loop(0, nx // (2 * pack), step, 0)


def np_edges(nx):
    order = np_modes(nx)
    edge = np_cosine(nx, order, np.zeros(nx)).astype(np.float64)
    return edge, np_cosine(nx, order, np.ones(nx)).astype(np.float64) - edge


def driven_kernel(dims, yc_ref, s0, s1, u_s, amp_s, f_s, ky_ref, vd, clos_ref, so_ref, s_s):
    nt, steps, nx, hy, cq = dims
    tiles = hy // SUB
    transform_second(ky_ref, yc_ref[0], s0, s1, s_s, so_ref)
    ha = nx // 2
    chunk = min(SUB, ha)
    edge, slope = np_edges(nx)
    for j in range(tiles):
        rows = slice(j * SUB, (j + 1) * SUB)
        for par in range(2):
            for first in range(0, ha, chunk):
                modes = [par * ha + first + i for i in range(chunk)]
                s = [s_s[a, rows, :] for a in modes]
                f = [f_s[a, rows, :] for a in modes]
                wv = [float(np.float32(edge[a] * edge[a])) for a in modes]
                wd = [float(np.float32(edge[a] * slope[a])) for a in modes]

                def window(w, cur, j=j, par=par, first=first, rows=rows, modes=modes, s=s, f=f, wv=wv, wd=wd):
                    cur = list(cur)
                    for k in range(steps):
                        r0 = u_s[w, 0, k, pl.ds(j, SUB, stride=tiles), :]
                        r1 = u_s[w, 1, k, pl.ds(j, SUB, stride=tiles), :]
                        u = r0 + r1 if par == 0 else r0 - r1
                        amp = amp_s[w, k : k + 1, :]
                        cur = [(x + (amp * y + u)) * z for x, y, z in zip(cur, s, f)]
                        m = w * steps + k
                        v = tree([x * y for x, y in zip(cur, wv)])
                        d = tree([x * y for x, y in zip(cur, wd)])
                        if first:
                            v = v + vd[par, 0, m, j]
                            d = d + vd[par, 1, m, j]
                        vd[par, 0, m, j] = v
                        vd[par, 1, m, j] = d
                    for a, x in zip(modes, cur):
                        clos_ref[w, a, rows, :] = x
                    return tuple(cur)

                lax.fori_loop(0, nt, window, (jnp.zeros((SUB, cq), F32),) * chunk)


def own_kernel(dims, q_ref, yc_ref, *refs):
    nt, steps, nx, hy, _ = dims
    params, (n0, n1, driven, clos_in, tab_ref, f_s, ky_ref) = refs[:3], refs[3:10]
    hands, (clos_ref, mo_ref) = refs[10 : 10 + nt], refs[10 + nt : 12 + nt]
    m_s, vd = refs[12 + nt :]
    tiles = hy // SUB
    transform_second(ky_ref, yc_ref[0], n0, n1, m_s, mo_ref)
    ha = nx // 2
    edge, slope = np_edges(nx)
    for j in range(tiles):
        rows = slice(j * SUB, (j + 1) * SUB)
        for par in range(2):
            modes = [par * ha + i for i in range(ha)]
            f = [f_s[a, rows, :] for a in modes]
            ratio = [float(np.float32(slope[a] / edge[a])) for a in modes]

            def window(w, cur, j=j, par=par, rows=rows, modes=modes, f=f, ratio=ratio):
                cur = list(cur)
                for k in range(steps):
                    cur = [x * z for x, z in zip(cur, f)]
                    m = w * steps + k
                    vd[par, 0, m, j] = tree(cur)
                    vd[par, 1, m, j] = tree([x * y for x, y in zip(cur, ratio)])
                for a, x in zip(modes, cur):
                    clos_ref[w, a, rows, :] = clos_in[w, a, rows, :] + x * float(np.float32(edge[a] ** -2))
                return tuple(cur)

            start = tuple(m_s[a, rows, :] * float(np.float32(edge[a] ** 2)) for a in modes)
            lax.fori_loop(0, nt, window, start)

    params = [ref[...] for ref in params]
    for slot in range(nt):
        w = jnp.bitwise_xor(q_ref[0], slot)

        def combine(k, _, slot=slot, w=w):
            m = w * steps + k
            left, right = [], []
            for j in range(tiles):
                ve, vo, de, do = (
                    driven[par, kind, m, j] + vd[par, kind, m, j] for kind in range(2) for par in range(2)
                )
                p = [
                    jnp.where(
                        tab_ref[i * hy + j * SUB : i * hy + (j + 1) * SUB, :] == 0, params[i], params[i + 1]
                    )
                    for i in range(2)
                ]
                left.append((de + do) + p[0] * (ve + vo))
                right.append(p[1] * (ve - vo) + (de - do))
            for face, line in enumerate((left, right)):
                for i, le in enumerate(closed_rows(tab_ref, face, tiles, hy)):
                    hands[slot][face, k, i * SUB : (i + 1) * SUB, :] = jnp.where(le, line[i + 1], line[i])
            return 0

        lax.fori_loop(0, steps, combine, 0)


def window_of(nt, q, slot):
    if nt == 4 and slot >= 2:
        return jnp.bitwise_xor(q, jnp.where(q == 1, 5 - slot, slot))
    return jnp.bitwise_xor(q, slot)


def late_slots(nt):
    return [0, 1, 3] if nt == 4 else list(range(nt))


def slot_parts(slots, nt, nx):
    parts = []
    for slot in slots:
        cuts = (0, nx // 2, nx) if slot == nt - 1 else (0, nx)
        parts += [(slot, lo, hi) for lo, hi in zip(cuts[:-1], cuts[1:])]
    return parts


def other_kernel(
    dims, stage, q_ref, yc_ref, m_ref, s_ref, f_ref, amp_ref, clos_ref, ki_ref, kxh_ref, kxl_ref, own_ref, *refs
):
    nt, steps, nx, hy, cq = dims
    parts = slot_parts(late_slots(nt) if stage == 2 else range(nt), nt, nx)
    given = nt - 3 if stage == 0 else 1
    prior = 0 if stage == 0 else len(parts)
    chunks, refs = refs[:given], refs[given + prior :]
    outs = refs[: len(parts)]
    st_ref, cl, t_s, x_s, u_s = refs[len(parts) :]
    q = q_ref[0]
    edge = jnp.where(q < nt - 2, nt - 2, nt - 3)
    lo, hi = ((0, edge), (edge, edge + 1), (edge + 1, nt))[stage]

    def put(when, at, ref):
        @pl.when(when)
        def _():
            u_s[at] = ref[...]

    if stage == 0:
        for w in range(nt - 2):
            put(q == w, w, own_ref)
            if w < nt - 3:
                put(q > w, w, chunks[w])
            if w > 0:
                put(q < w, w, chunks[w - 1])
    elif stage == 1:
        u_s[0] = chunks[0][...]
    else:
        put(q != nt - 2, 0, chunks[0])
        put(q == nt - 2, 0, own_ref)
        put(q == nt - 2, 1, chunks[0])
        put(q == nt - 1, 1, own_ref)
    base = lo
    tiles = hy // SUB
    ha = nx // 2
    for j in range(tiles):
        rows = slice(j * SUB, (j + 1) * SUB)
        for par in range(2):
            modes = [par * ha + i for i in range(ha)]
            s = [s_ref[a, rows, :] for a in modes]
            f = [f_ref[a, rows, :] for a in modes]

            def window(w, cur, j=j, par=par, rows=rows, modes=modes, s=s, f=f):
                cur = list(cur)
                for k in range(steps):
                    r0 = u_s[w - base, 0, k, pl.ds(j, SUB, stride=tiles), :]
                    r1 = u_s[w - base, 1, k, pl.ds(j, SUB, stride=tiles), :]
                    u = r0 + r1 if par == 0 else r0 - r1
                    amp = amp_ref[w, k : k + 1, :]
                    cur = [(x + (amp * y + u)) * z for x, y, z in zip(cur, s, f)]
                for a, x in zip(modes, cur):
                    cl[w - base, a, rows, :] = x
                return tuple(cur)

            end = lax.fori_loop(lo, hi, window, tuple(m_ref[a, rows, :] for a in modes))
            for a, x in zip(modes, end):
                st_ref[a, rows, :] = x
    pack = ki_ref.shape[2] // hy
    half = pack * hy
    yc = yc_ref[0]

    def back(w, _):
        def yback(ag, _):
            at = pl.ds(ag * pack, pack)
            col = [clos_ref[w, at].reshape(half, cq), cl[w - base, at].reshape(half, cq)]
            res = const_times(ki_ref[yc, 0], ki_ref[yc, 1], jnp.concatenate(col, axis=0))
            t_s[at] = res.reshape(pack, hy, cq)
            return 0

        lax.fori_loop(0, nx // pack, yback, 0, unroll=2)
        for yb in range(tiles):
            at = slice(yb * SUB, (yb + 1) * SUB)
            res = const_times(kxh_ref[...], kxl_ref[...], t_s[:, at, :].reshape(nx * SUB, cq))
            x_s[:, at, :] = res.reshape(nx, SUB, cq)
        for (slot, r0, r1), out in zip(parts, outs):

            @pl.when(window_of(nt, q, slot) == w)
            def _(out=out, r0=r0, r1=r1):
                out[...] = x_s[r0:r1]

        return 0

    lax.fori_loop(lo, hi, back, 0)


def relay_kernel(nt, at, q_ref, early_ref, late_ref, out_ref):
    @pl.when(q_ref[0] == nt - 1)
    def _():
        out_ref[...] = early_ref[at : at + out_ref.shape[0]]

    @pl.when(q_ref[0] != nt - 1)
    def _():
        out_ref[...] = late_ref[...]


def half_kernel(nt, q_ref, c_ref, *refs):
    ins, (acc_ref, wh_ref, wl_ref) = refs[:2], refs[2:]
    nx, hy, nz = acc_ref.shape
    cq = nz // nt
    q = q_ref[0]
    for d in range(2, nt):
        at = slice((d - 2) * cq, (d - 1) * cq)
        wh_ref[at, :] = c_ref[jnp.bitwise_xor(q, d), 0]
        wl_ref[at, :] = c_ref[jnp.bitwise_xor(q, d), 1]
    wh, wl = (jnp.concatenate([c_ref[jnp.bitwise_xor(q, d), i] for d in range(2)], axis=0) for i in range(2))
    for x in range(0, nx, SUB):
        part = [ref[x : x + SUB].reshape(SUB * hy, cq) for ref in ins]
        xh, xl = cut(jnp.concatenate(part, axis=1))
        res = mm(xh, wh) + mm(xh, wl) + mm(xl, wh)
        acc_ref[x : x + SUB] = res.reshape(SUB, hy, nz)


def final_kernel(nt, at, q_ref, acc_ref, wh_ref, wl_ref, *refs):
    count = nt - 2 + (nt == 4)
    ins, (out_ref, blocks, sem) = refs[:count], refs[-3:]
    n, xb, hy, nz = blocks.shape
    cq = nz // nt
    copies = []
    for i in range(n):
        rows = slice(i * xb, (i + 1) * xb)
        whole = slice(at + i * xb, at + (i + 1) * xb)
        parts = [x[whole if d < nt - 3 else rows].reshape(xb * hy, cq) for d, x in enumerate(ins)]
        if nt == 4:
            relayed = parts.pop()
            parts[0] = jnp.where(q_ref[0] == 3, relayed, parts[0])
            parts[1] = jnp.where(q_ref[0] == 2, relayed, parts[1])
        xh, xl = cut(jnp.concatenate(parts, axis=1))
        res = mm(xh, wh_ref[...]) + mm(xh, wl_ref[...]) + mm(xl, wh_ref[...])
        blocks[i] = acc_ref[whole] + res.reshape(xb, hy, nz)
        copies.append(pltpu.make_async_copy(blocks.at[i], out_ref.at[0, whole], sem.at[i]))
        copies[-1].start()
    for copy in copies:
        copy.wait()


def merge_kernel(nt, q_ref, *refs):
    ins, outs = refs[:nt], refs[nt:]
    for d in range(nt):
        for face in range(2):
            outs[face][jnp.bitwise_xor(q_ref[0], d)] = ins[d][face]


def spread_kernel(nt, steps, tab_ref, left_ref, right_ref, out_ref, line, lanes, sem):
    hy = out_ref.shape[3]
    cq = out_ref.shape[4] // nt
    copies = []
    tiles = hy // SUB
    zero = jnp.zeros((SUB, cq), F32)
    for face, ref in enumerate((left_ref, right_ref)):
        le = closed_rows(tab_ref, face, tiles, hy)
        for c in range(nt):

            def step(k, _, face=face, c=c, ref=ref, le=le):
                r = [ref[c, k, i * SUB : (i + 1) * SUB, :] for i in range(tiles - 1)]
                for j in range(tiles):
                    if j == 0:
                        v = jnp.where(le[0], zero, r[0])
                    elif j < tiles - 1:
                        v = jnp.where(le[j], jnp.where(le[j - 1], r[j - 1], zero), r[j])
                    else:
                        v = jnp.where(le[j - 1], r[j - 1], zero)
                    line[face, k, pl.ds(j, SUB, stride=tiles), :] = v
                lanes[face, k, :, c * cq : (c + 1) * cq] = line[face, k]
                return 0

            lax.fori_loop(0, steps, step, 0)
        for part in range(2):
            ks = slice(part * steps // 2, (part + 1) * steps // 2)
            copy = pltpu.make_async_copy(lanes.at[face, ks], out_ref.at[0, face, ks], sem.at[2 * face + part])
            copy.start()
            copies.append(copy)
    for copy in copies:
        copy.wait()


def sds(*shape):
    return jax.ShapeDtypeStruct(shape, F32)


def cost(flops, nbytes):
    return pl.CostEstimate(flops=int(flops), bytes_accessed=int(nbytes), transcendentals=0)


def grant(mib):
    return pltpu.CompilerParams(vmem_limit_bytes=mib << 20)


def local(
    initial_state,
    heat_source,
    source_amplitude,
    diffusivity,
    robin_param,
    spectrum_x,
    spectrum_y,
    spectrum_z,
    robin_in,
    open_flag,
    owner_side,
):
    nx, hy, nz = initial_state.shape
    nt = lax.axis_size("tm")
    ncores = lax.axis_size("cores")
    assert ncores == 2 and nt & (nt - 1) == 0 and nt >= 4
    cq = nz // nt
    steps = source_amplitude.shape[0]
    tiles = hy // SUB
    assert tiles == 4 and nx % 4 == 0
    q = lax.axis_index("tm")
    yc = lax.axis_index("cores")
    space = lax.axis_size("space")
    me = lax.axis_index("space")
    qv, ycv, mev = (jnp.reshape(i, (1,)).astype(jnp.int32) for i in (q, yc, me))
    dims = (nt, steps, nx, hy, cq)

    def xor_permute(x, d):
        return lax.ppermute(x, "tm", [(i, i ^ d) for i in range(nt)])

    def swap(x):
        return lax.ppermute(x, "cores", [(0, 1), (1, 0)])

    def along(x, by):
        return lax.ppermute(x, "space", [(i, (i + by) % space) for i in range(space)])

    base = np.stack(np_halves(np_cosine(nz, np.arange(nz)[:, None], np.arange(nz)[None])))
    base = jnp.asarray(base.reshape(2, nt, cq, nz).swapaxes(0, 1))
    kxh, kxl = (jnp.asarray(w) for w in np_bar(nx, False))
    kxih, kxil = (jnp.asarray(w) for w in np_bar(nx, True))
    ky, ki = (jnp.asarray(w) for w in np_second(hy))

    rows = 2 * steps * hy
    block = (None, 2, steps, hy, cq)
    AN = pl.BlockSpec(memory_space=pl.ANY)
    cutting = pl.pallas_call(
        functools.partial(split_kernel, nt),
        out_shape=[sds(rows + steps, cq)] * nt + [sds(2, steps, hy, cq)],
        grid_spec=pltpu.PrefetchScalarGridSpec(
            num_scalar_prefetch=3,
            grid=(1,),
            in_specs=[SM]
            + [
                pl.BlockSpec(block, lambda i, q, y, z, d=d: (0, 0, 0, 0, jnp.bitwise_xor(q[0], d)))
                for d in range(nt)
            ],
            out_specs=[pl.BlockSpec((rows + steps, cq), lambda i, q, y, z: (0, 0))] * nt
            + [pl.BlockSpec((2, steps, hy, cq), lambda i, q, y, z: (0, 0, 0, 0))],
        ),
        compiler_params=grant(18),
        cost_estimate=cost(0, 8 * nt * rows * cq),
        name="split",
    )
    *dealt, piece = cutting(qv, ycv, mev, source_amplitude, *([robin_in] * nt))
    piece = swap(piece)
    for d in range(1, nt):
        dealt[d] = xor_permute(dealt[d], d)

    s0 = pl.pallas_call(
        functools.partial(forward_kernel, True),
        out_shape=sds(nx + 1, hy, cq),
        in_specs=[SM] * 2 + [VM] * 4,
        out_specs=VM,
        compiler_params=grant(18),
        cost_estimate=cost(1e9, 3e6),
        name="forward0",
    )(qv, spectrum_y, heat_source, base, kxh, kxl)
    s1 = swap(s0)
    n0, diff_rows, robin_param = pl.pallas_call(
        forward_second_kernel,
        out_shape=[sds(nx, hy, cq), sds(SUB, cq), sds(SUB, cq)],
        in_specs=[SM] * 3 + [VM] * 4,
        out_specs=[VM] * 3,
        compiler_params=grant(18),
        cost_estimate=cost(1e9, 3e6),
        name="forward1",
    )(qv, diffusivity, robin_param, initial_state, base, kxh, kxl)
    n1 = swap(n0)
    right_param = along(robin_param, -1)
    left_param = along(robin_param, 1)

    table = jax.ShapeDtypeStruct((2 * hy + 2 * (tiles - 1) * SUB, cq), jnp.int32)
    u_own, amps, tab, f_own, f_there, *chunks = pl.pallas_call(
        functools.partial(order_kernel, nt, space),
        out_shape=[sds(nt, 2, steps, hy, cq), sds(nt, steps, cq), table]
        + [sds(nx, hy, cq)] * 2
        + [sds(2, steps, hy, cq)] * (nt - 1),
        in_specs=[SM] * 6 + [VM] * (3 + nt),
        out_specs=[VM] * (4 + nt),
        compiler_params=grant(18),
        cost_estimate=cost(0, 3e6),
        name="order",
    )(
        qv, mev, spectrum_x, spectrum_y, open_flag, owner_side, diff_rows,
        spectrum_z.reshape(nt, cq), s1, *dealt,
    )
    for i in range(nt - 1):
        chunks[i] = swap(chunks[i])

    ends_shape, traces = sds(nt, nx, hy, cq), sds(2, 2, nt * steps, tiles, SUB, cq)
    driven, clos, s_there = pl.pallas_call(
        functools.partial(driven_kernel, dims),
        out_shape=[traces, ends_shape, sds(nx, hy, cq)],
        in_specs=[SM] + [VM] * 6,
        out_specs=[VM] * 3,
        scratch_shapes=[pltpu.VMEM((nx, hy, cq), F32)],
        compiler_params=grant(18),
        cost_estimate=cost(3e9, 6e6),
        name="driven",
    )(ycv, s0, s1, u_own, amps, f_own, ky)
    short = sds(2, steps, (tiles - 1) * SUB, cq)
    *hands, clos, m_there = pl.pallas_call(
        functools.partial(own_kernel, dims),
        out_shape=[short] * nt + [ends_shape, sds(nx, hy, cq)],
        in_specs=[SM] * 2 + [VM] * 10,
        out_specs=[VM] * (nt + 2),
        scratch_shapes=[pltpu.VMEM((nx, hy, cq), F32), pltpu.VMEM(traces.shape, F32)],
        compiler_params=grant(18),
        cost_estimate=cost(3e9, 8e6),
        name="own",
    )(qv, ycv, left_param, robin_param, right_param, n0, n1, driven, clos, tab, f_own, ky)
    for d in range(1, nt):
        hands[d] = xor_permute(hands[d], d)

    state, ends = m_there, {}
    for stage, got in enumerate((chunks[:-2], chunks[-2:-1], chunks[-1:])):
        span = (nt - 2, 1, 2)[stage]
        parts = slot_parts(late_slots(nt) if stage == 2 else range(nt), nt, nx)
        prior = [ends[part] for part in parts] if stage else []
        *outs, state = pl.pallas_call(
            functools.partial(other_kernel, dims, stage),
            out_shape=[sds(r1 - r0, hy, cq) for _, r0, r1 in parts] + [sds(nx, hy, cq)],
            in_specs=[SM] * 2 + [VM] * (9 + len(got) + len(prior)),
            out_specs=[VM] * (len(parts) + 1),
            scratch_shapes=[
                pltpu.VMEM((span, nx, hy, cq), F32),
                pltpu.VMEM((nx, hy, cq), F32),
                pltpu.VMEM((nx, hy, cq), F32),
                pltpu.VMEM((span, 2, steps, hy, cq), F32),
            ],
            input_output_aliases={11 + len(got) + d: d for d in range(len(prior))},
            compiler_params=grant(18),
            cost_estimate=cost(2e9 * span, 2e6 * span),
        )(qv, ycv, state, s_there, f_there, amps, clos, ki, kxih, kxil, piece, *got, *prior)
        for part, out in zip(parts, outs):
            ends[part] = out
        early = slot_parts([d for d in range(1, nt) if d not in late_slots(nt)], nt, nx)
        for d, r0, r1 in (early, parts)[stage - 1] if stage else ():
            if d:
                ends[d, r0, r1] = xor_permute(ends[d, r0, r1], d)
    middle = [ends[d, 0, nx] for d in range(nt - 1)]
    lasts = [ends[nt - 1, r0, r1] for r0, r1 in ((0, nx // 2), (nx // 2, nx))]
    passed = []
    for h, last in enumerate(lasts if nt == 4 else []):
        passing = pl.pallas_call(
            functools.partial(relay_kernel, nt, h * nx // 2),
            out_shape=sds(nx // 2, hy, cq),
            in_specs=[SM] + [VM] * 2,
            out_specs=VM,
            compiler_params=grant(18),
            cost_estimate=cost(0, 1e6),
        )(qv, middle[2], last)
        passed.append(xor_permute(passing, 1))
    left, right = pl.pallas_call(
        functools.partial(merge_kernel, nt),
        out_shape=[sds(nt, steps, (tiles - 1) * SUB, cq)] * 2,
        in_specs=[SM] + [VM] * nt,
        out_specs=[VM] * 2,
        compiler_params=grant(18),
        cost_estimate=cost(0, 2e6),
        name="merge",
    )(qv, *hands)
    from_right = along(left, -1)
    from_left = along(right, 1)
    acc, wh, wl = pl.pallas_call(
        functools.partial(half_kernel, nt),
        out_shape=[sds(nx, hy, nz)] + [jax.ShapeDtypeStruct(((nt - 2) * cq, nz), BF16)] * 2,
        in_specs=[SM] + [VM] * 3,
        out_specs=[VM] * 3,
        compiler_params=grant(18),
        cost_estimate=cost(1e9, 4e6),
        name="half",
    )(qv, base, *middle[:2])
    xb = 4
    window_end = []
    for h, last in enumerate(lasts):
        operands = (qv, acc, wh, wl, *middle[2:], last, *passed[h : h + 1])
        window_end = [
            pl.pallas_call(
                functools.partial(final_kernel, nt, h * nx // 2),
                out_shape=sds(1, nx, hy, nz),
                in_specs=[SM] + [VM] * (len(operands) - 1) + [AN] * len(window_end),
                out_specs=AN,
                scratch_shapes=[
                    pltpu.VMEM((nx // 2 // xb, xb, hy, nz), F32),
                    pltpu.SemaphoreType.DMA((nx // 2 // xb,)),
                ],
                input_output_aliases={len(operands): 0} if window_end else {},
                compiler_params=grant(18),
                cost_estimate=cost(1e9, 3e6),
            )(*operands, *window_end)
        ]

    robin_out = pl.pallas_call(
        functools.partial(spread_kernel, nt, steps),
        out_shape=sds(1, 2, steps, hy, nz),
        in_specs=[VM] * 3,
        out_specs=AN,
        scratch_shapes=[
            pltpu.VMEM((2, steps, hy, cq), F32),
            pltpu.VMEM((2, steps, hy, nz), F32),
            pltpu.SemaphoreType.DMA((4,)),
        ],
        compiler_params=grant(18),
        cost_estimate=cost(0, 2e6),
        name="spread",
    )(tab, from_left, from_right)
    return robin_out, window_end[0]


def solution(mesh):
    placed = (
        P("space", "cores", None),
        P("space", "cores", None),
        P("tm"),
        P("space"),
        P("space"),
        P(),
        P("cores"),
        P(),
        P("space", None, "tm", "cores", None),
        P(None, "cores"),
        P(None, "cores"),
    )

    return jax.shard_map(
        local,
        mesh=mesh,
        in_specs=placed,
        out_specs=(P("space", None, "tm", "cores", None), P("tm", "space", "cores", None)),
        check_vma=False,
    )
```

```python
import functools
import jax
import numpy as np
import jax.numpy as jnp
from jax import lax
from jax.experimental import pallas as pl
from jax.experimental.pallas import tpu as pltpu
from jax.sharding import PartitionSpec as P


F32 = jnp.float32
BF16 = jnp.bfloat16
SUB = 8


VM = pl.BlockSpec(memory_space=pltpu.VMEM)
SM = pl.BlockSpec(memory_space=pltpu.SMEM)


def cut(x):
    hi = x.astype(BF16)
    return hi, (x - hi.astype(F32)).astype(BF16)


def mm(a, b):
    return jnp.dot(a, b, preferred_element_type=F32)


def mmt(a, b):
    return lax.dot_general(a, b, (((1,), (1,)), ((), ())), preferred_element_type=F32)


def const_times(wh, wl, x):
    n = x.shape[1]
    xh, xl = cut(x)
    if n > 128:
        return mm(wh, xh) + mm(wh, xl) + mm(wl, xh)
    both = mm(wh, jnp.concatenate([xh, xl], axis=1))
    return both[:, :n] + both[:, n:] + mm(wl, xh)


def np_cosine(order, mode, node):
    mode = np.asarray(mode, np.float32)
    node = np.asarray(node, np.float32)
    scaling = np.where(mode == 0, np.sqrt(np.float32(1.0 / order)), np.sqrt(np.float32(2.0 / order)))
    angle = np.float32(np.pi) * mode * (node + np.float32(0.5)) / np.float32(order)
    return (scaling * np.cos(angle.astype(np.float64))).astype(np.float32)


def np_halves(w):
    hi = w.astype(BF16)
    return hi, (w - hi.astype(np.float32)).astype(BF16)


def np_modes(n):
    return np.concatenate([np.arange(0, n, 2), np.arange(1, n, 2)])


def np_bar(n, back):
    a = np_modes(n)
    base = np_cosine(n, a[:, None], np.arange(n)[None])
    edge = np_cosine(n, a, np.zeros(n))[:, None]
    w = (base * edge).T if back else base / edge
    return np_halves(np.kron(w, np.eye(SUB, dtype=np.float32)))


def np_second(hy):
    ny = 2 * hy
    pack = 256 // ny
    tiles = hy // SUB
    line = np.arange(hy)
    modes = tiles * (line % SUB) + line // SUB
    eye = np.eye(pack, dtype=np.float32)
    there, back = [], []
    for yc in range(2):
        sides = (yc, 1 - yc)
        blocks = [[np_cosine(ny, (m * hy + modes)[:, None], (n * hy + line)[None]) for n in sides] for m in sides]
        there.append(np.block([[np.kron(eye, b) for b in row] for row in blocks]))
        back.append(np.concatenate([np.kron(eye, row[0].T) for row in blocks], axis=1))
    return [np.stack([np_halves(w) for w in ws]) for ws in map(np.stack, (there, back))]


def tree(parts):
    while len(parts) > 1:
        parts = [a + b for a, b in zip(parts[::2], parts[1::2])] + (
            [parts[-1]] if len(parts) % 2 else []
        )
    return parts[0]


def split_kernel(nt, q_ref, yc_ref, me_ref, *refs):
    for share, out in zip(refs[:nt], refs[nt:]):
        out[...] = share[...]


def forward_block(x, c_ref, kxh_ref, kxl_ref):
    nx, _, nz = x.shape
    cq = c_ref.shape[1]
    xh, xl = cut(x.reshape(nx * SUB, nz))
    both = mmt(xh, c_ref[...].reshape(2 * cq, nz))
    z = both[:, :cq] + both[:, cq:] + mmt(xl, c_ref[0])
    return const_times(kxh_ref[...], kxl_ref[...], z).reshape(nx, SUB, cq)


def forward_kernel(q_ref, x_ref, c_ref, kxh_ref, kxl_ref, out_ref):
    tiles = x_ref.shape[1] // SUB
    for t in range(tiles):
        at = slice(t * SUB, (t + 1) * SUB)
        out_ref[:, at, :] = forward_block(x_ref[:, at, :], c_ref.at[q_ref[0]], kxh_ref, kxl_ref)


def forward_second_kernel(q_ref, diff_ref, par_ref, x_ref, c_ref, kxh_ref, kxl_ref, out_ref, diff_out, par_out):
    diff_out[...] = jnp.full(diff_out.shape, diff_ref[0], F32)
    par_out[...] = jnp.full(par_out.shape, par_ref[0], F32)
    forward_kernel(q_ref, x_ref, c_ref, kxh_ref, kxl_ref, out_ref)


def factor_into(f_ref, sx_ref, diff_ref, sy, sz):
    for i, a in enumerate(np_modes(f_ref.shape[0])):
        rate = (sx_ref[int(a)] + sy) + sz
        f_ref[i] = 1.0 / (1.0 + diff_ref[0:1, :] * rate)


def order_kernel(nt, space, q_ref, me_ref, sx_ref, sy_ref, syt_ref, open_ref, owner_ref, *refs):
    amps, (diff_ref, sz_ref), refs = refs[:nt], refs[nt : nt + 2], refs[nt + 2 :]
    ins, (u_ref, amp_ref, tab_ref, fo_ref, ft_ref), outs = refs[:nt], refs[nt : nt + 5], refs[nt + 5 :]
    steps = amp_ref.shape[1]
    _, hy, cq = fo_ref.shape
    tiles = hy // SUB
    for d in range(nt):
        w = jnp.bitwise_xor(q_ref[0], d)
        u_ref[w] = ins[d][...]
        for k in range(steps):
            amp_ref[w, k : k + 1, :] = jnp.full((1, cq), amps[d][k], F32)
    for i, out in enumerate(outs):
        out[...] = u_ref[jnp.where(i < q_ref[0], i, i + 1)]
    for face in range(2):
        i = lax.rem(me_ref[0] + space - 1, space) if face == 0 else me_ref[0]
        for g in range(hy // tiles):
            closed = False
            for j in range(tiles):
                b = tiles * g + j
                r = face * hy + j * SUB + g
                tab_ref[r : r + 1, :] = jnp.full((1, cq), owner_ref[i, b], jnp.int32)
                closed = jnp.logical_or(closed, open_ref[i, b] == 0)
                if j < tiles - 1:
                    r = 2 * hy + (face * (tiles - 1) + j) * SUB + g
                    tab_ref[r : r + 1, :] = jnp.full((1, cq), closed.astype(jnp.int32), jnp.int32)
    sz = sz_ref[pl.ds(q_ref[0], 1), :]
    for r in range(hy):
        b = tiles * (r % SUB) + r // SUB
        fo_ref[0, r : r + 1, :] = jnp.full((1, cq), sy_ref[b], F32)
        ft_ref[0, r : r + 1, :] = jnp.full((1, cq), syt_ref[b], F32)
    factor_into(fo_ref, sx_ref, diff_ref, fo_ref[0], sz)
    factor_into(ft_ref, sx_ref, diff_ref, ft_ref[0], sz)


def closed_rows(tab_ref, face, tiles, hy):
    base = 2 * hy + face * (tiles - 1) * SUB
    return [tab_ref[base + i * SUB : base + (i + 1) * SUB, :] > 0 for i in range(tiles - 1)]


def transform_second(ky_ref, yc, here, there, own, oth):
    nx, hy, cq = own.shape
    pack = ky_ref.shape[2] // (2 * hy)
    half = pack * hy

    def step(ag, _):
        ats = [pl.ds((2 * ag + i) * pack, pack) for i in range(2)]
        cols = [
            jnp.concatenate([here[at].reshape(half, cq), there[at].reshape(half, cq)], axis=0) for at in ats
        ]
        res = const_times(ky_ref[yc, 0], ky_ref[yc, 1], jnp.concatenate(cols, axis=1))
        for i, at in enumerate(ats):
            part = res[:, i * cq : (i + 1) * cq]
            own[at] = part[:half].reshape(pack, hy, cq)
            oth[at] = part[half:].reshape(pack, hy, cq)
        return 0

    lax.fori_loop(0, nx // (2 * pack), step, 0)


def np_edges(nx):
    order = np_modes(nx)
    edge = np_cosine(nx, order, np.zeros(nx)).astype(np.float64)
    return edge, np_cosine(nx, order, np.ones(nx)).astype(np.float64) - edge


def driven_kernel(dims, yc_ref, s0, s1, u_s, amp_s, f_s, ky_ref, vd, clos_ref, so_ref, s_s):
    nt, steps, nx, hy, cq = dims
    tiles = hy // SUB
    transform_second(ky_ref, yc_ref[0], s0, s1, s_s, so_ref)
    ha = nx // 2
    chunk = min(SUB, ha)
    edge, slope = np_edges(nx)
    for j in range(tiles):
        rows = slice(j * SUB, (j + 1) * SUB)
        for par in range(2):
            for first in range(0, ha, chunk):
                modes = [par * ha + first + i for i in range(chunk)]
                s = [s_s[a, rows, :] for a in modes]
                f = [f_s[a, rows, :] for a in modes]
                wv = [float(np.float32(edge[a] * edge[a])) for a in modes]
                wd = [float(np.float32(edge[a] * slope[a])) for a in modes]

                def window(w, cur, j=j, par=par, first=first, rows=rows, modes=modes, s=s, f=f, wv=wv, wd=wd):
                    cur = list(cur)
                    for k in range(steps):
                        r0 = u_s[w, 0, k, pl.ds(j, SUB, stride=tiles), :]
                        r1 = u_s[w, 1, k, pl.ds(j, SUB, stride=tiles), :]
                        u = r0 + r1 if par == 0 else r0 - r1
                        amp = amp_s[w, k : k + 1, :]
                        cur = [(x + (amp * y + u)) * z for x, y, z in zip(cur, s, f)]
                        m = w * steps + k
                        v = tree([x * y for x, y in zip(cur, wv)])
                        d = tree([x * y for x, y in zip(cur, wd)])
                        if first:
                            v = v + vd[par, 0, m, j]
                            d = d + vd[par, 1, m, j]
                        vd[par, 0, m, j] = v
                        vd[par, 1, m, j] = d
                    for a, x in zip(modes, cur):
                        clos_ref[w, a, rows, :] = x
                    return tuple(cur)

                lax.fori_loop(0, nt, window, (jnp.zeros((SUB, cq), F32),) * chunk)


def own_kernel(dims, q_ref, yc_ref, *refs):
    nt, steps, nx, hy, _ = dims
    params, (n0, n1, driven, clos_in, tab_ref, f_s, ky_ref) = refs[:3], refs[3:10]
    hands, (clos_ref, mo_ref) = refs[10 : 10 + nt], refs[10 + nt : 12 + nt]
    m_s, vd = refs[12 + nt :]
    tiles = hy // SUB
    transform_second(ky_ref, yc_ref[0], n0, n1, m_s, mo_ref)
    ha = nx // 2
    edge, slope = np_edges(nx)
    for j in range(tiles):
        rows = slice(j * SUB, (j + 1) * SUB)
        for par in range(2):
            modes = [par * ha + i for i in range(ha)]
            f = [f_s[a, rows, :] for a in modes]
            ratio = [float(np.float32(slope[a] / edge[a])) for a in modes]

            def window(w, cur, j=j, par=par, rows=rows, modes=modes, f=f, ratio=ratio):
                cur = list(cur)
                for k in range(steps):
                    cur = [x * z for x, z in zip(cur, f)]
                    m = w * steps + k
                    vd[par, 0, m, j] = tree(cur)
                    vd[par, 1, m, j] = tree([x * y for x, y in zip(cur, ratio)])
                for a, x in zip(modes, cur):
                    clos_ref[w, a, rows, :] = clos_in[w, a, rows, :] + x * float(np.float32(edge[a] ** -2))
                return tuple(cur)

            start = tuple(m_s[a, rows, :] * float(np.float32(edge[a] ** 2)) for a in modes)
            lax.fori_loop(0, nt, window, start)

    params = [ref[...] for ref in params]
    for slot in range(nt):
        w = jnp.bitwise_xor(q_ref[0], slot)

        def combine(k, _, slot=slot, w=w):
            m = w * steps + k
            left, right = [], []
            for j in range(tiles):
                ve, vo, de, do = (
                    driven[par, kind, m, j] + vd[par, kind, m, j] for kind in range(2) for par in range(2)
                )
                p = [
                    jnp.where(
                        tab_ref[i * hy + j * SUB : i * hy + (j + 1) * SUB, :] == 0, params[i], params[i + 1]
                    )
                    for i in range(2)
                ]
                left.append((de + do) + p[0] * (ve + vo))
                right.append(p[1] * (ve - vo) + (de - do))
            for face, line in enumerate((left, right)):
                for i, le in enumerate(closed_rows(tab_ref, face, tiles, hy)):
                    hands[slot][face, k, i * SUB : (i + 1) * SUB, :] = jnp.where(le, line[i + 1], line[i])
            return 0

        lax.fori_loop(0, steps, combine, 0)


def window_of(nt, q, slot):
    if nt == 4 and slot >= 2:
        return jnp.bitwise_xor(q, jnp.where(q == 1, 5 - slot, slot))
    return jnp.bitwise_xor(q, slot)


def late_slots(nt):
    return [0, 1, 3] if nt == 4 else list(range(nt))


def late_cut(nx):
    return max(nx * 5 // 8 // 4 * 4, 4)


def slot_parts(slots, nt, nx):
    parts = []
    for slot in slots:
        cuts = (0, late_cut(nx), nx) if slot == nt - 1 else (0, nx)
        parts += [(slot, lo, hi) for lo, hi in zip(cuts[:-1], cuts[1:])]
    return parts


def other_kernel(
    dims, stage, q_ref, yc_ref, m_ref, s_ref, f_ref, amp_ref, clos_ref, ki_ref, kxh_ref, kxl_ref, own_ref, *refs
):
    nt, steps, nx, hy, cq = dims
    parts = slot_parts(late_slots(nt) if stage == 2 else range(nt), nt, nx)
    given = nt - 3 if stage == 0 else 1
    prior = 0 if stage == 0 else len(parts)
    chunks, refs = refs[:given], refs[given + prior :]
    outs = refs[: len(parts)]
    st_ref, cl, t_s, x_s, u_s = refs[len(parts) :]
    q = q_ref[0]
    edge = jnp.where(q < nt - 2, nt - 2, nt - 3)
    lo, hi = ((0, edge), (edge, edge + 1), (edge + 1, nt))[stage]

    def put(when, at, ref):
        @pl.when(when)
        def _():
            u_s[at] = ref[...]

    if stage == 0:
        for w in range(nt - 2):
            put(q == w, w, own_ref)
            if w < nt - 3:
                put(q > w, w, chunks[w])
            if w > 0:
                put(q < w, w, chunks[w - 1])
    elif stage == 1:
        u_s[0] = chunks[0][...]
    else:
        put(q != nt - 2, 0, chunks[0])
        put(q == nt - 2, 0, own_ref)
        put(q == nt - 2, 1, chunks[0])
        put(q == nt - 1, 1, own_ref)
    base = lo
    tiles = hy // SUB
    ha = nx // 2
    for j in range(tiles):
        rows = slice(j * SUB, (j + 1) * SUB)
        for par in range(2):
            modes = [par * ha + i for i in range(ha)]
            s = [s_ref[a, rows, :] for a in modes]
            f = [f_ref[a, rows, :] for a in modes]

            def window(w, cur, j=j, par=par, rows=rows, modes=modes, s=s, f=f):
                cur = list(cur)
                for k in range(steps):
                    r0 = u_s[w - base, 0, k, pl.ds(j, SUB, stride=tiles), :]
                    r1 = u_s[w - base, 1, k, pl.ds(j, SUB, stride=tiles), :]
                    u = r0 + r1 if par == 0 else r0 - r1
                    amp = amp_ref[w, k : k + 1, :]
                    cur = [(x + (amp * y + u)) * z for x, y, z in zip(cur, s, f)]
                for a, x in zip(modes, cur):
                    cl[w - base, a, rows, :] = x
                return tuple(cur)

            end = lax.fori_loop(lo, hi, window, tuple(m_ref[a, rows, :] for a in modes))
            for a, x in zip(modes, end):
                st_ref[a, rows, :] = x
    pack = ki_ref.shape[2] // hy
    half = pack * hy
    yc = yc_ref[0]

    def back(w, _):
        def yback(ag, _):
            at = pl.ds(ag * pack, pack)
            col = [clos_ref[w, at].reshape(half, cq), cl[w - base, at].reshape(half, cq)]
            res = const_times(ki_ref[yc, 0], ki_ref[yc, 1], jnp.concatenate(col, axis=0))
            t_s[at] = res.reshape(pack, hy, cq)
            return 0

        lax.fori_loop(0, nx // pack, yback, 0, unroll=2)
        for yb in range(tiles):
            at = slice(yb * SUB, (yb + 1) * SUB)
            res = const_times(kxh_ref[...], kxl_ref[...], t_s[:, at, :].reshape(nx * SUB, cq))
            x_s[:, at, :] = res.reshape(nx, SUB, cq)
        for (slot, r0, r1), out in zip(parts, outs):

            @pl.when(window_of(nt, q, slot) == w)
            def _(out=out, r0=r0, r1=r1):
                out[...] = x_s[r0:r1]

        return 0

    lax.fori_loop(lo, hi, back, 0)


def relay_kernel(nt, at, q_ref, early_ref, late_ref, out_ref):
    @pl.when(q_ref[0] == nt - 1)
    def _():
        out_ref[...] = early_ref[at : at + out_ref.shape[0]]

    @pl.when(q_ref[0] != nt - 1)
    def _():
        out_ref[...] = late_ref[...]


def half_kernel(nt, q_ref, c_ref, *refs):
    ins, (acc_ref, wh_ref, wl_ref) = refs[:2], refs[2:]
    nx, hy, nz = acc_ref.shape
    cq = nz // nt
    q = q_ref[0]
    for d in range(2, nt):
        at = slice((d - 2) * cq, (d - 1) * cq)
        wh_ref[at, :] = c_ref[jnp.bitwise_xor(q, d), 0]
        wl_ref[at, :] = c_ref[jnp.bitwise_xor(q, d), 1]
    wh, wl = (jnp.concatenate([c_ref[jnp.bitwise_xor(q, d), i] for d in range(2)], axis=0) for i in range(2))
    for x in range(0, nx, SUB):
        part = [ref[x : x + SUB].reshape(SUB * hy, cq) for ref in ins]
        xh, xl = cut(jnp.concatenate(part, axis=1))
        res = mm(xh, wh) + mm(xh, wl) + mm(xl, wh)
        acc_ref[x : x + SUB] = res.reshape(SUB, hy, nz)


def final_kernel(nt, at, q_ref, acc_ref, wh_ref, wl_ref, *refs):
    count = nt - 2 + (nt == 4)
    ins, (out_ref, blocks, sem) = refs[:count], refs[-3:]
    n, xb, hy, nz = blocks.shape
    cq = nz // nt
    copies = []
    for i in range(n):
        rows = slice(i * xb, (i + 1) * xb)
        whole = slice(at + i * xb, at + (i + 1) * xb)
        parts = [x[whole if d < nt - 3 else rows].reshape(xb * hy, cq) for d, x in enumerate(ins)]
        if nt == 4:
            relayed = parts.pop()
            parts[0] = jnp.where(q_ref[0] == 3, relayed, parts[0])
            parts[1] = jnp.where(q_ref[0] == 2, relayed, parts[1])
        xh, xl = cut(jnp.concatenate(parts, axis=1))
        res = mm(xh, wh_ref[...]) + mm(xh, wl_ref[...]) + mm(xl, wh_ref[...])
        blocks[i] = acc_ref[whole] + res.reshape(xb, hy, nz)
        copies.append(pltpu.make_async_copy(blocks.at[i], out_ref.at[0, whole], sem.at[i]))
        copies[-1].start()
    for copy in copies:
        copy.wait()


def merge_kernel(nt, q_ref, *refs):
    ins, outs = refs[:nt], refs[nt:]
    for d in range(nt):
        for face in range(2):
            outs[face][jnp.bitwise_xor(q_ref[0], d)] = ins[d][face]


def spread_kernel(nt, steps, tab_ref, left_ref, right_ref, out_ref, line, lanes, sem):
    hy = out_ref.shape[3]
    cq = out_ref.shape[4] // nt
    copies = []
    tiles = hy // SUB
    zero = jnp.zeros((SUB, cq), F32)
    for face, ref in enumerate((left_ref, right_ref)):
        le = closed_rows(tab_ref, face, tiles, hy)
        for c in range(nt):

            def step(k, _, face=face, c=c, ref=ref, le=le):
                r = [ref[c, k, i * SUB : (i + 1) * SUB, :] for i in range(tiles - 1)]
                for j in range(tiles):
                    if j == 0:
                        v = jnp.where(le[0], zero, r[0])
                    elif j < tiles - 1:
                        v = jnp.where(le[j], jnp.where(le[j - 1], r[j - 1], zero), r[j])
                    else:
                        v = jnp.where(le[j - 1], r[j - 1], zero)
                    line[face, k, pl.ds(j, SUB, stride=tiles), :] = v
                lanes[face, k, :, c * cq : (c + 1) * cq] = line[face, k]
                return 0

            lax.fori_loop(0, steps, step, 0)
        for part in range(2):
            ks = slice(part * steps // 2, (part + 1) * steps // 2)
            copy = pltpu.make_async_copy(lanes.at[face, ks], out_ref.at[0, face, ks], sem.at[2 * face + part])
            copy.start()
            copies.append(copy)
    for copy in copies:
        copy.wait()


def sds(*shape):
    return jax.ShapeDtypeStruct(shape, F32)


def cost(flops, nbytes):
    return pl.CostEstimate(flops=int(flops), bytes_accessed=int(nbytes), transcendentals=0)


def grant(mib):
    return pltpu.CompilerParams(vmem_limit_bytes=mib << 20)


def local(
    initial_state,
    heat_source,
    source_amplitude,
    diffusivity,
    robin_param,
    spectrum_x,
    spectrum_y,
    spectrum_z,
    robin_in,
    open_flag,
    owner_side,
):
    nx, hy, nz = initial_state.shape
    nt = lax.axis_size("tm")
    ncores = lax.axis_size("cores")
    assert ncores == 2 and nt & (nt - 1) == 0 and nt >= 4
    cq = nz // nt
    steps = source_amplitude.shape[0]
    tiles = hy // SUB
    assert tiles == 4 and nx % 4 == 0
    q = lax.axis_index("tm")
    yc = lax.axis_index("cores")
    space = lax.axis_size("space")
    me = lax.axis_index("space")
    qv, ycv, mev = (jnp.reshape(i, (1,)).astype(jnp.int32) for i in (q, yc, me))
    dims = (nt, steps, nx, hy, cq)

    def xor_permute(x, d):
        return lax.ppermute(x, "tm", [(i, i ^ d) for i in range(nt)])

    def swap(x):
        return lax.ppermute(x, "cores", [(0, 1), (1, 0)])

    def along(x, by):
        return lax.ppermute(x, "space", [(i, (i + by) % space) for i in range(space)])

    base = np.stack(np_halves(np_cosine(nz, np.arange(nz)[:, None], np.arange(nz)[None])))
    base = jnp.asarray(base.reshape(2, nt, cq, nz).swapaxes(0, 1))
    kxh, kxl = (jnp.asarray(w) for w in np_bar(nx, False))
    kxih, kxil = (jnp.asarray(w) for w in np_bar(nx, True))
    ky, ki = (jnp.asarray(w) for w in np_second(hy))

    rows = 2 * steps * hy
    block = (None, 2, steps, hy, cq)
    AN = pl.BlockSpec(memory_space=pl.ANY)
    cutting = pl.pallas_call(
        functools.partial(split_kernel, nt),
        out_shape=[sds(2, steps, hy, cq)] * nt,
        grid_spec=pltpu.PrefetchScalarGridSpec(
            num_scalar_prefetch=3,
            grid=(1,),
            in_specs=[
                pl.BlockSpec(block, lambda i, q, y, z, d=d: (0, 0, 0, 0, jnp.bitwise_xor(q[0], d)))
                for d in range(nt)
            ],
            out_specs=[pl.BlockSpec((2, steps, hy, cq), lambda i, q, y, z: (0, 0, 0, 0))] * nt,
        ),
        compiler_params=grant(18),
        cost_estimate=cost(0, 8 * nt * rows * cq),
        name="split",
    )
    dealt = list(cutting(qv, ycv, mev, *([robin_in] * nt)))
    piece = swap(dealt[0])
    for d in range(1, nt):
        dealt[d] = xor_permute(dealt[d], d)

    s0 = pl.pallas_call(
        forward_kernel,
        out_shape=sds(nx, hy, cq),
        in_specs=[SM] + [VM] * 4,
        out_specs=VM,
        compiler_params=grant(18),
        cost_estimate=cost(1e9, 3e6),
        name="forward0",
    )(qv, heat_source, base, kxh, kxl)
    s1 = swap(s0)
    n0, diff_rows, robin_param = pl.pallas_call(
        forward_second_kernel,
        out_shape=[sds(nx, hy, cq), sds(SUB, cq), sds(SUB, cq)],
        in_specs=[SM] * 3 + [VM] * 4,
        out_specs=[VM] * 3,
        compiler_params=grant(18),
        cost_estimate=cost(1e9, 3e6),
        name="forward1",
    )(qv, diffusivity, robin_param, initial_state, base, kxh, kxl)
    n1 = swap(n0)
    amplitudes = [source_amplitude]
    for d in range(1, nt):
        amplitudes.append(xor_permute(source_amplitude, d))
    sy_there = swap(spectrum_y)
    right_param = along(robin_param, -1)
    left_param = along(robin_param, 1)

    table = jax.ShapeDtypeStruct((2 * hy + 2 * (tiles - 1) * SUB, cq), jnp.int32)
    u_own, amps, tab, f_own, f_there, *chunks = pl.pallas_call(
        functools.partial(order_kernel, nt, space),
        out_shape=[sds(nt, 2, steps, hy, cq), sds(nt, steps, cq), table]
        + [sds(nx, hy, cq)] * 2
        + [sds(2, steps, hy, cq)] * (nt - 1),
        in_specs=[SM] * (7 + nt) + [VM] * (2 + nt),
        out_specs=[VM] * (4 + nt),
        compiler_params=grant(18),
        cost_estimate=cost(0, 3e6),
        name="order",
    )(
        qv, mev, spectrum_x, spectrum_y, sy_there, open_flag, owner_side, *amplitudes, diff_rows,
        spectrum_z.reshape(nt, cq), *dealt,
    )
    for i in range(nt - 1):
        chunks[i] = swap(chunks[i])

    ends_shape, traces = sds(nt, nx, hy, cq), sds(2, 2, nt * steps, tiles, SUB, cq)
    driven, clos, s_there = pl.pallas_call(
        functools.partial(driven_kernel, dims),
        out_shape=[traces, ends_shape, sds(nx, hy, cq)],
        in_specs=[SM] + [VM] * 6,
        out_specs=[VM] * 3,
        scratch_shapes=[pltpu.VMEM((nx, hy, cq), F32)],
        compiler_params=grant(18),
        cost_estimate=cost(3e9, 6e6),
        name="driven",
    )(ycv, s0, s1, u_own, amps, f_own, ky)
    short = sds(2, steps, (tiles - 1) * SUB, cq)
    *hands, clos, m_there = pl.pallas_call(
        functools.partial(own_kernel, dims),
        out_shape=[short] * nt + [ends_shape, sds(nx, hy, cq)],
        in_specs=[SM] * 2 + [VM] * 10,
        out_specs=[VM] * (nt + 2),
        scratch_shapes=[pltpu.VMEM((nx, hy, cq), F32), pltpu.VMEM(traces.shape, F32)],
        compiler_params=grant(18),
        cost_estimate=cost(3e9, 8e6),
        name="own",
    )(qv, ycv, left_param, robin_param, right_param, n0, n1, driven, clos, tab, f_own, ky)
    for d in range(1, nt):
        hands[d] = xor_permute(hands[d], d)

    state, ends = m_there, {}
    for stage, got in enumerate((chunks[:-2], chunks[-2:-1], chunks[-1:])):
        span = (nt - 2, 1, 2)[stage]
        parts = slot_parts(late_slots(nt) if stage == 2 else range(nt), nt, nx)
        prior = [ends[part] for part in parts] if stage else []
        *outs, state = pl.pallas_call(
            functools.partial(other_kernel, dims, stage),
            out_shape=[sds(r1 - r0, hy, cq) for _, r0, r1 in parts] + [sds(nx, hy, cq)],
            in_specs=[SM] * 2 + [VM] * (9 + len(got) + len(prior)),
            out_specs=[VM] * (len(parts) + 1),
            scratch_shapes=[
                pltpu.VMEM((span, nx, hy, cq), F32),
                pltpu.VMEM((nx, hy, cq), F32),
                pltpu.VMEM((nx, hy, cq), F32),
                pltpu.VMEM((span, 2, steps, hy, cq), F32),
            ],
            input_output_aliases={11 + len(got) + d: d for d in range(len(prior))},
            compiler_params=grant(18),
            cost_estimate=cost(2e9 * span, 2e6 * span),
        )(qv, ycv, state, s_there, f_there, amps, clos, ki, kxih, kxil, piece, *got, *prior)
        for part, out in zip(parts, outs):
            ends[part] = out
        early = slot_parts([d for d in range(1, nt) if d not in late_slots(nt)], nt, nx)
        for d, r0, r1 in (early, parts)[stage - 1] if stage else ():
            if d:
                ends[d, r0, r1] = xor_permute(ends[d, r0, r1], d)
    middle = [ends[d, 0, nx] for d in range(nt - 1)]
    spans = [(0, late_cut(nx)), (late_cut(nx), nx)]
    lasts = [ends[nt - 1, r0, r1] for r0, r1 in spans]
    passed = []
    for h, last in enumerate(lasts if nt == 4 else []):
        passing = pl.pallas_call(
            functools.partial(relay_kernel, nt, spans[h][0]),
            out_shape=sds(*last.shape),
            in_specs=[SM] + [VM] * 2,
            out_specs=VM,
            compiler_params=grant(18),
            cost_estimate=cost(0, 1e6),
        )(qv, middle[2], last)
        passed.append(xor_permute(passing, 1))
    left, right = pl.pallas_call(
        functools.partial(merge_kernel, nt),
        out_shape=[sds(nt, steps, (tiles - 1) * SUB, cq)] * 2,
        in_specs=[SM] + [VM] * nt,
        out_specs=[VM] * 2,
        compiler_params=grant(18),
        cost_estimate=cost(0, 2e6),
        name="merge",
    )(qv, *hands)
    from_right = along(left, -1)
    from_left = along(right, 1)
    acc, wh, wl = pl.pallas_call(
        functools.partial(half_kernel, nt),
        out_shape=[sds(nx, hy, nz)] + [jax.ShapeDtypeStruct(((nt - 2) * cq, nz), BF16)] * 2,
        in_specs=[SM] + [VM] * 3,
        out_specs=[VM] * 3,
        compiler_params=grant(18),
        cost_estimate=cost(1e9, 4e6),
        name="half",
    )(qv, base, *middle[:2])
    xb = 4
    window_end = []
    for h, last in enumerate(lasts):
        operands = (qv, acc, wh, wl, *middle[2:], last, *passed[h : h + 1])
        window_end = [
            pl.pallas_call(
                functools.partial(final_kernel, nt, spans[h][0]),
                out_shape=sds(1, nx, hy, nz),
                in_specs=[SM] + [VM] * (len(operands) - 1) + [AN] * len(window_end),
                out_specs=AN,
                scratch_shapes=[
                    pltpu.VMEM((last.shape[0] // xb, xb, hy, nz), F32),
                    pltpu.SemaphoreType.DMA((last.shape[0] // xb,)),
                ],
                input_output_aliases={len(operands): 0} if window_end else {},
                compiler_params=grant(18),
                cost_estimate=cost(1e9, 3e6),
            )(*operands, *window_end)
        ]

    robin_out = pl.pallas_call(
        functools.partial(spread_kernel, nt, steps),
        out_shape=sds(1, 2, steps, hy, nz),
        in_specs=[VM] * 3,
        out_specs=AN,
        scratch_shapes=[
            pltpu.VMEM((2, steps, hy, cq), F32),
            pltpu.VMEM((2, steps, hy, nz), F32),
            pltpu.SemaphoreType.DMA((4,)),
        ],
        compiler_params=grant(18),
        cost_estimate=cost(0, 2e6),
        name="spread",
    )(tab, from_left, from_right)
    return robin_out, window_end[0]


def solution(mesh):
    placed = (
        P("space", "cores", None),
        P("space", "cores", None),
        P("tm"),
        P("space"),
        P("space"),
        P(),
        P("cores"),
        P(),
        P("space", None, "tm", "cores", None),
        P(None, "cores"),
        P(None, "cores"),
    )

    return jax.shard_map(
        local,
        mesh=mesh,
        in_specs=placed,
        out_specs=(P("space", None, "tm", "cores", None), P("tm", "space", "cores", None)),
        check_vma=False,
    )
```
